256 devices in a mesh: rep: 4 (over x_hi, core), tp: 32 (over z, y), dec: 2 (over x_lo).
Axes of the slice: x: 4 (x_hi: 2, x_lo: 2; x = x_hi * 2 + x_lo), y: 4, z: 8, core: 2. Of those that a mesh axis runs over, the one named last changes fastest.
Arguments:
- residual: bfloat16 [4096, 4096], P(('rep', 'tp', 'dec')), may hold values from -6 to 6
- queries: bfloat16 [128, 2, 16, 4096], P('rep', 'dec', None, 'tp'), may hold values from -64 to 64
- kv_pool: bfloat16 [256, 8, 128, 256], P(('rep', 'tp', 'dec')), may hold values from -8 to 8
- prior_len: int32 [16], P('rep'), may hold values from 0 to 1792, as said below
- page_table: int32 [16, 16], P('rep'), may hold values from -1 to 255, as said below
- page_target: int32 [256], P(('rep', 'tp', 'dec')), may hold values from 0 to 3, as said below
- out_weight: bfloat16 [4096, 4096], P('tp'), may hold values from -0.5 to 0.5
- moe_gain: float32 [4096], replicated, may hold values from 0.1 to 1.9
- expert_ids: int32 [4096, 2], P(('rep', 'tp', 'dec')), may hold values from 0 to 7, as said below
- expert_gates: float32 [4096, 2], P(('rep', 'tp', 'dec')), may hold values from 0.1 to 1
- w_gate: bfloat16 [2, 14336, 4096], P('dec', 'tp'), may hold values from -0.09375 to 0.09375
- w_up: bfloat16 [2, 14336, 4096], P('dec', 'tp'), may hold values from -0.09375 to 0.09375
- w_down: bfloat16 [2, 14336, 4096], P('dec', 'tp'), may hold values from -0.1875 to 0.1875
Outputs:
- layer_out: bfloat16 [4096, 4096], P(('rep', 'tp', 'dec'))
- decode_pages: bfloat16 [256, 8, 128, 256], P(('rep', 'tp', 'dec'))
The draws below stay inside these ranges and needn't reach their ends.
Inputs may be any that keep to these rules, and one draw needn't show every extreme that they name: `prior_len`: each value is a multiple of 256; in every rep index's 4 requests one request has the largest value. `page_table`: for request q, the first (prior_len[q] + 256) // 128 entries are distinct slots among the 64 slots of q's rep index (slots r * 64 to r * 64 + 63), no slot named twice in a rep index; the other entries are -1. Slots that no entry names hold data that attention never reads. `page_target`: for every m, the slots r * 64 + m over all rep indices r go to distinct rep indices. `expert_ids`: each row names two different experts; among the 16 rows of each device (aligned blocks of rows) every expert is named by exactly 4 rows.
All inputs are finite; a program needn't handle non-finite values.
Results may differ from the reference program's by a relative error of at most 0.02.
Values may be sent and summed in bfloat16 or wider, within the bound.
A program may use at most 64 MiB of HBM per device.

```python
import jax
import jax.numpy as jnp
from jax import lax

D = 4096
QH = 32
KVH = 8
HD = 128
FF = 14336
EXPERTS = 8
TOPK = 2
EXP_WIN = 2
PAGE = 128
SPANS_MAX = 8
R_DEV = 4
NEW_TOK = 256
REQUESTS = 16
TOKENS = 4096
TOK_DEV = 16
PAGES_MAX = 16
GROUP_SLOTS = 64
SLOTS = 256
N_REP = 4
N_DEC = 2


def layout(key):
    base_key = jax.random.fold_in(key, 11)
    pick_key, span_key, slot_key = jax.random.split(base_key, 3)
    groups = REQUESTS // R_DEV
    longest = jax.random.randint(pick_key, (groups,), 0, R_DEV)
    span_counts = jax.random.randint(span_key, (groups, R_DEV), 1, SPANS_MAX + 1)
    span_counts = jnp.where(jnp.arange(R_DEV)[None, :] == longest[:, None], SPANS_MAX, span_counts)

    def shuffle_slots(item_key):
        return jax.random.permutation(item_key, GROUP_SLOTS)
    orders = jax.vmap(shuffle_slots)(jax.random.split(slot_key, groups))
    chosen = orders[:, :R_DEV * PAGES_MAX].reshape(groups, R_DEV, PAGES_MAX)
    live_pages = jnp.arange(PAGES_MAX)[None, None, :] < (span_counts * (NEW_TOK // PAGE))[:, :, None]
    offsets = (jnp.arange(groups) * GROUP_SLOTS)[:, None, None]
    slot_table = jnp.where(live_pages, chosen + offsets, -1)
    return (span_counts.reshape(REQUESTS).astype(jnp.int32), slot_table.reshape(REQUESTS, PAGES_MAX).astype(jnp.int32))


def draw_prior_len(key, part):
    span_counts, slot_table = layout(key)
    return ((span_counts - 1) * NEW_TOK).astype(jnp.int32)


def draw_page_table(key, part):
    span_counts, slot_table = layout(key)
    return slot_table


def draw_page_target(key, part):
    target_key = jax.random.fold_in(key, 13)

    def shuffle_reps(item_key):
        return jax.random.permutation(item_key, SLOTS // GROUP_SLOTS)
    orders = jax.vmap(shuffle_reps)(jax.random.split(target_key, GROUP_SLOTS))
    return jnp.transpose(orders).reshape(SLOTS).astype(jnp.int32)


def draw_expert_ids(key, part):
    ids_key = jax.random.fold_in(key, 17)
    row_key, label_key, swap_key = jax.random.split(ids_key, 3)
    blocks = TOKENS // TOK_DEV
    rank_index = jnp.arange(TOK_DEV)
    first_id = rank_index % EXPERTS
    second = (first_id + 1 + rank_index // EXPERTS % (EXPERTS - 1)) % EXPERTS
    id_pairs = jnp.stack([first_id, second], axis=-1)
    swapped = jax.random.randint(swap_key, (blocks, TOK_DEV, 1), 0, 2)
    id_pairs = jnp.where(swapped == 1, id_pairs[None, :, ::-1], id_pairs[None, :, :])

    def shuffle_rows(item_key):
        return jax.random.permutation(item_key, TOK_DEV)

    def shuffle_labels(item_key):
        return jax.random.permutation(item_key, EXPERTS)
    row_orders = jax.vmap(shuffle_rows)(jax.random.split(row_key, blocks))
    id_pairs = jnp.take_along_axis(id_pairs, row_orders[:, :, None], axis=1)
    labels = jax.vmap(shuffle_labels)(jax.random.split(label_key, blocks))
    named_ids = jnp.take_along_axis(labels, id_pairs.reshape(blocks, TOK_DEV * 2), axis=1)
    return named_ids.reshape(TOKENS, TOPK).astype(jnp.int32)


def draw_queries(key, part):
    values = jax.random.normal(jax.random.fold_in(key, 31), (TOKENS, QH * HD), jnp.float32) * 2.0
    values = jnp.clip(values, -12.0, 12.0)
    values = values.reshape(TOKENS // (N_DEC * TOK_DEV), N_DEC, TOK_DEV, QH * HD)
    return values.astype(jnp.bfloat16)


def draw_kv_pool(key, part):
    pool_values = jax.random.normal(jax.random.fold_in(key, 43), (SLOTS, KVH, PAGE, 2 * HD), jnp.float32)
    pool_values = jnp.clip(pool_values, -6.0, 6.0)
    return pool_values.astype(jnp.bfloat16)


def shard_levels(rng, extent, cuts, low, largest):
    def one(axis_at, blocks):
        draws = jax.random.uniform(jax.random.fold_in(jax.random.fold_in(rng, 6), axis_at), (blocks,), jnp.float32, low / len(cuts), largest / len(cuts))
        return jnp.repeat(jnp.exp(draws), extent[axis_at] // blocks).reshape((-1,) + (1,) * (len(extent) - axis_at - 1))

    gain = one(*cuts[0])
    for cut in cuts[1:]:
        gain = gain * one(*cut)
    return gain


def centred(own_key, extent, spread, most, cuts=(), held_as=jnp.bfloat16):
    gain = shard_levels(own_key, extent, cuts, -0.22, 0.18) if cuts else 1.0
    result = jax.random.normal(own_key, extent, jnp.float32) * spread * gain
    return jnp.minimum(jnp.maximum(result, -most), most).astype(held_as)


def setup_inputs(seed: int = 0) -> dict:
    keys = jax.random.split(jax.random.key(seed), 14)
    return {
        "residual": centred(keys[0], (TOKENS, D), 1.0, 6.0, ((0, 256),)),
        "queries": draw_queries(jax.random.fold_in(keys[13], 71), 0),
        "kv_pool": draw_kv_pool(jax.random.fold_in(keys[13], 71), 0),
        "prior_len": draw_prior_len(jax.random.fold_in(keys[13], 71), 0),
        "page_table": draw_page_table(jax.random.fold_in(keys[13], 71), 0),
        "page_target": draw_page_target(jax.random.fold_in(keys[13], 71), 0),
        "out_weight": centred(keys[6], (QH * HD, D), HD ** -0.5, 0.5, ((0, 32),)),
        "moe_gain": jnp.clip(1.0 + 0.18 * jax.random.normal(keys[7], (D,), jnp.float32), 0.1, 1.9),
        "expert_ids": draw_expert_ids(jax.random.fold_in(keys[13], 71), 0),
        "expert_gates": jnp.clip(0.1 + 0.9 * jax.random.uniform(keys[9], (TOKENS, TOPK), jnp.float32) ** shard_levels(keys[9], (TOKENS, TOPK), ((0, 256),), -0.2, 0.2), 0.1, 1.0),
        "w_gate": centred(keys[10], (EXP_WIN, FF, D), D ** -0.5, 0.09375, ((0, 2), (1, 32))),
        "w_up": centred(keys[11], (EXP_WIN, FF, D), D ** -0.5, 0.09375, ((0, 2), (1, 32))),
        "w_down": centred(keys[12], (EXP_WIN, FF, D), (FF // 16) ** -0.5, 0.1875, ((0, 2), (1, 32))),
    }


def attend_one(query_block, gathered_pages, prior):
    group_size = QH // KVH
    grouped = query_block.astype(jnp.float32).reshape(NEW_TOK, KVH, group_size, HD)
    keys_part = gathered_pages[..., :HD].astype(jnp.float32)
    values_part = gathered_pages[..., HD:].astype(jnp.float32)
    key_count = PAGES_MAX * PAGE
    scores = jnp.einsum('ukgd,pkwd->ukgpw', grouped, keys_part)
    scores = scores.reshape(NEW_TOK, KVH, group_size, key_count) * HD ** (-0.5)
    position = jnp.arange(key_count, dtype=jnp.int32)
    last_seen = prior + jnp.arange(NEW_TOK, dtype=jnp.int32)
    visible = (position[None, :] <= last_seen[:, None])[:, None, None, :]
    scores = jnp.where(visible, scores, -1e+30)
    row_top = lax.optimization_barrier(jnp.max(scores, axis=-1, keepdims=True))
    raw_weights = jnp.where(visible, jnp.exp(scores - row_top), 0.0)
    totals = lax.optimization_barrier(jnp.sum(raw_weights, axis=-1))
    weights_low = lax.optimization_barrier(raw_weights.astype(jnp.bfloat16)).astype(jnp.float32)
    weights_low = weights_low.reshape(NEW_TOK, KVH, group_size, PAGES_MAX, PAGE)
    weighted = jnp.einsum('ukgpw,pkwd->ukgd', weights_low, values_part)
    attended = (weighted / totals[..., None]).astype(jnp.bfloat16)
    return attended.reshape(NEW_TOK, QH * HD)

def reference(residual, queries, kv_pool, prior_len, page_table, page_target, out_weight, moe_gain, expert_ids, expert_gates, w_gate, w_up, w_down):
    flat_queries = queries.reshape(TOKENS, QH * HD)

    def per_request(request):
        query_block = lax.dynamic_slice_in_dim(flat_queries, request * NEW_TOK, NEW_TOK, 0)
        slot_list = jnp.maximum(page_table[request], 0).astype(jnp.int32)
        gathered_pages = kv_pool[slot_list]
        return attend_one(query_block, gathered_pages, prior_len[request])
    attended = lax.map(per_request, jnp.arange(REQUESTS, dtype=jnp.int32)).reshape(TOKENS, QH * HD)
    mid_state = residual.astype(jnp.float32) + jnp.dot(attended, out_weight, preferred_element_type=jnp.float32)
    inverse = lax.rsqrt(lax.optimization_barrier(jnp.mean(mid_state * mid_state, axis=-1, keepdims=True)) + 1e-05)
    normed = (mid_state * inverse * moe_gain).astype(jnp.bfloat16)
    routed_total = TOKENS * TOPK // EXPERTS
    mixture = jnp.zeros_like(mid_state)
    for expert in range(EXP_WIN):
        names_it = expert_ids == expert
        chosen_rows = jnp.nonzero(jnp.any(names_it, axis=-1), size=routed_total)[0].astype(jnp.int32)
        gate_sum = lax.optimization_barrier(jnp.sum(jnp.where(names_it, expert_gates, 0.0), axis=-1))
        picked = normed[chosen_rows]
        gate_part = jnp.dot(picked, w_gate[expert].T, preferred_element_type=jnp.float32)
        up_part = jnp.dot(picked, w_up[expert].T, preferred_element_type=jnp.float32)
        hidden = (jax.nn.silu(gate_part) * up_part).astype(jnp.bfloat16)
        expert_out = jnp.dot(hidden, w_down[expert], preferred_element_type=jnp.float32)
        mixture = mixture.at[chosen_rows].add(expert_out * gate_sum[chosen_rows][:, None])
    layer_out = (mid_state + mixture).astype(jnp.bfloat16)
    group_slots = SLOTS // N_REP
    pool_groups = kv_pool.reshape(N_REP, group_slots, KVH, PAGE, 2 * HD)
    targets = page_target.reshape(N_REP, group_slots).astype(jnp.int32)
    spots = jnp.broadcast_to(jnp.arange(group_slots, dtype=jnp.int32)[None, :], (N_REP, group_slots))
    decode_pages = jnp.zeros_like(pool_groups).at[targets, spots].set(pool_groups)
    return (layer_out, decode_pages.reshape(SLOTS, KVH, PAGE, 2 * HD))
```

```python
import jax
import jax.numpy as jnp
from jax import lax
from jax.sharding import PartitionSpec as P

QH = 32
KVH = 8
EXPERTS = 8
TOPK = 2
EXP_WIN = 2


def hand_over(kv_pool, page_target):
    rep_size = lax.axis_size("rep")
    owners = jnp.arange(rep_size, dtype=jnp.int32)
    selected = (page_target[None, :] == owners[:, None])[:, :, None, None, None]
    outgoing = jnp.where(selected, kv_pool[None], jnp.zeros((), kv_pool.dtype))
    incoming = lax.all_to_all(outgoing, "rep", split_axis=0, concat_axis=0, tiled=True)
    return jnp.sum(incoming, axis=0)


def on_device(
    residual,
    queries,
    kv_pool,
    prior_len,
    page_table,
    page_target,
    out_weight,
    moe_gain,
    expert_ids,
    expert_gates,
    w_gate,
    w_up,
    w_down,
):
    tp_size = lax.axis_size("tp")
    dec_size = lax.axis_size("dec")
    dec_index = lax.axis_index("dec")
    slots_dev, kv_heads, page_rows, both_dim = kv_pool.shape
    head_dim = both_dim // 2
    heads_dev = queries.shape[3] // head_dim
    group_size = QH // KVH
    kv_dev = max(1, heads_dev // group_size)
    copies = max(1, group_size // heads_dev)
    per_kv = heads_dev // kv_dev
    requests = prior_len.shape[0]
    tok_dev = queries.shape[2]
    half_rows = queries.shape[0] * tok_dev // requests
    pages_max = page_table.shape[1]
    team_size = tp_size * dec_size
    spread = jnp.repeat(kv_pool, copies, axis=1).reshape(
        slots_dev, tp_size, kv_dev, page_rows, both_dim
    )
    holder = page_table // slots_dev % team_size
    number = page_table % slots_dev
    outgoing = jnp.broadcast_to(
        spread[:, :, None], (slots_dev, tp_size, dec_size, kv_dev, page_rows, both_dim)
    )
    outgoing = outgoing.reshape(slots_dev, team_size, kv_dev, page_rows, both_dim)
    received = lax.all_to_all(outgoing, ("tp", "dec"), split_axis=1, concat_axis=0, tiled=True)
    local_index = holder * slots_dev + number
    received = received.reshape(team_size * slots_dev, kv_dev, page_rows, both_dim)
    gathered_pages = received[local_index]
    keys_part = gathered_pages[..., :head_dim]
    values_part = gathered_pages[..., head_dim:]
    query_rows = queries.reshape(requests, half_rows, kv_dev, per_kv, head_dim)
    key_count = pages_max * page_rows
    scores = jnp.einsum(
        "rukgd,rpkwd->rukgpw", query_rows, keys_part, preferred_element_type=jnp.float32
    )
    scores = scores.reshape(requests, half_rows, kv_dev, per_kv, key_count) * head_dim ** (-0.5)
    position = jnp.arange(key_count, dtype=jnp.int32)
    local_row = jnp.arange(half_rows, dtype=jnp.int32)
    offset = (local_row // tok_dev * dec_size + dec_index) * tok_dev + local_row % tok_dev
    last_seen = prior_len[:, None] + offset[None, :]
    visible = (position[None, None, :] <= last_seen[:, :, None])[:, :, None, None, :]
    scores = jnp.where(visible, scores, -1e30)
    row_top = jnp.max(scores, axis=-1, keepdims=True)
    raw_weights = jnp.where(visible, jnp.exp(scores - row_top), 0.0)
    totals = jnp.sum(raw_weights, axis=-1)
    weights_low = raw_weights.astype(jnp.bfloat16).reshape(
        requests, half_rows, kv_dev, per_kv, pages_max, page_rows
    )
    weighted = jnp.einsum(
        "rukgpw,rpkwd->rukgd", weights_low, values_part, preferred_element_type=jnp.float32
    )
    attended = (
        (weighted / totals[..., None])
        .astype(jnp.bfloat16)
        .reshape(requests * half_rows, heads_dev * head_dim)
    )
    partial = jnp.dot(attended, out_weight, preferred_element_type=jnp.float32).astype(jnp.bfloat16)
    partial = partial.reshape(tp_size, -1, partial.shape[1])
    pieces = lax.all_to_all(partial, "tp", split_axis=0, concat_axis=0, tiled=True)
    projected = jnp.sum(pieces.astype(jnp.float32), axis=0)
    mid_state = residual.astype(jnp.float32) + projected
    routed_dev = tok_dev * TOPK // EXPERTS
    row_lists = []
    gate_lists = []
    for expert in range(EXP_WIN):
        names_it = expert_ids == expert
        chosen_rows = jnp.nonzero(jnp.any(names_it, axis=-1), size=routed_dev)[0].astype(jnp.int32)
        row_lists.append(chosen_rows)
        gate_lists.append(jnp.sum(jnp.where(names_it, expert_gates, 0.0), axis=-1)[chosen_rows])
    picked_rows = jnp.stack(row_lists, axis=0)
    picked_gates = jnp.stack(gate_lists, axis=0)
    inverse = lax.rsqrt(jnp.mean(mid_state * mid_state, axis=-1, keepdims=True) + 1e-05)
    normed_all = (mid_state * inverse * moe_gain).astype(jnp.bfloat16)
    width = normed_all.shape[1]
    by_expert = normed_all[picked_rows]
    outgoing = jnp.broadcast_to(by_expert[None], (tp_size, dec_size, routed_dev, width))
    outgoing = outgoing.reshape(team_size, routed_dev, width)
    row_piece = lax.all_to_all(outgoing, ("tp", "dec"), split_axis=0, concat_axis=0, tiled=True)
    row_piece = row_piece.reshape(team_size * routed_dev, width)
    gate_part = jnp.dot(row_piece, w_gate[0].T, preferred_element_type=jnp.float32)
    up_part = jnp.dot(row_piece, w_up[0].T, preferred_element_type=jnp.float32)
    hidden = (jax.nn.silu(gate_part) * up_part).astype(jnp.bfloat16)
    expert_part = jnp.dot(hidden, w_down[0], preferred_element_type=jnp.float32).astype(jnp.bfloat16)
    expert_part = expert_part.reshape(team_size, routed_dev, width)
    returned = lax.all_to_all(expert_part, ("tp", "dec"), split_axis=0, concat_axis=0, tiled=True)
    returned = returned.reshape(tp_size, dec_size, routed_dev, width).astype(jnp.float32)
    expert_out = jnp.sum(returned, axis=0)
    mixture = jnp.zeros_like(mid_state)
    for expert in range(EXP_WIN):
        mixture = mixture.at[picked_rows[expert]].add(
            expert_out[expert] * picked_gates[expert][:, None]
        )
    layer_out = (mid_state + mixture).astype(jnp.bfloat16)
    decode_pages = hand_over(kv_pool, page_target)
    return (layer_out, decode_pages)


def solution(mesh):
    return jax.shard_map(
        on_device,
        mesh=mesh,
        in_specs=(
            P(("rep", "tp", "dec"), None),
            P("rep", "dec", None, "tp"),
            P(("rep", "tp", "dec"), None, None, None),
            P("rep"),
            P("rep", None),
            P(("rep", "tp", "dec")),
            P("tp", None),
            P(),
            P(("rep", "tp", "dec"), None),
            P(("rep", "tp", "dec"), None),
            P("dec", "tp", None),
            P("dec", "tp", None),
            P("dec", "tp", None),
        ),
        out_specs=(P(("rep", "tp", "dec"), None), P(("rep", "tp", "dec"), None, None, None)),
        check_vma=False,
    )
```

```python
import jax
import jax.numpy as jnp
from jax import lax
from jax.sharding import PartitionSpec as P

QH = 32
KVH = 8
EXPERTS = 8
TOPK = 2
EXP_WIN = 2


def hand_over(kv_pool, page_target):
    rep_size = lax.axis_size("rep")
    owners = jnp.arange(rep_size, dtype=jnp.int32)
    selected = (page_target[None, :] == owners[:, None])[:, :, None, None, None]
    outgoing = jnp.where(selected, kv_pool[None], jnp.zeros((), kv_pool.dtype))
    incoming = lax.all_to_all(outgoing, "rep", split_axis=0, concat_axis=0, tiled=True)
    return jnp.sum(incoming, axis=0)


def on_device(
    residual,
    queries,
    kv_pool,
    prior_len,
    page_table,
    page_target,
    out_weight,
    moe_gain,
    expert_ids,
    expert_gates,
    w_gate,
    w_up,
    w_down,
):
    tp_size = lax.axis_size("z") * lax.axis_size("y")
    dec_size = lax.axis_size("dec")
    dec_index = lax.axis_index("dec")
    slots_dev, kv_heads, page_rows, both_dim = kv_pool.shape
    head_dim = both_dim // 2
    heads_dev = queries.shape[3] // head_dim
    group_size = QH // KVH
    kv_dev = max(1, heads_dev // group_size)
    copies = max(1, group_size // heads_dev)
    per_kv = heads_dev // kv_dev
    requests = prior_len.shape[0]
    tok_dev = queries.shape[2]
    half_rows = queries.shape[0] * tok_dev // requests
    pages_max = page_table.shape[1]
    team_size = tp_size * dec_size
    z_size = lax.axis_size("z")
    plane_size = team_size // z_size
    spread = kv_pool.reshape(slots_dev, z_size, kv_dev, page_rows, both_dim)
    spread = jnp.swapaxes(spread, 0, 1)
    by_plane = lax.all_to_all(spread, "z", split_axis=0, concat_axis=0, tiled=True)
    outgoing = jnp.broadcast_to(by_plane[None], (plane_size,) + by_plane.shape)
    received = lax.all_to_all(outgoing, ("y", "dec"), split_axis=0, concat_axis=0, tiled=True)
    received = jnp.swapaxes(received, 0, 1)
    received = received.reshape(team_size * slots_dev, kv_dev, page_rows, both_dim)
    gathered_pages = received[page_table % (team_size * slots_dev)]
    keys_part = gathered_pages[..., :head_dim]
    values_part = gathered_pages[..., head_dim:]
    query_rows = queries.reshape(requests, half_rows, kv_dev, per_kv, head_dim)
    key_count = pages_max * page_rows
    scores = jnp.einsum(
        "rukgd,rpkwd->rukgpw", query_rows, keys_part, preferred_element_type=jnp.float32
    )
    scores = scores.reshape(requests, half_rows, kv_dev, per_kv, key_count) * head_dim ** (-0.5)
    position = jnp.arange(key_count, dtype=jnp.int32)
    local_row = jnp.arange(half_rows, dtype=jnp.int32)
    offset = (local_row // tok_dev * dec_size + dec_index) * tok_dev + local_row % tok_dev
    last_seen = prior_len[:, None] + offset[None, :]
    visible = (position[None, None, :] <= last_seen[:, :, None])[:, :, None, None, :]
    scores = jnp.where(visible, scores, -1e30)
    row_top = jnp.max(scores, axis=-1, keepdims=True)
    raw_weights = jnp.where(visible, jnp.exp(scores - row_top), 0.0)
    totals = jnp.sum(raw_weights, axis=-1)
    weights_low = raw_weights.astype(jnp.bfloat16).reshape(
        requests, half_rows, kv_dev, per_kv, pages_max, page_rows
    )
    weighted = jnp.einsum(
        "rukgpw,rpkwd->rukgd", weights_low, values_part, preferred_element_type=jnp.float32
    )
    attended = (
        (weighted / totals[..., None])
        .astype(jnp.bfloat16)
        .reshape(requests * half_rows, heads_dev * head_dim)
    )
    partial = jnp.dot(attended, out_weight, preferred_element_type=jnp.float32).astype(jnp.bfloat16)
    partial = partial.reshape(tp_size, -1, partial.shape[1])
    pieces = lax.all_to_all(partial, ("z", "y"), split_axis=0, concat_axis=0, tiled=True)
    projected = jnp.sum(pieces.astype(jnp.float32), axis=0)
    mid_state = residual.astype(jnp.float32) + projected
    routed_dev = tok_dev * TOPK // EXPERTS
    row_lists = []
    gate_lists = []
    for expert in range(EXP_WIN):
        names_it = expert_ids == expert
        chosen_rows = jnp.nonzero(jnp.any(names_it, axis=-1), size=routed_dev)[0].astype(jnp.int32)
        row_lists.append(chosen_rows)
        gate_lists.append(jnp.sum(jnp.where(names_it, expert_gates, 0.0), axis=-1)[chosen_rows])
    picked_rows = jnp.stack(row_lists, axis=0)
    picked_gates = jnp.stack(gate_lists, axis=0)
    inverse = lax.rsqrt(jnp.mean(mid_state * mid_state, axis=-1, keepdims=True) + 1e-05)
    normed_all = (mid_state * inverse * moe_gain).astype(jnp.bfloat16)
    width = normed_all.shape[1]
    by_expert = normed_all[picked_rows]
    outgoing = jnp.broadcast_to(by_expert[None], (tp_size, dec_size, routed_dev, width))
    outgoing = outgoing.reshape(team_size, routed_dev, width)
    row_piece = lax.all_to_all(outgoing, ("z", "y", "dec"), split_axis=0, concat_axis=0, tiled=True)
    row_piece = row_piece.reshape(team_size * routed_dev, width)
    gate_part = jnp.dot(row_piece, w_gate[0].T, preferred_element_type=jnp.float32)
    up_part = jnp.dot(row_piece, w_up[0].T, preferred_element_type=jnp.float32)
    hidden = (jax.nn.silu(gate_part) * up_part).astype(jnp.bfloat16)
    expert_part = jnp.dot(hidden, w_down[0], preferred_element_type=jnp.float32).astype(jnp.bfloat16)
    expert_part = expert_part.reshape(team_size, routed_dev, width)
    returned = lax.all_to_all(expert_part, ("z", "y", "dec"), split_axis=0, concat_axis=0, tiled=True)
    returned = returned.reshape(tp_size, dec_size, routed_dev, width).astype(jnp.float32)
    expert_out = jnp.sum(returned, axis=0)
    mixture = jnp.zeros_like(mid_state)
    for expert in range(EXP_WIN):
        mixture = mixture.at[picked_rows[expert]].add(
            expert_out[expert] * picked_gates[expert][:, None]
        )
    layer_out = (mid_state + mixture).astype(jnp.bfloat16)
    decode_pages = hand_over(kv_pool, page_target)
    return (layer_out, decode_pages)


def fine_mesh(mesh):
    tp_devices = mesh.devices[0, :, 0]
    y_size = len({device.coords[1] for device in tp_devices})
    shape = (mesh.shape["rep"], mesh.shape["tp"] // y_size, y_size, mesh.shape["dec"])
    return jax.sharding.Mesh(mesh.devices.reshape(shape), ("rep", "z", "y", "dec"))


def solution(mesh):
    team = ("rep", "z", "y", "dec")
    return jax.shard_map(
        on_device,
        mesh=fine_mesh(mesh),
        in_specs=(
            P(team, None),
            P("rep", "dec", None, ("z", "y")),
            P(team, None, None, None),
            P("rep"),
            P("rep", None),
            P(team),
            P(("z", "y"), None),
            P(),
            P(team, None),
            P(team, None),
            P("dec", ("z", "y"), None),
            P("dec", ("z", "y"), None),
            P("dec", ("z", "y"), None),
        ),
        out_specs=(P(team, None), P(team, None, None, None)),
        check_vma=False,
    )
```

```python
import jax
import jax.numpy as jnp
from jax import lax
from jax.sharding import PartitionSpec as P
from jax.experimental import pallas as pl
from jax.experimental.pallas import tpu as pltpu

QH = 32
KVH = 8
EXPERTS = 8
TOPK = 2
EXP_WIN = 2


MESH = pl.DeviceIdType.MESH

def _ring_kernel(part_ref, out_ref, recv_buf, send_buf, send_sem, recv_sem):
    n = part_ref.shape[1]
    me = lax.axis_index("z")
    rep = lax.axis_index("rep")
    yy = lax.axis_index("y")
    dd = lax.axis_index("dec")
    right = lax.rem(me + 1, n)
    left = lax.rem(me + n - 1, n)
    barrier = pltpu.get_barrier_semaphore()
    for neighbour in (left, right):
        pl.semaphore_signal(barrier, inc=1, device_id=(rep, neighbour, yy, dd), device_id_type=MESH)
    pl.semaphore_wait(barrier, 2)
    for step in range(n - 1):
        copies = []
        for way in range(2):
            if way == 0:
                target, block = right, lax.rem(me + 2 * n - 1 - step, n)
            else:
                target, block = left, lax.rem(me + 1 + step, n)
            source = part_ref.at[way, block] if step == 0 else send_buf.at[way, step - 1]
            copy = pltpu.make_async_remote_copy(
                src_ref=source,
                dst_ref=recv_buf.at[way, step],
                send_sem=send_sem.at[way, step],
                recv_sem=recv_sem.at[way, step],
                device_id=(rep, target, yy, dd),
                device_id_type=MESH,
            )
            copy.start()
            copies.append(copy)
        for way in range(2):
            copies[way].wait()
            if way == 0:
                block = lax.rem(me + 2 * n - 2 - step, n)
            else:
                block = lax.rem(me + 2 + step, n)
            total = recv_buf[way, step].astype(jnp.float32) + part_ref[way, block].astype(jnp.float32)
            if step < n - 2:
                send_buf[way, step] = total.astype(send_buf.dtype)
            else:
                out_ref[way] = total


def ring_reduce_scatter(part):
    ways, n = part.shape[:2]
    block_shape = part.shape[2:]
    return pl.pallas_call(
        _ring_kernel,
        out_shape=jax.ShapeDtypeStruct((ways,) + block_shape, jnp.float32),
        in_specs=[pl.BlockSpec(memory_space=pltpu.VMEM)],
        out_specs=pl.BlockSpec(memory_space=pltpu.VMEM),
        scratch_shapes=[
            pltpu.VMEM((ways, n - 1) + block_shape, part.dtype),
            pltpu.VMEM((ways, n - 2) + block_shape, part.dtype),
            pltpu.SemaphoreType.DMA((ways, n - 1)),
            pltpu.SemaphoreType.DMA((ways, n - 1)),
        ],
        compiler_params=pltpu.CompilerParams(collective_id=0, has_side_effects=True),
    )(part)


def hand_over(kv_pool, page_target):
    rep_size = lax.axis_size("rep")
    owners = jnp.arange(rep_size, dtype=jnp.int32)
    selected = (page_target[None, :] == owners[:, None])[:, :, None, None, None]
    outgoing = jnp.where(selected, kv_pool[None], jnp.zeros((), kv_pool.dtype))
    incoming = lax.all_to_all(outgoing, "rep", split_axis=0, concat_axis=0, tiled=True)
    return jnp.sum(incoming, axis=0)


def on_device(
    residual,
    queries,
    kv_pool,
    prior_len,
    page_table,
    page_target,
    out_weight,
    moe_gain,
    expert_ids,
    expert_gates,
    w_gate,
    w_up,
    w_down,
):
    tp_size = lax.axis_size("z") * lax.axis_size("y")
    dec_size = lax.axis_size("dec")
    dec_index = lax.axis_index("dec")
    slots_dev, kv_heads, page_rows, both_dim = kv_pool.shape
    head_dim = both_dim // 2
    heads_dev = queries.shape[3] // head_dim
    group_size = QH // KVH
    kv_dev = max(1, heads_dev // group_size)
    copies = max(1, group_size // heads_dev)
    per_kv = heads_dev // kv_dev
    requests = prior_len.shape[0]
    tok_dev = queries.shape[2]
    half_rows = queries.shape[0] * tok_dev // requests
    pages_max = page_table.shape[1]
    team_size = tp_size * dec_size
    z_size = lax.axis_size("z")
    plane_size = team_size // z_size
    spread = kv_pool.reshape(slots_dev, z_size, kv_dev, page_rows, both_dim)
    spread = jnp.swapaxes(spread, 0, 1)
    by_plane = lax.all_to_all(spread, "z", split_axis=0, concat_axis=0, tiled=True)
    outgoing = jnp.broadcast_to(by_plane[None], (plane_size,) + by_plane.shape)
    received = lax.all_to_all(outgoing, ("y", "dec"), split_axis=0, concat_axis=0, tiled=True)
    received = jnp.swapaxes(received, 0, 1)
    received = received.reshape(team_size * slots_dev, kv_dev, page_rows, both_dim)
    gathered_pages = received[page_table % (team_size * slots_dev)]
    keys_part = gathered_pages[..., :head_dim]
    values_part = gathered_pages[..., head_dim:]
    query_rows = queries.reshape(requests, half_rows, kv_dev, per_kv, head_dim)
    key_count = pages_max * page_rows
    scores = jnp.einsum(
        "rukgd,rpkwd->rukgpw", query_rows, keys_part, preferred_element_type=jnp.float32
    )
    scores = scores.reshape(requests, half_rows, kv_dev, per_kv, key_count) * head_dim ** (-0.5)
    position = jnp.arange(key_count, dtype=jnp.int32)
    local_row = jnp.arange(half_rows, dtype=jnp.int32)
    offset = (local_row // tok_dev * dec_size + dec_index) * tok_dev + local_row % tok_dev
    last_seen = prior_len[:, None] + offset[None, :]
    visible = (position[None, None, :] <= last_seen[:, :, None])[:, :, None, None, :]
    scores = jnp.where(visible, scores, -1e30)
    row_top = jnp.max(scores, axis=-1, keepdims=True)
    raw_weights = jnp.where(visible, jnp.exp(scores - row_top), 0.0)
    totals = jnp.sum(raw_weights, axis=-1)
    weights_low = raw_weights.astype(jnp.bfloat16).reshape(
        requests, half_rows, kv_dev, per_kv, pages_max, page_rows
    )
    weighted = jnp.einsum(
        "rukgpw,rpkwd->rukgd", weights_low, values_part, preferred_element_type=jnp.float32
    )
    attended = (
        (weighted / totals[..., None])
        .astype(jnp.bfloat16)
        .reshape(requests * half_rows, heads_dev * head_dim)
    )
    partial = jnp.dot(attended, out_weight, preferred_element_type=jnp.float32).astype(jnp.bfloat16)
    y_size = lax.axis_size("y")
    width = partial.shape[1]
    partial = partial.reshape(z_size, y_size, tok_dev, 2, width // 2)
    partial = jnp.transpose(partial, (3, 0, 1, 2, 4))
    plane_sum = ring_reduce_scatter(partial)
    plane_sum = jnp.transpose(plane_sum, (1, 2, 0, 3)).reshape(y_size, tok_dev, width)
    pieces = lax.all_to_all(plane_sum.astype(jnp.bfloat16), "y", split_axis=0, concat_axis=0, tiled=True)
    projected = jnp.sum(pieces.astype(jnp.float32), axis=0)
    mid_state = residual.astype(jnp.float32) + projected
    routed_dev = tok_dev * TOPK // EXPERTS
    row_lists = []
    gate_lists = []
    for expert in range(EXP_WIN):
        names_it = expert_ids == expert
        chosen_rows = jnp.nonzero(jnp.any(names_it, axis=-1), size=routed_dev)[0].astype(jnp.int32)
        row_lists.append(chosen_rows)
        gate_lists.append(jnp.sum(jnp.where(names_it, expert_gates, 0.0), axis=-1)[chosen_rows])
    picked_rows = jnp.stack(row_lists, axis=0)
    picked_gates = jnp.stack(gate_lists, axis=0)
    inverse = lax.rsqrt(jnp.mean(mid_state * mid_state, axis=-1, keepdims=True) + 1e-05)
    normed_all = (mid_state * inverse * moe_gain).astype(jnp.bfloat16)
    width = normed_all.shape[1]
    by_expert = normed_all[picked_rows]
    outgoing = jnp.broadcast_to(by_expert[None], (tp_size, dec_size, routed_dev, width))
    outgoing = outgoing.reshape(team_size, routed_dev, width)
    row_piece = lax.all_to_all(outgoing, ("z", "y", "dec"), split_axis=0, concat_axis=0, tiled=True)
    row_piece = row_piece.reshape(team_size * routed_dev, width)
    gate_part = jnp.dot(row_piece, w_gate[0].T, preferred_element_type=jnp.float32)
    up_part = jnp.dot(row_piece, w_up[0].T, preferred_element_type=jnp.float32)
    hidden = (jax.nn.silu(gate_part) * up_part).astype(jnp.bfloat16)
    expert_part = jnp.dot(hidden, w_down[0], preferred_element_type=jnp.float32).astype(jnp.bfloat16)
    expert_part = expert_part.reshape(team_size, routed_dev, width)
    returned = lax.all_to_all(expert_part, ("z", "y", "dec"), split_axis=0, concat_axis=0, tiled=True)
    returned = returned.reshape(tp_size, dec_size, routed_dev, width).astype(jnp.float32)
    expert_out = jnp.sum(returned, axis=0)
    mixture = jnp.zeros_like(mid_state)
    for expert in range(EXP_WIN):
        mixture = mixture.at[picked_rows[expert]].add(
            expert_out[expert] * picked_gates[expert][:, None]
        )
    layer_out = (mid_state + mixture).astype(jnp.bfloat16)
    decode_pages = hand_over(kv_pool, page_target)
    return (layer_out, decode_pages)


def fine_mesh(mesh):
    tp_devices = mesh.devices[0, :, 0]
    y_size = len({device.coords[1] for device in tp_devices})
    shape = (mesh.shape["rep"], mesh.shape["tp"] // y_size, y_size, mesh.shape["dec"])
    return jax.sharding.Mesh(mesh.devices.reshape(shape), ("rep", "z", "y", "dec"))


def solution(mesh):
    team = ("rep", "z", "y", "dec")
    return jax.shard_map(
        on_device,
        mesh=fine_mesh(mesh),
        in_specs=(
            P(team, None),
            P("rep", "dec", None, ("z", "y")),
            P(team, None, None, None),
            P("rep"),
            P("rep", None),
            P(team),
            P(("z", "y"), None),
            P(),
            P(team, None),
            P(team, None),
            P("dec", ("z", "y"), None),
            P("dec", ("z", "y"), None),
            P("dec", ("z", "y"), None),
        ),
        out_specs=(P(team, None), P(team, None, None, None)),
        check_vma=False,
    )
```

```python
import jax
import jax.numpy as jnp
from jax import lax
from jax.sharding import PartitionSpec as P
from jax.experimental import pallas as pl
from jax.experimental.pallas import tpu as pltpu

QH = 32
KVH = 8
EXPERTS = 8
TOPK = 2
EXP_WIN = 2


MESH = pl.DeviceIdType.MESH

def _ring_kernel(rows_ref, weight_ref, out_ref, recv_buf, send_buf, send_sem, recv_sem):
    n = recv_buf.shape[1] + 1
    half = recv_buf.shape[2]
    me = lax.axis_index("z")
    rep = lax.axis_index("rep")
    yy = lax.axis_index("y")
    dd = lax.axis_index("dec")
    right = lax.rem(me + 1, n)
    left = lax.rem(me + n - 1, n)

    def block_part(block, way):
        start = pl.multiple_of(block * (2 * half) + way * half, half)
        piece = rows_ref[pl.ds(start, half), :]
        return jnp.dot(piece, weight_ref[...], preferred_element_type=jnp.float32)

    barrier = pltpu.get_barrier_semaphore()
    for neighbour in (left, right):
        pl.semaphore_signal(barrier, inc=1, device_id=(rep, neighbour, yy, dd), device_id_type=MESH)
    pl.semaphore_wait(barrier, 2)
    for way in range(2):
        if way == 0:
            block = lax.rem(me + n - 1, n)
        else:
            block = lax.rem(me + 1, n)
        send_buf[way, 0] = block_part(block, way).astype(send_buf.dtype)
    for step in range(n - 1):
        copies = []
        for way in range(2):
            target = right if way == 0 else left
            copy = pltpu.make_async_remote_copy(
                src_ref=send_buf.at[way, step],
                dst_ref=recv_buf.at[way, step],
                send_sem=send_sem.at[way, step],
                recv_sem=recv_sem.at[way, step],
                device_id=(rep, target, yy, dd),
                device_id_type=MESH,
            )
            copy.start()
            copies.append(copy)
        for way in range(2):
            if way == 0:
                block = lax.rem(me + 2 * n - 2 - step, n)
            else:
                block = lax.rem(me + 2 + step, n)
            own = block_part(block, way)
            copies[way].wait()
            total = recv_buf[way, step].astype(jnp.float32) + own
            if step < n - 2:
                send_buf[way, step + 1] = total.astype(send_buf.dtype)
            else:
                out_ref[pl.ds(way * half, half), :] = total


def ring_reduce_scatter(rows, weight, n):
    half = rows.shape[0] // (2 * n)
    width = weight.shape[1]
    return pl.pallas_call(
        _ring_kernel,
        out_shape=jax.ShapeDtypeStruct((2 * half, width), jnp.float32),
        in_specs=[pl.BlockSpec(memory_space=pltpu.VMEM)] * 2,
        out_specs=pl.BlockSpec(memory_space=pltpu.VMEM),
        scratch_shapes=[
            pltpu.VMEM((2, n - 1, half, width), jnp.bfloat16),
            pltpu.VMEM((2, n - 1, half, width), jnp.bfloat16),
            pltpu.SemaphoreType.DMA((2, n - 1)),
            pltpu.SemaphoreType.DMA((2, n - 1)),
        ],
        compiler_params=pltpu.CompilerParams(collective_id=0, has_side_effects=True),
    )(rows, weight)


def hand_over(kv_pool, page_target):
    rep_size = lax.axis_size("rep")
    owners = jnp.arange(rep_size, dtype=jnp.int32)
    selected = (page_target[None, :] == owners[:, None])[:, :, None, None, None]
    outgoing = jnp.where(selected, kv_pool[None], jnp.zeros((), kv_pool.dtype))
    incoming = lax.all_to_all(outgoing, "rep", split_axis=0, concat_axis=0, tiled=True)
    return jnp.sum(incoming, axis=0)


def on_device(
    residual,
    queries,
    kv_pool,
    prior_len,
    page_table,
    page_target,
    out_weight,
    moe_gain,
    expert_ids,
    expert_gates,
    w_gate,
    w_up,
    w_down,
):
    tp_size = lax.axis_size("z") * lax.axis_size("y")
    dec_size = lax.axis_size("dec")
    dec_index = lax.axis_index("dec")
    slots_dev, kv_heads, page_rows, both_dim = kv_pool.shape
    head_dim = both_dim // 2
    heads_dev = queries.shape[3] // head_dim
    group_size = QH // KVH
    kv_dev = max(1, heads_dev // group_size)
    copies = max(1, group_size // heads_dev)
    per_kv = heads_dev // kv_dev
    requests = prior_len.shape[0]
    tok_dev = queries.shape[2]
    half_rows = queries.shape[0] * tok_dev // requests
    pages_max = page_table.shape[1]
    team_size = tp_size * dec_size
    z_size = lax.axis_size("z")
    plane_size = team_size // z_size
    spread = kv_pool.reshape(slots_dev, z_size, kv_dev, page_rows, both_dim)
    spread = jnp.swapaxes(spread, 0, 1)
    by_plane = lax.all_to_all(spread, "z", split_axis=0, concat_axis=0, tiled=True)
    outgoing = jnp.broadcast_to(by_plane[None], (plane_size,) + by_plane.shape)
    received = lax.all_to_all(outgoing, ("y", "dec"), split_axis=0, concat_axis=0, tiled=True)
    received = jnp.swapaxes(received, 0, 1)
    received = received.reshape(team_size * slots_dev, kv_dev, page_rows, both_dim)
    gathered_pages = received[page_table % (team_size * slots_dev)]
    keys_part = gathered_pages[..., :head_dim]
    values_part = gathered_pages[..., head_dim:]
    query_rows = queries.reshape(requests, half_rows, kv_dev, per_kv, head_dim)
    key_count = pages_max * page_rows
    scores = jnp.einsum(
        "rukgd,rpkwd->rukgpw", query_rows, keys_part, preferred_element_type=jnp.float32
    )
    scores = scores.reshape(requests, half_rows, kv_dev, per_kv, key_count) * head_dim ** (-0.5)
    position = jnp.arange(key_count, dtype=jnp.int32)
    local_row = jnp.arange(half_rows, dtype=jnp.int32)
    offset = (local_row // tok_dev * dec_size + dec_index) * tok_dev + local_row % tok_dev
    last_seen = prior_len[:, None] + offset[None, :]
    visible = (position[None, None, :] <= last_seen[:, :, None])[:, :, None, None, :]
    scores = jnp.where(visible, scores, -1e30)
    row_top = jnp.max(scores, axis=-1, keepdims=True)
    raw_weights = jnp.where(visible, jnp.exp(scores - row_top), 0.0)
    totals = jnp.sum(raw_weights, axis=-1)
    weights_low = raw_weights.astype(jnp.bfloat16).reshape(
        requests, half_rows, kv_dev, per_kv, pages_max, page_rows
    )
    weighted = jnp.einsum(
        "rukgpw,rpkwd->rukgd", weights_low, values_part, preferred_element_type=jnp.float32
    )
    attended = (
        (weighted / totals[..., None])
        .astype(jnp.bfloat16)
        .reshape(requests * half_rows, heads_dev * head_dim)
    )
    y_size = lax.axis_size("y")
    width = out_weight.shape[1]
    plane_sum = ring_reduce_scatter(attended, out_weight, z_size).reshape(y_size, tok_dev, width)
    pieces = lax.all_to_all(plane_sum.astype(jnp.bfloat16), "y", split_axis=0, concat_axis=0, tiled=True)
    projected = jnp.sum(pieces.astype(jnp.float32), axis=0)
    mid_state = residual.astype(jnp.float32) + projected
    routed_dev = tok_dev * TOPK // EXPERTS
    row_lists = []
    gate_lists = []
    for expert in range(EXP_WIN):
        names_it = expert_ids == expert
        chosen_rows = jnp.nonzero(jnp.any(names_it, axis=-1), size=routed_dev)[0].astype(jnp.int32)
        row_lists.append(chosen_rows)
        gate_lists.append(jnp.sum(jnp.where(names_it, expert_gates, 0.0), axis=-1)[chosen_rows])
    picked_rows = jnp.stack(row_lists, axis=0)
    picked_gates = jnp.stack(gate_lists, axis=0)
    inverse = lax.rsqrt(jnp.mean(mid_state * mid_state, axis=-1, keepdims=True) + 1e-05)
    normed_all = (mid_state * inverse * moe_gain).astype(jnp.bfloat16)
    width = normed_all.shape[1]
    by_expert = normed_all[picked_rows]
    outgoing = jnp.broadcast_to(by_expert[None], (tp_size, dec_size, routed_dev, width))
    outgoing = outgoing.reshape(team_size, routed_dev, width)
    row_piece = lax.all_to_all(outgoing, ("z", "y", "dec"), split_axis=0, concat_axis=0, tiled=True)
    row_piece = row_piece.reshape(team_size * routed_dev, width)
    gate_part = jnp.dot(row_piece, w_gate[0].T, preferred_element_type=jnp.float32)
    up_part = jnp.dot(row_piece, w_up[0].T, preferred_element_type=jnp.float32)
    hidden = (jax.nn.silu(gate_part) * up_part).astype(jnp.bfloat16)
    expert_part = jnp.dot(hidden, w_down[0], preferred_element_type=jnp.float32).astype(jnp.bfloat16)
    expert_part = expert_part.reshape(team_size, routed_dev, width)
    returned = lax.all_to_all(expert_part, ("z", "y", "dec"), split_axis=0, concat_axis=0, tiled=True)
    returned = returned.reshape(tp_size, dec_size, routed_dev, width).astype(jnp.float32)
    expert_out = jnp.sum(returned, axis=0)
    mixture = jnp.zeros_like(mid_state)
    for expert in range(EXP_WIN):
        mixture = mixture.at[picked_rows[expert]].add(
            expert_out[expert] * picked_gates[expert][:, None]
        )
    layer_out = (mid_state + mixture).astype(jnp.bfloat16)
    decode_pages = hand_over(kv_pool, page_target)
    return (layer_out, decode_pages)


def fine_mesh(mesh):
    tp_devices = mesh.devices[0, :, 0]
    y_size = len({device.coords[1] for device in tp_devices})
    shape = (mesh.shape["rep"], mesh.shape["tp"] // y_size, y_size, mesh.shape["dec"])
    return jax.sharding.Mesh(mesh.devices.reshape(shape), ("rep", "z", "y", "dec"))


def solution(mesh):
    team = ("rep", "z", "y", "dec")
    return jax.shard_map(
        on_device,
        mesh=fine_mesh(mesh),
        in_specs=(
            P(team, None),
            P("rep", "dec", None, ("z", "y")),
            P(team, None, None, None),
            P("rep"),
            P("rep", None),
            P(team),
            P(("z", "y"), None),
            P(),
            P(team, None),
            P(team, None),
            P("dec", ("z", "y"), None),
            P("dec", ("z", "y"), None),
            P("dec", ("z", "y"), None),
        ),
        out_specs=(P(team, None), P(team, None, None, None)),
        check_vma=False,
    )
```

```python
import jax
import jax.numpy as jnp
from jax import lax
from jax.sharding import PartitionSpec as P
from jax.experimental import pallas as pl
from jax.experimental.pallas import tpu as pltpu

QH = 32
KVH = 8
EXPERTS = 8
TOPK = 2
EXP_WIN = 2


MESH = pl.DeviceIdType.MESH

def _ring_phase(rings):
    for ring in rings:
        for way in range(2):
            block = ring["first"](way)
            for index, piece in enumerate(ring["own"](block, way)):
                ring["send"][way, 0, index] = piece.astype(ring["send"].dtype)
    longest = max(ring["n"] for ring in rings)
    for step in range(longest - 1):
        live = [ring for ring in rings if step < ring["n"] - 1]
        copies = {}
        for number, ring in enumerate(live):
            for way in range(2):
                copy = pltpu.make_async_remote_copy(
                    src_ref=ring["send"].at[way, step],
                    dst_ref=ring["recv"].at[way, step],
                    send_sem=ring["send_sem"].at[way, step],
                    recv_sem=ring["recv_sem"].at[way, step],
                    device_id=ring["targets"][way],
                    device_id_type=MESH,
                )
                copy.start()
                copies[number, way] = copy
        for number, ring in enumerate(live):
            for way in range(2):
                block = ring["later"](step, way)
                pieces = ring["own"](block, way)
                copies[number, way].wait()
                for index, piece in enumerate(pieces):
                    total = ring["recv"][way, step, index].astype(jnp.float32) + piece
                    if step < ring["n"] - 2:
                        ring["send"][way, step + 1, index] = total.astype(ring["send"].dtype)
                    else:
                        ring["store"](way, index, total)


def _plane_kernel(rows_ref, weight_ref, out_ref, z1_send, z1_recv, y1_send, y1_recv,
                  z2_send, z2_recv, y2_send, y2_recv, z_done, y_done, *sems):
    nz = z1_recv.shape[1] + 1
    ny = y1_recv.shape[1] + 1
    rows, width = out_ref.shape
    half = width // 2
    quarter = width // 4
    mz = lax.axis_index("z")
    my = lax.axis_index("y")
    rep = lax.axis_index("rep")
    dd = lax.axis_index("dec")
    z_targets = ((rep, lax.rem(mz + 1, nz), my, dd), (rep, lax.rem(mz + nz - 1, nz), my, dd))
    y_targets = ((rep, mz, lax.rem(my + 1, ny), dd), (rep, mz, lax.rem(my + ny - 1, ny), dd))
    barrier = pltpu.get_barrier_semaphore()
    for target in z_targets + y_targets:
        pl.semaphore_signal(barrier, inc=1, device_id=target, device_id_type=MESH)
    pl.semaphore_wait(barrier, 4)

    def product(start, columns):
        piece = rows_ref[pl.ds(pl.multiple_of(start, rows), rows), :]
        return jnp.dot(piece, weight_ref[:, columns], preferred_element_type=jnp.float32)

    def z1_own(block, way):
        return [product((block * ny + way * (ny // 2) + i) * rows, slice(0, half))
                for i in range(ny // 2)]

    def y1_own(block, way):
        return [product(((way * (nz // 2) + i) * ny + block) * rows, slice(half, width))
                for i in range(nz // 2)]

    def z1_store(way, index, total):
        z_done[way * (ny // 2) + index] = total

    def y1_store(way, index, total):
        y_done[way * (nz // 2) + index] = total

    def z2_own(block, way):
        return [y_done[block, :, pl.ds(way * quarter, quarter)]]

    def y2_own(block, way):
        return [z_done[block, :, pl.ds(way * quarter, quarter)]]

    def z2_store(way, index, total):
        out_ref[:, pl.ds(half + way * quarter, quarter)] = total

    def y2_store(way, index, total):
        out_ref[:, pl.ds(way * quarter, quarter)] = total

    def ring(n, me, targets, send, recv, send_sem, recv_sem, own, store):
        return dict(
            n=n, targets=targets, send=send, recv=recv, send_sem=send_sem, recv_sem=recv_sem,
            own=own, store=store,
            first=lambda way: lax.rem(me + n - 1, n) if way == 0 else lax.rem(me + 1, n),
            later=lambda step, way: (
                lax.rem(me + 2 * n - 2 - step, n) if way == 0 else lax.rem(me + 2 + step, n)
            ),
        )

    _ring_phase([
        ring(nz, mz, z_targets, z1_send, z1_recv, sems[0], sems[1], z1_own, z1_store),
        ring(ny, my, y_targets, y1_send, y1_recv, sems[2], sems[3], y1_own, y1_store),
    ])
    _ring_phase([
        ring(nz, mz, z_targets, z2_send, z2_recv, sems[4], sems[5], z2_own, z2_store),
        ring(ny, my, y_targets, y2_send, y2_recv, sems[6], sems[7], y2_own, y2_store),
    ])


def plane_reduce_scatter(rows_in, weight, nz, ny, call_id):
    rows = rows_in.shape[0] // (nz * ny)
    width = weight.shape[1]
    half = width // 2
    quarter = width // 4
    link = jnp.bfloat16
    return pl.pallas_call(
        _plane_kernel,
        out_shape=jax.ShapeDtypeStruct((rows, width), jnp.float32),
        in_specs=[pl.BlockSpec(memory_space=pltpu.VMEM)] * 2,
        out_specs=pl.BlockSpec(memory_space=pltpu.VMEM),
        scratch_shapes=[
            pltpu.VMEM((2, nz - 1, ny // 2, rows, half), link),
            pltpu.VMEM((2, nz - 1, ny // 2, rows, half), link),
            pltpu.VMEM((2, ny - 1, nz // 2, rows, half), link),
            pltpu.VMEM((2, ny - 1, nz // 2, rows, half), link),
            pltpu.VMEM((2, nz - 1, 1, rows, quarter), link),
            pltpu.VMEM((2, nz - 1, 1, rows, quarter), link),
            pltpu.VMEM((2, ny - 1, 1, rows, quarter), link),
            pltpu.VMEM((2, ny - 1, 1, rows, quarter), link),
            pltpu.VMEM((ny, rows, half), jnp.float32),
            pltpu.VMEM((nz, rows, half), jnp.float32),
        ]
        + [pltpu.SemaphoreType.DMA((2, nz - 1))] * 2
        + [pltpu.SemaphoreType.DMA((2, ny - 1))] * 2
        + [pltpu.SemaphoreType.DMA((2, nz - 1))] * 2
        + [pltpu.SemaphoreType.DMA((2, ny - 1))] * 2,
        compiler_params=pltpu.CompilerParams(collective_id=call_id, has_side_effects=True),
    )(rows_in, weight)


def hand_over(kv_pool, page_target):
    rep_size = lax.axis_size("rep")
    owners = jnp.arange(rep_size, dtype=jnp.int32)
    selected = (page_target[None, :] == owners[:, None])[:, :, None, None, None]
    outgoing = jnp.where(selected, kv_pool[None], jnp.zeros((), kv_pool.dtype))
    incoming = lax.all_to_all(outgoing, "rep", split_axis=0, concat_axis=0, tiled=True)
    return jnp.sum(incoming, axis=0)


def on_device(
    residual,
    queries,
    kv_pool,
    prior_len,
    page_table,
    page_target,
    out_weight,
    moe_gain,
    expert_ids,
    expert_gates,
    w_gate,
    w_up,
    w_down,
):
    tp_size = lax.axis_size("z") * lax.axis_size("y")
    dec_size = lax.axis_size("dec")
    dec_index = lax.axis_index("dec")
    slots_dev, kv_heads, page_rows, both_dim = kv_pool.shape
    head_dim = both_dim // 2
    heads_dev = queries.shape[3] // head_dim
    group_size = QH // KVH
    kv_dev = max(1, heads_dev // group_size)
    copies = max(1, group_size // heads_dev)
    per_kv = heads_dev // kv_dev
    requests = prior_len.shape[0]
    tok_dev = queries.shape[2]
    half_rows = queries.shape[0] * tok_dev // requests
    pages_max = page_table.shape[1]
    team_size = tp_size * dec_size
    z_size = lax.axis_size("z")
    plane_size = team_size // z_size
    spread = kv_pool.reshape(slots_dev, z_size, kv_dev, page_rows, both_dim)
    spread = jnp.swapaxes(spread, 0, 1)
    by_plane = lax.all_to_all(spread, "z", split_axis=0, concat_axis=0, tiled=True)
    outgoing = jnp.broadcast_to(by_plane[None], (plane_size,) + by_plane.shape)
    received = lax.all_to_all(outgoing, ("y", "dec"), split_axis=0, concat_axis=0, tiled=True)
    received = jnp.swapaxes(received, 0, 1)
    received = received.reshape(team_size * slots_dev, kv_dev, page_rows, both_dim)
    gathered_pages = received[page_table % (team_size * slots_dev)]
    keys_part = gathered_pages[..., :head_dim]
    values_part = gathered_pages[..., head_dim:]
    query_rows = queries.reshape(requests, half_rows, kv_dev, per_kv, head_dim)
    key_count = pages_max * page_rows
    scores = jnp.einsum(
        "rukgd,rpkwd->rukgpw", query_rows, keys_part, preferred_element_type=jnp.float32
    )
    scores = scores.reshape(requests, half_rows, kv_dev, per_kv, key_count) * head_dim ** (-0.5)
    position = jnp.arange(key_count, dtype=jnp.int32)
    local_row = jnp.arange(half_rows, dtype=jnp.int32)
    offset = (local_row // tok_dev * dec_size + dec_index) * tok_dev + local_row % tok_dev
    last_seen = prior_len[:, None] + offset[None, :]
    visible = (position[None, None, :] <= last_seen[:, :, None])[:, :, None, None, :]
    scores = jnp.where(visible, scores, -1e30)
    row_top = jnp.max(scores, axis=-1, keepdims=True)
    raw_weights = jnp.where(visible, jnp.exp(scores - row_top), 0.0)
    totals = jnp.sum(raw_weights, axis=-1)
    weights_low = raw_weights.astype(jnp.bfloat16).reshape(
        requests, half_rows, kv_dev, per_kv, pages_max, page_rows
    )
    weighted = jnp.einsum(
        "rukgpw,rpkwd->rukgd", weights_low, values_part, preferred_element_type=jnp.float32
    )
    attended = (
        (weighted / totals[..., None])
        .astype(jnp.bfloat16)
        .reshape(requests * half_rows, heads_dev * head_dim)
    )
    y_size = lax.axis_size("y")
    projected = plane_reduce_scatter(attended, out_weight, z_size, y_size, 0)
    mid_state = residual.astype(jnp.float32) + projected
    routed_dev = tok_dev * TOPK // EXPERTS
    row_lists = []
    gate_lists = []
    for expert in range(EXP_WIN):
        names_it = expert_ids == expert
        chosen_rows = jnp.nonzero(jnp.any(names_it, axis=-1), size=routed_dev)[0].astype(jnp.int32)
        row_lists.append(chosen_rows)
        gate_lists.append(jnp.sum(jnp.where(names_it, expert_gates, 0.0), axis=-1)[chosen_rows])
    picked_rows = jnp.stack(row_lists, axis=0)
    picked_gates = jnp.stack(gate_lists, axis=0)
    inverse = lax.rsqrt(jnp.mean(mid_state * mid_state, axis=-1, keepdims=True) + 1e-05)
    normed_all = (mid_state * inverse * moe_gain).astype(jnp.bfloat16)
    width = normed_all.shape[1]
    by_expert = normed_all[picked_rows]
    outgoing = jnp.broadcast_to(by_expert[None], (tp_size, dec_size, routed_dev, width))
    outgoing = outgoing.reshape(team_size, routed_dev, width)
    row_piece = lax.all_to_all(outgoing, ("z", "y", "dec"), split_axis=0, concat_axis=0, tiled=True)
    row_piece = row_piece.reshape(team_size * routed_dev, width)
    gate_part = jnp.dot(row_piece, w_gate[0].T, preferred_element_type=jnp.float32)
    up_part = jnp.dot(row_piece, w_up[0].T, preferred_element_type=jnp.float32)
    hidden = (jax.nn.silu(gate_part) * up_part).astype(jnp.bfloat16)
    expert_part = jnp.dot(hidden, w_down[0], preferred_element_type=jnp.float32).astype(jnp.bfloat16)
    expert_part = expert_part.reshape(team_size, routed_dev, width)
    returned = lax.all_to_all(expert_part, ("z", "y", "dec"), split_axis=0, concat_axis=0, tiled=True)
    returned = returned.reshape(tp_size, dec_size, routed_dev, width).astype(jnp.float32)
    expert_out = jnp.sum(returned, axis=0)
    mixture = jnp.zeros_like(mid_state)
    for expert in range(EXP_WIN):
        mixture = mixture.at[picked_rows[expert]].add(
            expert_out[expert] * picked_gates[expert][:, None]
        )
    layer_out = (mid_state + mixture).astype(jnp.bfloat16)
    decode_pages = hand_over(kv_pool, page_target)
    return (layer_out, decode_pages)


def fine_mesh(mesh):
    tp_devices = mesh.devices[0, :, 0]
    y_size = len({device.coords[1] for device in tp_devices})
    shape = (mesh.shape["rep"], mesh.shape["tp"] // y_size, y_size, mesh.shape["dec"])
    return jax.sharding.Mesh(mesh.devices.reshape(shape), ("rep", "z", "y", "dec"))


def solution(mesh):
    team = ("rep", "z", "y", "dec")
    return jax.shard_map(
        on_device,
        mesh=fine_mesh(mesh),
        in_specs=(
            P(team, None),
            P("rep", "dec", None, ("z", "y")),
            P(team, None, None, None),
            P("rep"),
            P("rep", None),
            P(team),
            P(("z", "y"), None),
            P(),
            P(team, None),
            P(team, None),
            P("dec", ("z", "y"), None),
            P("dec", ("z", "y"), None),
            P("dec", ("z", "y"), None),
        ),
        out_specs=(P(team, None), P(team, None, None, None)),
        check_vma=False,
    )
```

```python
import jax
import jax.numpy as jnp
from jax import lax
from jax.sharding import PartitionSpec as P
from jax.experimental import pallas as pl
from jax.experimental.pallas import tpu as pltpu

QH = 32
KVH = 8
EXPERTS = 8
TOPK = 2
EXP_WIN = 2


MESH = pl.DeviceIdType.MESH

def _ring_kernel(rows_ref, weight_ref, out_ref, recv_buf, send_buf, send_sem, recv_sem):
    n = recv_buf.shape[1] + 1
    half = recv_buf.shape[2]
    me = lax.axis_index("z")
    rep = lax.axis_index("rep")
    yy = lax.axis_index("y")
    dd = lax.axis_index("dec")
    right = lax.rem(me + 1, n)
    left = lax.rem(me + n - 1, n)

    def block_part(block, way):
        start = pl.multiple_of(block * (2 * half) + way * half, half)
        piece = rows_ref[pl.ds(start, half), :]
        return jnp.dot(piece, weight_ref[...], preferred_element_type=jnp.float32)

    barrier = pltpu.get_barrier_semaphore()
    for neighbour in (left, right):
        pl.semaphore_signal(barrier, inc=1, device_id=(rep, neighbour, yy, dd), device_id_type=MESH)
    pl.semaphore_wait(barrier, 2)
    for way in range(2):
        if way == 0:
            block = lax.rem(me + n - 1, n)
        else:
            block = lax.rem(me + 1, n)
        send_buf[way, 0] = block_part(block, way).astype(send_buf.dtype)
    for step in range(n - 1):
        copies = []
        for way in range(2):
            target = right if way == 0 else left
            copy = pltpu.make_async_remote_copy(
                src_ref=send_buf.at[way, step],
                dst_ref=recv_buf.at[way, step],
                send_sem=send_sem.at[way, step],
                recv_sem=recv_sem.at[way, step],
                device_id=(rep, target, yy, dd),
                device_id_type=MESH,
            )
            copy.start()
            copies.append(copy)
        for way in range(2):
            if way == 0:
                block = lax.rem(me + 2 * n - 2 - step, n)
            else:
                block = lax.rem(me + 2 + step, n)
            own = block_part(block, way)
            copies[way].wait()
            total = recv_buf[way, step].astype(jnp.float32) + own
            if step < n - 2:
                send_buf[way, step + 1] = total.astype(send_buf.dtype)
            else:
                out_ref[pl.ds(way * half, half), :] = total


def ring_reduce_scatter(rows, weight, n, call_id):
    half = rows.shape[0] // (2 * n)
    width = weight.shape[1]
    return pl.pallas_call(
        _ring_kernel,
        out_shape=jax.ShapeDtypeStruct((2 * half, width), jnp.float32),
        in_specs=[pl.BlockSpec(memory_space=pltpu.VMEM)] * 2,
        out_specs=pl.BlockSpec(memory_space=pltpu.VMEM),
        scratch_shapes=[
            pltpu.VMEM((2, n - 1, half, width), jnp.bfloat16),
            pltpu.VMEM((2, n - 1, half, width), jnp.bfloat16),
            pltpu.SemaphoreType.DMA((2, n - 1)),
            pltpu.SemaphoreType.DMA((2, n - 1)),
        ],
        compiler_params=pltpu.CompilerParams(collective_id=call_id, has_side_effects=True),
    )(rows, weight)


def hand_over(kv_pool, page_target):
    rep_size = lax.axis_size("rep")
    owners = jnp.arange(rep_size, dtype=jnp.int32)
    selected = (page_target[None, :] == owners[:, None])[:, :, None, None, None]
    outgoing = jnp.where(selected, kv_pool[None], jnp.zeros((), kv_pool.dtype))
    incoming = lax.all_to_all(outgoing, "rep", split_axis=0, concat_axis=0, tiled=True)
    return jnp.sum(incoming, axis=0)


def on_device(
    residual,
    queries,
    kv_pool,
    prior_len,
    page_table,
    page_target,
    out_weight,
    moe_gain,
    expert_ids,
    expert_gates,
    w_gate,
    w_up,
    w_down,
):
    tp_size = lax.axis_size("z") * lax.axis_size("y")
    dec_size = lax.axis_size("dec")
    dec_index = lax.axis_index("dec")
    slots_dev, kv_heads, page_rows, both_dim = kv_pool.shape
    head_dim = both_dim // 2
    heads_dev = queries.shape[3] // head_dim
    group_size = QH // KVH
    kv_dev = max(1, heads_dev // group_size)
    copies = max(1, group_size // heads_dev)
    per_kv = heads_dev // kv_dev
    requests = prior_len.shape[0]
    tok_dev = queries.shape[2]
    half_rows = queries.shape[0] * tok_dev // requests
    pages_max = page_table.shape[1]
    team_size = tp_size * dec_size
    z_size = lax.axis_size("z")
    plane_size = team_size // z_size
    spread = kv_pool.reshape(slots_dev, z_size, kv_dev, page_rows, both_dim)
    spread = jnp.swapaxes(spread, 0, 1)
    by_plane = lax.all_to_all(spread, "z", split_axis=0, concat_axis=0, tiled=True)
    outgoing = jnp.broadcast_to(by_plane[None], (plane_size,) + by_plane.shape)
    received = lax.all_to_all(outgoing, ("y", "dec"), split_axis=0, concat_axis=0, tiled=True)
    received = jnp.swapaxes(received, 0, 1)
    received = received.reshape(team_size * slots_dev, kv_dev, page_rows, both_dim)
    gathered_pages = received[page_table % (team_size * slots_dev)]
    keys_part = gathered_pages[..., :head_dim]
    values_part = gathered_pages[..., head_dim:]
    query_rows = queries.reshape(requests, half_rows, kv_dev, per_kv, head_dim)
    key_count = pages_max * page_rows
    scores = jnp.einsum(
        "rukgd,rpkwd->rukgpw", query_rows, keys_part, preferred_element_type=jnp.float32
    )
    scores = scores.reshape(requests, half_rows, kv_dev, per_kv, key_count) * head_dim ** (-0.5)
    position = jnp.arange(key_count, dtype=jnp.int32)
    local_row = jnp.arange(half_rows, dtype=jnp.int32)
    offset = (local_row // tok_dev * dec_size + dec_index) * tok_dev + local_row % tok_dev
    last_seen = prior_len[:, None] + offset[None, :]
    visible = (position[None, None, :] <= last_seen[:, :, None])[:, :, None, None, :]
    scores = jnp.where(visible, scores, -1e30)
    row_top = jnp.max(scores, axis=-1, keepdims=True)
    raw_weights = jnp.where(visible, jnp.exp(scores - row_top), 0.0)
    totals = jnp.sum(raw_weights, axis=-1)
    weights_low = raw_weights.astype(jnp.bfloat16).reshape(
        requests, half_rows, kv_dev, per_kv, pages_max, page_rows
    )
    weighted = jnp.einsum(
        "rukgpw,rpkwd->rukgd", weights_low, values_part, preferred_element_type=jnp.float32
    )
    attended = (
        (weighted / totals[..., None])
        .astype(jnp.bfloat16)
        .reshape(requests * half_rows, heads_dev * head_dim)
    )
    y_size = lax.axis_size("y")
    width = out_weight.shape[1]
    plane_sum = ring_reduce_scatter(attended, out_weight, z_size, 0).reshape(y_size, tok_dev, width)
    pieces = lax.all_to_all(plane_sum.astype(jnp.bfloat16), "y", split_axis=0, concat_axis=0, tiled=True)
    projected = jnp.sum(pieces.astype(jnp.float32), axis=0)
    mid_state = residual.astype(jnp.float32) + projected
    routed_dev = tok_dev * TOPK // EXPERTS
    row_lists = []
    gate_lists = []
    for expert in range(EXP_WIN):
        names_it = expert_ids == expert
        chosen_rows = jnp.nonzero(jnp.any(names_it, axis=-1), size=routed_dev)[0].astype(jnp.int32)
        row_lists.append(chosen_rows)
        gate_lists.append(jnp.sum(jnp.where(names_it, expert_gates, 0.0), axis=-1)[chosen_rows])
    picked_rows = jnp.stack(row_lists, axis=0)
    picked_gates = jnp.stack(gate_lists, axis=0)
    inverse = lax.rsqrt(jnp.mean(mid_state * mid_state, axis=-1, keepdims=True) + 1e-05)
    normed_all = (mid_state * inverse * moe_gain).astype(jnp.bfloat16)
    width = normed_all.shape[1]
    by_expert = normed_all[picked_rows]
    outgoing = jnp.broadcast_to(by_expert[None], (tp_size, dec_size, routed_dev, width))
    outgoing = outgoing.reshape(team_size, routed_dev, width)
    row_piece = lax.all_to_all(outgoing, ("z", "y", "dec"), split_axis=0, concat_axis=0, tiled=True)
    row_piece = row_piece.reshape(team_size * routed_dev, width)
    gate_part = jnp.dot(row_piece, w_gate[0].T, preferred_element_type=jnp.float32)
    up_part = jnp.dot(row_piece, w_up[0].T, preferred_element_type=jnp.float32)
    hidden = (jax.nn.silu(gate_part) * up_part).astype(jnp.bfloat16)
    expert_part = ring_reduce_scatter(hidden, w_down[0], z_size, 1)
    expert_part = expert_part.reshape(y_size * dec_size, routed_dev, width).astype(jnp.bfloat16)
    returned = lax.all_to_all(expert_part, ("y", "dec"), split_axis=0, concat_axis=0, tiled=True)
    returned = returned.reshape(y_size, dec_size, routed_dev, width).astype(jnp.float32)
    expert_out = jnp.sum(returned, axis=0)
    mixture = jnp.zeros_like(mid_state)
    for expert in range(EXP_WIN):
        mixture = mixture.at[picked_rows[expert]].add(
            expert_out[expert] * picked_gates[expert][:, None]
        )
    layer_out = (mid_state + mixture).astype(jnp.bfloat16)
    decode_pages = hand_over(kv_pool, page_target)
    return (layer_out, decode_pages)


def fine_mesh(mesh):
    tp_devices = mesh.devices[0, :, 0]
    y_size = len({device.coords[1] for device in tp_devices})
    shape = (mesh.shape["rep"], mesh.shape["tp"] // y_size, y_size, mesh.shape["dec"])
    return jax.sharding.Mesh(mesh.devices.reshape(shape), ("rep", "z", "y", "dec"))


def solution(mesh):
    team = ("rep", "z", "y", "dec")
    return jax.shard_map(
        on_device,
        mesh=fine_mesh(mesh),
        in_specs=(
            P(team, None),
            P("rep", "dec", None, ("z", "y")),
            P(team, None, None, None),
            P("rep"),
            P("rep", None),
            P(team),
            P(("z", "y"), None),
            P(),
            P(team, None),
            P(team, None),
            P("dec", ("z", "y"), None),
            P("dec", ("z", "y"), None),
            P("dec", ("z", "y"), None),
        ),
        out_specs=(P(team, None), P(team, None, None, None)),
        check_vma=False,
    )
```

```python
import functools

import jax
import jax.numpy as jnp
from jax import lax
from jax.sharding import PartitionSpec as P
from jax.experimental import pallas as pl
from jax.experimental.pallas import tpu as pltpu

QH = 32
KVH = 8
EXPERTS = 8
TOPK = 2
EXP_WIN = 2


MESH = pl.DeviceIdType.MESH

def _ring_kernel(whole, rows_ref, weight_ref, out_ref, recv_buf, send_buf, send_sem, recv_sem, *product):
    n = recv_buf.shape[1] + 1
    half = recv_buf.shape[2]
    me = lax.axis_index("z")
    rep = lax.axis_index("rep")
    yy = lax.axis_index("y")
    dd = lax.axis_index("dec")
    right = lax.rem(me + 1, n)
    left = lax.rem(me + n - 1, n)

    if whole:
        product[0][...] = jnp.dot(rows_ref[...], weight_ref[...], preferred_element_type=jnp.float32)

    def block_part(block, way):
        start = pl.multiple_of(block * (2 * half) + way * half, half)
        if whole:
            return product[0][pl.ds(start, half), :]
        piece = rows_ref[pl.ds(start, half), :]
        return jnp.dot(piece, weight_ref[...], preferred_element_type=jnp.float32)

    barrier = pltpu.get_barrier_semaphore()
    for neighbour in (left, right):
        pl.semaphore_signal(barrier, inc=1, device_id=(rep, neighbour, yy, dd), device_id_type=MESH)
    pl.semaphore_wait(barrier, 2)
    for way in range(2):
        if way == 0:
            block = lax.rem(me + n - 1, n)
        else:
            block = lax.rem(me + 1, n)
        send_buf[way, 0] = block_part(block, way).astype(send_buf.dtype)
    for step in range(n - 1):
        copies = []
        for way in range(2):
            target = right if way == 0 else left
            copy = pltpu.make_async_remote_copy(
                src_ref=send_buf.at[way, step],
                dst_ref=recv_buf.at[way, step],
                send_sem=send_sem.at[way, step],
                recv_sem=recv_sem.at[way, step],
                device_id=(rep, target, yy, dd),
                device_id_type=MESH,
            )
            copy.start()
            copies.append(copy)
        for way in range(2):
            if way == 0:
                block = lax.rem(me + 2 * n - 2 - step, n)
            else:
                block = lax.rem(me + 2 + step, n)
            own = block_part(block, way)
            copies[way].wait()
            total = recv_buf[way, step].astype(jnp.float32) + own
            if step < n - 2:
                send_buf[way, step + 1] = total.astype(send_buf.dtype)
            else:
                out_ref[pl.ds(way * half, half), :] = total


def ring_reduce_scatter(rows, weight, n, call_id, whole=False):
    half = rows.shape[0] // (2 * n)
    width = weight.shape[1]
    return pl.pallas_call(
        functools.partial(_ring_kernel, whole),
        out_shape=jax.ShapeDtypeStruct((2 * half, width), jnp.float32),
        in_specs=[pl.BlockSpec(memory_space=pltpu.VMEM)] * 2,
        out_specs=pl.BlockSpec(memory_space=pltpu.VMEM),
        scratch_shapes=[
            pltpu.VMEM((2, n - 1, half, width), jnp.bfloat16),
            pltpu.VMEM((2, n - 1, half, width), jnp.bfloat16),
            pltpu.SemaphoreType.DMA((2, n - 1)),
            pltpu.SemaphoreType.DMA((2, n - 1)),
        ]
        + ([pltpu.VMEM((rows.shape[0], width), jnp.float32)] if whole else []),
        compiler_params=pltpu.CompilerParams(collective_id=call_id, has_side_effects=True),
    )(rows, weight)


def hand_over(kv_pool, page_target):
    rep_size = lax.axis_size("rep")
    owners = jnp.arange(rep_size, dtype=jnp.int32)
    selected = (page_target[None, :] == owners[:, None])[:, :, None, None, None]
    outgoing = jnp.where(selected, kv_pool[None], jnp.zeros((), kv_pool.dtype))
    incoming = lax.all_to_all(outgoing, "rep", split_axis=0, concat_axis=0, tiled=True)
    return jnp.sum(incoming, axis=0)


def on_device(
    residual,
    queries,
    kv_pool,
    prior_len,
    page_table,
    page_target,
    out_weight,
    moe_gain,
    expert_ids,
    expert_gates,
    w_gate,
    w_up,
    w_down,
):
    tp_size = lax.axis_size("z") * lax.axis_size("y")
    dec_size = lax.axis_size("dec")
    dec_index = lax.axis_index("dec")
    slots_dev, kv_heads, page_rows, both_dim = kv_pool.shape
    head_dim = both_dim // 2
    heads_dev = queries.shape[3] // head_dim
    group_size = QH // KVH
    kv_dev = max(1, heads_dev // group_size)
    copies = max(1, group_size // heads_dev)
    per_kv = heads_dev // kv_dev
    requests = prior_len.shape[0]
    tok_dev = queries.shape[2]
    half_rows = queries.shape[0] * tok_dev // requests
    pages_max = page_table.shape[1]
    team_size = tp_size * dec_size
    z_size = lax.axis_size("z")
    plane_size = team_size // z_size
    spread = kv_pool.reshape(slots_dev, z_size, kv_dev, page_rows, both_dim)
    spread = jnp.swapaxes(spread, 0, 1)
    by_plane = lax.all_to_all(spread, "z", split_axis=0, concat_axis=0, tiled=True)
    outgoing = jnp.broadcast_to(by_plane[None], (plane_size,) + by_plane.shape)
    received = lax.all_to_all(outgoing, ("y", "dec"), split_axis=0, concat_axis=0, tiled=True)
    received = jnp.swapaxes(received, 0, 1)
    received = received.reshape(team_size * slots_dev, kv_dev, page_rows, both_dim)
    gathered_pages = received[page_table % (team_size * slots_dev)]
    keys_part = gathered_pages[..., :head_dim]
    values_part = gathered_pages[..., head_dim:]
    query_rows = queries.reshape(requests, half_rows, kv_dev, per_kv, head_dim)
    key_count = pages_max * page_rows
    scores = jnp.einsum(
        "rukgd,rpkwd->rukgpw", query_rows, keys_part, preferred_element_type=jnp.float32
    )
    scores = scores.reshape(requests, half_rows, kv_dev, per_kv, key_count) * head_dim ** (-0.5)
    position = jnp.arange(key_count, dtype=jnp.int32)
    local_row = jnp.arange(half_rows, dtype=jnp.int32)
    offset = (local_row // tok_dev * dec_size + dec_index) * tok_dev + local_row % tok_dev
    last_seen = prior_len[:, None] + offset[None, :]
    visible = (position[None, None, :] <= last_seen[:, :, None])[:, :, None, None, :]
    scores = jnp.where(visible, scores, -1e30)
    row_top = jnp.max(scores, axis=-1, keepdims=True)
    raw_weights = jnp.where(visible, jnp.exp(scores - row_top), 0.0)
    totals = jnp.sum(raw_weights, axis=-1)
    weights_low = raw_weights.astype(jnp.bfloat16).reshape(
        requests, half_rows, kv_dev, per_kv, pages_max, page_rows
    )
    weighted = jnp.einsum(
        "rukgpw,rpkwd->rukgd", weights_low, values_part, preferred_element_type=jnp.float32
    )
    attended = (
        (weighted / totals[..., None])
        .astype(jnp.bfloat16)
        .reshape(requests * half_rows, heads_dev * head_dim)
    )
    y_size = lax.axis_size("y")
    width = out_weight.shape[1]
    plane_sum = ring_reduce_scatter(attended, out_weight, z_size, 0).reshape(y_size, tok_dev, width)
    pieces = lax.all_to_all(plane_sum.astype(jnp.bfloat16), "y", split_axis=0, concat_axis=0, tiled=True)
    projected = jnp.sum(pieces.astype(jnp.float32), axis=0)
    mid_state = residual.astype(jnp.float32) + projected
    routed_dev = tok_dev * TOPK // EXPERTS
    row_lists = []
    gate_lists = []
    for expert in range(EXP_WIN):
        names_it = expert_ids == expert
        chosen_rows = jnp.nonzero(jnp.any(names_it, axis=-1), size=routed_dev)[0].astype(jnp.int32)
        row_lists.append(chosen_rows)
        gate_lists.append(jnp.sum(jnp.where(names_it, expert_gates, 0.0), axis=-1)[chosen_rows])
    picked_rows = jnp.stack(row_lists, axis=0)
    picked_gates = jnp.stack(gate_lists, axis=0)
    inverse = lax.rsqrt(jnp.mean(mid_state * mid_state, axis=-1, keepdims=True) + 1e-05)
    normed_all = (mid_state * inverse * moe_gain).astype(jnp.bfloat16)
    width = normed_all.shape[1]
    by_expert = normed_all[picked_rows]
    outgoing = jnp.broadcast_to(by_expert[None], (tp_size, dec_size, routed_dev, width))
    outgoing = outgoing.reshape(team_size, routed_dev, width)
    row_piece = lax.all_to_all(outgoing, ("z", "y", "dec"), split_axis=0, concat_axis=0, tiled=True)
    row_piece = row_piece.reshape(team_size * routed_dev, width)
    gate_part = jnp.dot(row_piece, w_gate[0].T, preferred_element_type=jnp.float32)
    up_part = jnp.dot(row_piece, w_up[0].T, preferred_element_type=jnp.float32)
    hidden = (jax.nn.silu(gate_part) * up_part).astype(jnp.bfloat16)
    expert_part = ring_reduce_scatter(hidden, w_down[0], z_size, 1, whole=True)
    expert_part = expert_part.reshape(y_size * dec_size, routed_dev, width).astype(jnp.bfloat16)
    returned = lax.all_to_all(expert_part, ("y", "dec"), split_axis=0, concat_axis=0, tiled=True)
    returned = returned.reshape(y_size, dec_size, routed_dev, width).astype(jnp.float32)
    expert_out = jnp.sum(returned, axis=0)
    mixture = jnp.zeros_like(mid_state)
    for expert in range(EXP_WIN):
        mixture = mixture.at[picked_rows[expert]].add(
            expert_out[expert] * picked_gates[expert][:, None]
        )
    layer_out = (mid_state + mixture).astype(jnp.bfloat16)
    decode_pages = hand_over(kv_pool, page_target)
    return (layer_out, decode_pages)


def fine_mesh(mesh):
    tp_devices = mesh.devices[0, :, 0]
    y_size = len({device.coords[1] for device in tp_devices})
    shape = (mesh.shape["rep"], mesh.shape["tp"] // y_size, y_size, mesh.shape["dec"])
    return jax.sharding.Mesh(mesh.devices.reshape(shape), ("rep", "z", "y", "dec"))


def solution(mesh):
    team = ("rep", "z", "y", "dec")
    return jax.shard_map(
        on_device,
        mesh=fine_mesh(mesh),
        in_specs=(
            P(team, None),
            P("rep", "dec", None, ("z", "y")),
            P(team, None, None, None),
            P("rep"),
            P("rep", None),
            P(team),
            P(("z", "y"), None),
            P(),
            P(team, None),
            P(team, None),
            P("dec", ("z", "y"), None),
            P("dec", ("z", "y"), None),
            P("dec", ("z", "y"), None),
        ),
        out_specs=(P(team, None), P(team, None, None, None)),
        check_vma=False,
    )
```

```python
import functools

import jax
import jax.numpy as jnp
from jax import lax
from jax.sharding import PartitionSpec as P
from jax.experimental import pallas as pl
from jax.experimental.pallas import tpu as pltpu

QH = 32
KVH = 8
EXPERTS = 8
TOPK = 2
EXP_WIN = 2


MESH = pl.DeviceIdType.MESH

def _ring_kernel(whole, plane, rows_ref, weight_ref, out_ref, recv_buf, send_buf, send_sem, recv_sem,
                 ring_out, plane_send, plane_recv, plane_send_sem, plane_recv_sem, *product):
    n = recv_buf.shape[1] + 1
    half = recv_buf.shape[2]
    peers = plane_send.shape[0]
    groups = out_ref.shape[0]
    per_peer = plane_send.shape[1]
    me = lax.axis_index("z")
    rep = lax.axis_index("rep")
    yy = lax.axis_index("y")
    dd = lax.axis_index("dec")
    right = lax.rem(me + 1, n)
    left = lax.rem(me + n - 1, n)
    if len(plane) == 2:
        me_plane = yy * groups + dd

        def plane_device(index):
            return (rep, me, index // groups, lax.rem(index, groups))
    else:
        me_plane = yy

        def plane_device(index):
            return (rep, me, index, dd)

    if whole:
        product[0][...] = jnp.dot(rows_ref[...], weight_ref[...], preferred_element_type=jnp.float32)

    def block_part(block, way):
        start = pl.multiple_of(block * (2 * half) + way * half, half)
        if whole:
            return product[0][pl.ds(start, half), :]
        piece = rows_ref[pl.ds(start, half), :]
        return jnp.dot(piece, weight_ref[...], preferred_element_type=jnp.float32)

    barrier = pltpu.get_barrier_semaphore()
    for neighbour in (left, right):
        pl.semaphore_signal(barrier, inc=1, device_id=(rep, neighbour, yy, dd), device_id_type=MESH)
    for offset in range(1, peers):
        target = lax.rem(me_plane + offset, peers)
        pl.semaphore_signal(barrier, inc=1, device_id=plane_device(target), device_id_type=MESH)
    pl.semaphore_wait(barrier, 2 + peers - 1)
    for way in range(2):
        if way == 0:
            block = lax.rem(me + n - 1, n)
        else:
            block = lax.rem(me + 1, n)
        send_buf[way, 0] = block_part(block, way).astype(send_buf.dtype)
    for step in range(n - 1):
        copies = []
        for way in range(2):
            target = right if way == 0 else left
            copy = pltpu.make_async_remote_copy(
                src_ref=send_buf.at[way, step],
                dst_ref=recv_buf.at[way, step],
                send_sem=send_sem.at[way, step],
                recv_sem=recv_sem.at[way, step],
                device_id=(rep, target, yy, dd),
                device_id_type=MESH,
            )
            copy.start()
            copies.append(copy)
        for way in range(2):
            if way == 0:
                block = lax.rem(me + 2 * n - 2 - step, n)
            else:
                block = lax.rem(me + 2 + step, n)
            own = block_part(block, way)
            copies[way].wait()
            total = recv_buf[way, step].astype(jnp.float32) + own
            if step < n - 2:
                send_buf[way, step + 1] = total.astype(send_buf.dtype)
            else:
                ring_out[pl.ds(way * half, half), :] = total
    for index in range(peers):
        plane_send[index] = ring_out[pl.ds(index * per_peer, per_peer), :].astype(plane_send.dtype)
    sent = []
    for offset in range(1, peers):
        target = lax.rem(me_plane + offset, peers)
        copy = pltpu.make_async_remote_copy(
            src_ref=plane_send.at[target],
            dst_ref=plane_recv.at[me_plane],
            send_sem=plane_send_sem.at[offset],
            recv_sem=plane_recv_sem.at[me_plane],
            device_id=plane_device(target),
            device_id_type=MESH,
        )
        copy.start()
        sent.append(copy)
    plane_recv[me_plane] = plane_send[me_plane]
    for copy in sent:
        copy.wait_send()
    for offset in range(1, peers):
        source = lax.rem(me_plane + peers - offset, peers)
        arrival = pltpu.make_async_remote_copy(
            src_ref=plane_send.at[source],
            dst_ref=plane_recv.at[source],
            send_sem=plane_send_sem.at[offset],
            recv_sem=plane_recv_sem.at[source],
            device_id=plane_device(source),
            device_id_type=MESH,
        )
        arrival.wait_recv()
    for group in range(groups):
        total = plane_recv[group].astype(jnp.float32)
        for index in range(group + groups, peers, groups):
            total = total + plane_recv[index].astype(jnp.float32)
        out_ref[group] = total


def ring_reduce_scatter(rows, weight, n, peers, plane, call_id, whole=False):
    half = rows.shape[0] // (2 * n)
    width = weight.shape[1]
    groups = 2 if len(plane) == 2 else 1
    per_peer = 2 * half // peers
    return pl.pallas_call(
        functools.partial(_ring_kernel, whole, plane),
        out_shape=jax.ShapeDtypeStruct((groups, per_peer, width), jnp.float32),
        in_specs=[pl.BlockSpec(memory_space=pltpu.VMEM)] * 2,
        out_specs=pl.BlockSpec(memory_space=pltpu.VMEM),
        scratch_shapes=[
            pltpu.VMEM((2, n - 1, half, width), jnp.bfloat16),
            pltpu.VMEM((2, n - 1, half, width), jnp.bfloat16),
            pltpu.SemaphoreType.DMA((2, n - 1)),
            pltpu.SemaphoreType.DMA((2, n - 1)),
            pltpu.VMEM((2 * half, width), jnp.float32),
            pltpu.VMEM((peers, per_peer, width), jnp.bfloat16),
            pltpu.VMEM((peers, per_peer, width), jnp.bfloat16),
            pltpu.SemaphoreType.DMA((peers,)),
            pltpu.SemaphoreType.DMA((peers,)),
        ]
        + ([pltpu.VMEM((rows.shape[0], width), jnp.float32)] if whole else []),
        compiler_params=pltpu.CompilerParams(collective_id=call_id, has_side_effects=True),
    )(rows, weight)


def hand_over(kv_pool, page_target):
    rep_size = lax.axis_size("rep")
    owners = jnp.arange(rep_size, dtype=jnp.int32)
    selected = (page_target[None, :] == owners[:, None])[:, :, None, None, None]
    outgoing = jnp.where(selected, kv_pool[None], jnp.zeros((), kv_pool.dtype))
    incoming = lax.all_to_all(outgoing, "rep", split_axis=0, concat_axis=0, tiled=True)
    return jnp.sum(incoming, axis=0)


def on_device(
    residual,
    queries,
    kv_pool,
    prior_len,
    page_table,
    page_target,
    out_weight,
    moe_gain,
    expert_ids,
    expert_gates,
    w_gate,
    w_up,
    w_down,
):
    tp_size = lax.axis_size("z") * lax.axis_size("y")
    dec_size = lax.axis_size("dec")
    dec_index = lax.axis_index("dec")
    slots_dev, kv_heads, page_rows, both_dim = kv_pool.shape
    head_dim = both_dim // 2
    heads_dev = queries.shape[3] // head_dim
    group_size = QH // KVH
    kv_dev = max(1, heads_dev // group_size)
    copies = max(1, group_size // heads_dev)
    per_kv = heads_dev // kv_dev
    requests = prior_len.shape[0]
    tok_dev = queries.shape[2]
    half_rows = queries.shape[0] * tok_dev // requests
    pages_max = page_table.shape[1]
    team_size = tp_size * dec_size
    z_size = lax.axis_size("z")
    plane_size = team_size // z_size
    spread = kv_pool.reshape(slots_dev, z_size, kv_dev, page_rows, both_dim)
    spread = jnp.swapaxes(spread, 0, 1)
    by_plane = lax.all_to_all(spread, "z", split_axis=0, concat_axis=0, tiled=True)
    outgoing = jnp.broadcast_to(by_plane[None], (plane_size,) + by_plane.shape)
    received = lax.all_to_all(outgoing, ("y", "dec"), split_axis=0, concat_axis=0, tiled=True)
    received = jnp.swapaxes(received, 0, 1)
    received = received.reshape(team_size * slots_dev, kv_dev, page_rows, both_dim)
    gathered_pages = received[page_table % (team_size * slots_dev)]
    keys_part = gathered_pages[..., :head_dim]
    values_part = gathered_pages[..., head_dim:]
    query_rows = queries.reshape(requests, half_rows, kv_dev, per_kv, head_dim)
    key_count = pages_max * page_rows
    scores = jnp.einsum(
        "rukgd,rpkwd->rukgpw", query_rows, keys_part, preferred_element_type=jnp.float32
    )
    scores = scores.reshape(requests, half_rows, kv_dev, per_kv, key_count) * head_dim ** (-0.5)
    position = jnp.arange(key_count, dtype=jnp.int32)
    local_row = jnp.arange(half_rows, dtype=jnp.int32)
    offset = (local_row // tok_dev * dec_size + dec_index) * tok_dev + local_row % tok_dev
    last_seen = prior_len[:, None] + offset[None, :]
    visible = (position[None, None, :] <= last_seen[:, :, None])[:, :, None, None, :]
    scores = jnp.where(visible, scores, -1e30)
    row_top = jnp.max(scores, axis=-1, keepdims=True)
    raw_weights = jnp.where(visible, jnp.exp(scores - row_top), 0.0)
    totals = jnp.sum(raw_weights, axis=-1)
    weights_low = raw_weights.astype(jnp.bfloat16).reshape(
        requests, half_rows, kv_dev, per_kv, pages_max, page_rows
    )
    weighted = jnp.einsum(
        "rukgpw,rpkwd->rukgd", weights_low, values_part, preferred_element_type=jnp.float32
    )
    attended = (
        (weighted / totals[..., None])
        .astype(jnp.bfloat16)
        .reshape(requests * half_rows, heads_dev * head_dim)
    )
    y_size = lax.axis_size("y")
    width = out_weight.shape[1]
    projected = ring_reduce_scatter(attended, out_weight, z_size, y_size, ("y",), 0)[0]
    mid_state = residual.astype(jnp.float32) + projected
    routed_dev = tok_dev * TOPK // EXPERTS
    row_lists = []
    gate_lists = []
    for expert in range(EXP_WIN):
        names_it = expert_ids == expert
        chosen_rows = jnp.nonzero(jnp.any(names_it, axis=-1), size=routed_dev)[0].astype(jnp.int32)
        row_lists.append(chosen_rows)
        gate_lists.append(jnp.sum(jnp.where(names_it, expert_gates, 0.0), axis=-1)[chosen_rows])
    picked_rows = jnp.stack(row_lists, axis=0)
    picked_gates = jnp.stack(gate_lists, axis=0)
    inverse = lax.rsqrt(jnp.mean(mid_state * mid_state, axis=-1, keepdims=True) + 1e-05)
    normed_all = (mid_state * inverse * moe_gain).astype(jnp.bfloat16)
    width = normed_all.shape[1]
    by_expert = normed_all[picked_rows]
    outgoing = jnp.broadcast_to(by_expert[None], (tp_size, dec_size, routed_dev, width))
    outgoing = outgoing.reshape(team_size, routed_dev, width)
    row_piece = lax.all_to_all(outgoing, ("z", "y", "dec"), split_axis=0, concat_axis=0, tiled=True)
    row_piece = row_piece.reshape(team_size * routed_dev, width)
    gate_part = jnp.dot(row_piece, w_gate[0].T, preferred_element_type=jnp.float32)
    up_part = jnp.dot(row_piece, w_up[0].T, preferred_element_type=jnp.float32)
    hidden = (jax.nn.silu(gate_part) * up_part).astype(jnp.bfloat16)
    expert_out = ring_reduce_scatter(
        hidden, w_down[0], z_size, y_size * dec_size, ("y", "dec"), 1, whole=True
    )
    mixture = jnp.zeros_like(mid_state)
    for expert in range(EXP_WIN):
        mixture = mixture.at[picked_rows[expert]].add(
            expert_out[expert] * picked_gates[expert][:, None]
        )
    layer_out = (mid_state + mixture).astype(jnp.bfloat16)
    decode_pages = hand_over(kv_pool, page_target)
    return (layer_out, decode_pages)


def fine_mesh(mesh):
    tp_devices = mesh.devices[0, :, 0]
    y_size = len({device.coords[1] for device in tp_devices})
    shape = (mesh.shape["rep"], mesh.shape["tp"] // y_size, y_size, mesh.shape["dec"])
    return jax.sharding.Mesh(mesh.devices.reshape(shape), ("rep", "z", "y", "dec"))


def solution(mesh):
    team = ("rep", "z", "y", "dec")
    return jax.shard_map(
        on_device,
        mesh=fine_mesh(mesh),
        in_specs=(
            P(team, None),
            P("rep", "dec", None, ("z", "y")),
            P(team, None, None, None),
            P("rep"),
            P("rep", None),
            P(team),
            P(("z", "y"), None),
            P(),
            P(team, None),
            P(team, None),
            P("dec", ("z", "y"), None),
            P("dec", ("z", "y"), None),
            P("dec", ("z", "y"), None),
        ),
        out_specs=(P(team, None), P(team, None, None, None)),
        check_vma=False,
    )
```

```python
import functools

import jax
import jax.numpy as jnp
from jax import lax
from jax.sharding import PartitionSpec as P
from jax.experimental import pallas as pl
from jax.experimental.pallas import tpu as pltpu

QH = 32
KVH = 8
EXPERTS = 8
TOPK = 2
EXP_WIN = 2


MESH = pl.DeviceIdType.MESH

def _ring_kernel(whole, plane, rows_ref, weight_ref, out_ref, recv_buf, send_buf, send_sem, recv_sem,
                 ring_out, plane_send, plane_recv, plane_send_sem, plane_recv_sem, *product):
    n = recv_buf.shape[1] + 1
    half = recv_buf.shape[2]
    peers = plane_send.shape[0]
    groups = out_ref.shape[0]
    per_peer = plane_send.shape[1]
    me = lax.axis_index("z")
    rep = lax.axis_index("rep")
    yy = lax.axis_index("y")
    dd = lax.axis_index("dec")
    right = lax.rem(me + 1, n)
    left = lax.rem(me + n - 1, n)
    if len(plane) == 2:
        me_plane = yy * groups + dd

        def plane_device(index):
            return (rep, me, index // groups, lax.rem(index, groups))
    else:
        me_plane = yy

        def plane_device(index):
            return (rep, me, index, dd)

    if whole:
        product[0][...] = jnp.dot(rows_ref[...], weight_ref[...], preferred_element_type=jnp.float32)

    def block_part(block, way):
        start = pl.multiple_of(block * (2 * half) + way * half, half)
        if whole:
            return product[0][pl.ds(start, half), :]
        piece = rows_ref[pl.ds(start, half), :]
        return jnp.dot(piece, weight_ref[...], preferred_element_type=jnp.float32)

    barrier = pltpu.get_barrier_semaphore()
    for neighbour in (left, right):
        pl.semaphore_signal(barrier, inc=1, device_id=(rep, neighbour, yy, dd), device_id_type=MESH)
    for offset in range(1, peers):
        target = lax.rem(me_plane + offset, peers)
        pl.semaphore_signal(barrier, inc=1, device_id=plane_device(target), device_id_type=MESH)
    pl.semaphore_wait(barrier, 2 + peers - 1)
    for way in range(2):
        if way == 0:
            block = lax.rem(me + n - 1, n)
        else:
            block = lax.rem(me + 1, n)
        send_buf[way, 0] = block_part(block, way).astype(send_buf.dtype)
    for step in range(n - 1):
        copies = []
        for way in range(2):
            target = right if way == 0 else left
            copy = pltpu.make_async_remote_copy(
                src_ref=send_buf.at[way, step],
                dst_ref=recv_buf.at[way, step],
                send_sem=send_sem.at[way, step],
                recv_sem=recv_sem.at[way, step],
                device_id=(rep, target, yy, dd),
                device_id_type=MESH,
            )
            copy.start()
            copies.append(copy)
        for way in range(2):
            if way == 0:
                block = lax.rem(me + 2 * n - 2 - step, n)
            else:
                block = lax.rem(me + 2 + step, n)
            own = block_part(block, way)
            copies[way].wait()
            total = recv_buf[way, step].astype(jnp.float32) + own
            if step < n - 2:
                send_buf[way, step + 1] = total.astype(send_buf.dtype)
            else:
                ring_out[pl.ds(way * half, half), :] = total
    for index in range(peers):
        plane_send[index] = ring_out[pl.ds(index * per_peer, per_peer), :].astype(plane_send.dtype)
    sent = []
    for offset in range(1, peers):
        target = lax.rem(me_plane + offset, peers)
        copy = pltpu.make_async_remote_copy(
            src_ref=plane_send.at[target],
            dst_ref=plane_recv.at[me_plane],
            send_sem=plane_send_sem.at[offset],
            recv_sem=plane_recv_sem.at[me_plane],
            device_id=plane_device(target),
            device_id_type=MESH,
        )
        copy.start()
        sent.append(copy)
    plane_recv[me_plane] = plane_send[me_plane]
    for copy in sent:
        copy.wait_send()
    for offset in range(1, peers):
        source = lax.rem(me_plane + peers - offset, peers)
        arrival = pltpu.make_async_remote_copy(
            src_ref=plane_send.at[source],
            dst_ref=plane_recv.at[source],
            send_sem=plane_send_sem.at[offset],
            recv_sem=plane_recv_sem.at[source],
            device_id=plane_device(source),
            device_id_type=MESH,
        )
        arrival.wait_recv()
    for group in range(groups):
        total = plane_recv[group].astype(jnp.float32)
        for index in range(group + groups, peers, groups):
            total = total + plane_recv[index].astype(jnp.float32)
        out_ref[group] = total


def ring_reduce_scatter(rows, weight, n, peers, plane, call_id, whole=False):
    half = rows.shape[0] // (2 * n)
    width = weight.shape[1]
    groups = 2 if len(plane) == 2 else 1
    per_peer = 2 * half // peers
    return pl.pallas_call(
        functools.partial(_ring_kernel, whole, plane),
        out_shape=jax.ShapeDtypeStruct((groups, per_peer, width), jnp.float32),
        in_specs=[pl.BlockSpec(memory_space=pltpu.VMEM)] * 2,
        out_specs=pl.BlockSpec(memory_space=pltpu.VMEM),
        scratch_shapes=[
            pltpu.VMEM((2, n - 1, half, width), jnp.bfloat16),
            pltpu.VMEM((2, n - 1, half, width), jnp.bfloat16),
            pltpu.SemaphoreType.DMA((2, n - 1)),
            pltpu.SemaphoreType.DMA((2, n - 1)),
            pltpu.VMEM((2 * half, width), jnp.float32),
            pltpu.VMEM((peers, per_peer, width), jnp.bfloat16),
            pltpu.VMEM((peers, per_peer, width), jnp.bfloat16),
            pltpu.SemaphoreType.DMA((peers,)),
            pltpu.SemaphoreType.DMA((peers,)),
        ]
        + ([pltpu.VMEM((rows.shape[0], width), jnp.float32)] if whole else []),
        compiler_params=pltpu.CompilerParams(collective_id=call_id, has_side_effects=True),
    )(rows, weight)


def _pages_kernel(pages_ref, out_ref, arrived, z_send, z_recv, p_send, p_recv):
    nz = pages_ref.shape[0]
    peers = out_ref.shape[1]
    groups = lax.axis_size("dec")
    mz = lax.axis_index("z")
    rep = lax.axis_index("rep")
    yy = lax.axis_index("y")
    dd = lax.axis_index("dec")
    mp = yy * groups + dd

    def z_device(index):
        return (rep, index, yy, dd)

    def plane_device(index):
        return (rep, mz, index // groups, lax.rem(index, groups))

    barrier = pltpu.get_barrier_semaphore()
    for offset in range(1, nz):
        pl.semaphore_signal(barrier, inc=1, device_id=z_device(lax.rem(mz + offset, nz)),
                            device_id_type=MESH)
    for offset in range(1, peers):
        pl.semaphore_signal(barrier, inc=1, device_id=plane_device(lax.rem(mp + offset, peers)),
                            device_id_type=MESH)
    pl.semaphore_wait(barrier, nz - 1 + peers - 1)
    z_copies = []
    for offset in range(1, nz):
        target = lax.rem(mz + offset, nz)
        copy = pltpu.make_async_remote_copy(
            src_ref=pages_ref.at[target],
            dst_ref=arrived.at[mz],
            send_sem=z_send.at[offset],
            recv_sem=z_recv.at[mz],
            device_id=z_device(target),
            device_id_type=MESH,
        )
        copy.start()
        z_copies.append(copy)
    forwards = []

    def forward(source, page_ref):
        for offset in range(1, peers):
            target = lax.rem(mp + offset, peers)
            copy = pltpu.make_async_remote_copy(
                src_ref=page_ref,
                dst_ref=out_ref.at[source, mp],
                send_sem=p_send.at[source, offset],
                recv_sem=p_recv.at[source, mp],
                device_id=plane_device(target),
                device_id_type=MESH,
            )
            copy.start()
            forwards.append(copy)
        out_ref[source, mp] = page_ref[...]

    forward(mz, pages_ref.at[mz])
    order = []
    for distance in range(1, nz // 2 + 1):
        for offset in (nz - distance, distance):
            if offset not in order:
                order.append(offset)
    for offset in order:
        source = lax.rem(mz + offset, nz)
        arrival = pltpu.make_async_remote_copy(
            src_ref=pages_ref.at[source],
            dst_ref=arrived.at[source],
            send_sem=z_send.at[offset],
            recv_sem=z_recv.at[source],
            device_id=z_device(source),
            device_id_type=MESH,
        )
        arrival.wait_recv()
        forward(source, arrived.at[source])
    for copy in z_copies:
        copy.wait_send()
    for copy in forwards:
        copy.wait_send()
    for source in range(nz):
        for offset in range(1, peers):
            sender = lax.rem(mp + peers - offset, peers)
            arrival = pltpu.make_async_remote_copy(
                src_ref=pages_ref.at[source],
                dst_ref=out_ref.at[source, sender],
                send_sem=p_send.at[source, offset],
                recv_sem=p_recv.at[source, sender],
                device_id=plane_device(sender),
                device_id_type=MESH,
            )
            arrival.wait_recv()


def exchange_pages(pages, peers):
    nz = pages.shape[0]
    block = pages.shape[1:]
    return pl.pallas_call(
        _pages_kernel,
        out_shape=jax.ShapeDtypeStruct((nz, peers) + block, pages.dtype),
        in_specs=[pl.BlockSpec(memory_space=pltpu.VMEM)],
        out_specs=pl.BlockSpec(memory_space=pltpu.VMEM),
        scratch_shapes=[
            pltpu.VMEM((nz,) + block, pages.dtype),
            pltpu.SemaphoreType.DMA((nz,)),
            pltpu.SemaphoreType.DMA((nz,)),
            pltpu.SemaphoreType.DMA((nz, peers)),
            pltpu.SemaphoreType.DMA((nz, peers)),
        ],
        compiler_params=pltpu.CompilerParams(collective_id=2, has_side_effects=True),
    )(pages)


def hand_over(kv_pool, page_target):
    rep_size = lax.axis_size("rep")
    owners = jnp.arange(rep_size, dtype=jnp.int32)
    selected = (page_target[None, :] == owners[:, None])[:, :, None, None, None]
    outgoing = jnp.where(selected, kv_pool[None], jnp.zeros((), kv_pool.dtype))
    incoming = lax.all_to_all(outgoing, "rep", split_axis=0, concat_axis=0, tiled=True)
    return jnp.sum(incoming, axis=0)


def on_device(
    residual,
    queries,
    kv_pool,
    prior_len,
    page_table,
    page_target,
    out_weight,
    moe_gain,
    expert_ids,
    expert_gates,
    w_gate,
    w_up,
    w_down,
):
    tp_size = lax.axis_size("z") * lax.axis_size("y")
    dec_size = lax.axis_size("dec")
    dec_index = lax.axis_index("dec")
    slots_dev, kv_heads, page_rows, both_dim = kv_pool.shape
    head_dim = both_dim // 2
    heads_dev = queries.shape[3] // head_dim
    group_size = QH // KVH
    kv_dev = max(1, heads_dev // group_size)
    copies = max(1, group_size // heads_dev)
    per_kv = heads_dev // kv_dev
    requests = prior_len.shape[0]
    tok_dev = queries.shape[2]
    half_rows = queries.shape[0] * tok_dev // requests
    pages_max = page_table.shape[1]
    team_size = tp_size * dec_size
    z_size = lax.axis_size("z")
    plane_size = team_size // z_size
    received = exchange_pages(kv_pool.reshape(z_size * kv_dev, page_rows, both_dim), plane_size)
    received = received.reshape(team_size * slots_dev, kv_dev, page_rows, both_dim)
    gathered_pages = received[page_table % (team_size * slots_dev)]
    keys_part = gathered_pages[..., :head_dim]
    values_part = gathered_pages[..., head_dim:]
    query_rows = queries.reshape(requests, half_rows, kv_dev, per_kv, head_dim)
    key_count = pages_max * page_rows
    scores = jnp.einsum(
        "rukgd,rpkwd->rukgpw", query_rows, keys_part, preferred_element_type=jnp.float32
    )
    scores = scores.reshape(requests, half_rows, kv_dev, per_kv, key_count) * head_dim ** (-0.5)
    position = jnp.arange(key_count, dtype=jnp.int32)
    local_row = jnp.arange(half_rows, dtype=jnp.int32)
    offset = (local_row // tok_dev * dec_size + dec_index) * tok_dev + local_row % tok_dev
    last_seen = prior_len[:, None] + offset[None, :]
    visible = (position[None, None, :] <= last_seen[:, :, None])[:, :, None, None, :]
    scores = jnp.where(visible, scores, -1e30)
    row_top = jnp.max(scores, axis=-1, keepdims=True)
    raw_weights = jnp.where(visible, jnp.exp(scores - row_top), 0.0)
    totals = jnp.sum(raw_weights, axis=-1)
    weights_low = raw_weights.astype(jnp.bfloat16).reshape(
        requests, half_rows, kv_dev, per_kv, pages_max, page_rows
    )
    weighted = jnp.einsum(
        "rukgpw,rpkwd->rukgd", weights_low, values_part, preferred_element_type=jnp.float32
    )
    attended = (
        (weighted / totals[..., None])
        .astype(jnp.bfloat16)
        .reshape(requests * half_rows, heads_dev * head_dim)
    )
    y_size = lax.axis_size("y")
    width = out_weight.shape[1]
    projected = ring_reduce_scatter(attended, out_weight, z_size, y_size, ("y",), 0)[0]
    mid_state = residual.astype(jnp.float32) + projected
    routed_dev = tok_dev * TOPK // EXPERTS
    row_lists = []
    gate_lists = []
    for expert in range(EXP_WIN):
        names_it = expert_ids == expert
        chosen_rows = jnp.nonzero(jnp.any(names_it, axis=-1), size=routed_dev)[0].astype(jnp.int32)
        row_lists.append(chosen_rows)
        gate_lists.append(jnp.sum(jnp.where(names_it, expert_gates, 0.0), axis=-1)[chosen_rows])
    picked_rows = jnp.stack(row_lists, axis=0)
    picked_gates = jnp.stack(gate_lists, axis=0)
    inverse = lax.rsqrt(jnp.mean(mid_state * mid_state, axis=-1, keepdims=True) + 1e-05)
    normed_all = (mid_state * inverse * moe_gain).astype(jnp.bfloat16)
    width = normed_all.shape[1]
    by_expert = normed_all[picked_rows]
    outgoing = jnp.broadcast_to(by_expert[None], (tp_size, dec_size, routed_dev, width))
    outgoing = outgoing.reshape(team_size, routed_dev, width)
    row_piece = lax.all_to_all(outgoing, ("z", "y", "dec"), split_axis=0, concat_axis=0, tiled=True)
    row_piece = row_piece.reshape(team_size * routed_dev, width)
    gate_part = jnp.dot(row_piece, w_gate[0].T, preferred_element_type=jnp.float32)
    up_part = jnp.dot(row_piece, w_up[0].T, preferred_element_type=jnp.float32)
    hidden = (jax.nn.silu(gate_part) * up_part).astype(jnp.bfloat16)
    expert_out = ring_reduce_scatter(
        hidden, w_down[0], z_size, y_size * dec_size, ("y", "dec"), 1, whole=True
    )
    mixture = jnp.zeros_like(mid_state)
    for expert in range(EXP_WIN):
        mixture = mixture.at[picked_rows[expert]].add(
            expert_out[expert] * picked_gates[expert][:, None]
        )
    layer_out = (mid_state + mixture).astype(jnp.bfloat16)
    decode_pages = hand_over(kv_pool, page_target)
    return (layer_out, decode_pages)


def fine_mesh(mesh):
    tp_devices = mesh.devices[0, :, 0]
    y_size = len({device.coords[1] for device in tp_devices})
    shape = (mesh.shape["rep"], mesh.shape["tp"] // y_size, y_size, mesh.shape["dec"])
    return jax.sharding.Mesh(mesh.devices.reshape(shape), ("rep", "z", "y", "dec"))


def solution(mesh):
    team = ("rep", "z", "y", "dec")
    return jax.shard_map(
        on_device,
        mesh=fine_mesh(mesh),
        in_specs=(
            P(team, None),
            P("rep", "dec", None, ("z", "y")),
            P(team, None, None, None),
            P("rep"),
            P("rep", None),
            P(team),
            P(("z", "y"), None),
            P(),
            P(team, None),
            P(team, None),
            P("dec", ("z", "y"), None),
            P("dec", ("z", "y"), None),
            P("dec", ("z", "y"), None),
        ),
        out_specs=(P(team, None), P(team, None, None, None)),
        check_vma=False,
    )
```

```python
import functools

import jax
import jax.numpy as jnp
from jax import lax
from jax.sharding import PartitionSpec as P
from jax.experimental import pallas as pl
from jax.experimental.pallas import tpu as pltpu

QH = 32
KVH = 8
EXPERTS = 8
TOPK = 2
EXP_WIN = 2


MESH = pl.DeviceIdType.MESH

def _ring_kernel(whole, plane, rows_ref, weight_ref, out_ref, recv_buf, send_buf, send_sem, recv_sem,
                 ring_out, plane_send, plane_recv, plane_send_sem, plane_recv_sem, *product):
    n = recv_buf.shape[1] + 1
    half = recv_buf.shape[2]
    peers = plane_send.shape[0]
    groups = out_ref.shape[0]
    per_peer = plane_send.shape[1]
    me = lax.axis_index("z")
    rep = lax.axis_index("rep")
    yy = lax.axis_index("y")
    dd = lax.axis_index("dec")
    right = lax.rem(me + 1, n)
    left = lax.rem(me + n - 1, n)
    if len(plane) == 2:
        me_plane = yy * groups + dd

        def plane_device(index):
            return (rep, me, index // groups, lax.rem(index, groups))
    else:
        me_plane = yy

        def plane_device(index):
            return (rep, me, index, dd)

    if whole:
        product[0][...] = jnp.dot(rows_ref[...], weight_ref[...], preferred_element_type=jnp.float32)

    def block_part(block, way):
        start = pl.multiple_of(block * (2 * half) + way * half, half)
        if whole:
            return product[0][pl.ds(start, half), :]
        piece = rows_ref[pl.ds(start, half), :]
        return jnp.dot(piece, weight_ref[...], preferred_element_type=jnp.float32)

    barrier = pltpu.get_barrier_semaphore()
    for neighbour in (left, right):
        pl.semaphore_signal(barrier, inc=1, device_id=(rep, neighbour, yy, dd), device_id_type=MESH)
    for offset in range(1, peers):
        target = lax.rem(me_plane + offset, peers)
        pl.semaphore_signal(barrier, inc=1, device_id=plane_device(target), device_id_type=MESH)
    pl.semaphore_wait(barrier, 2 + peers - 1)
    for way in range(2):
        if way == 0:
            block = lax.rem(me + n - 1, n)
        else:
            block = lax.rem(me + 1, n)
        send_buf[way, 0] = block_part(block, way).astype(send_buf.dtype)
    for step in range(n - 1):
        copies = []
        for way in range(2):
            target = right if way == 0 else left
            copy = pltpu.make_async_remote_copy(
                src_ref=send_buf.at[way, step],
                dst_ref=recv_buf.at[way, step],
                send_sem=send_sem.at[way, step],
                recv_sem=recv_sem.at[way, step],
                device_id=(rep, target, yy, dd),
                device_id_type=MESH,
            )
            copy.start()
            copies.append(copy)
        for way in range(2):
            if way == 0:
                block = lax.rem(me + 2 * n - 2 - step, n)
            else:
                block = lax.rem(me + 2 + step, n)
            own = block_part(block, way)
            copies[way].wait()
            total = recv_buf[way, step].astype(jnp.float32) + own
            if step < n - 2:
                send_buf[way, step + 1] = total.astype(send_buf.dtype)
            else:
                ring_out[pl.ds(way * half, half), :] = total
    for index in range(peers):
        plane_send[index] = ring_out[pl.ds(index * per_peer, per_peer), :].astype(plane_send.dtype)
    sent = []
    for offset in range(1, peers):
        target = lax.rem(me_plane + offset, peers)
        copy = pltpu.make_async_remote_copy(
            src_ref=plane_send.at[target],
            dst_ref=plane_recv.at[me_plane],
            send_sem=plane_send_sem.at[offset],
            recv_sem=plane_recv_sem.at[me_plane],
            device_id=plane_device(target),
            device_id_type=MESH,
        )
        copy.start()
        sent.append(copy)
    plane_recv[me_plane] = plane_send[me_plane]
    for copy in sent:
        copy.wait_send()
    for offset in range(1, peers):
        source = lax.rem(me_plane + peers - offset, peers)
        arrival = pltpu.make_async_remote_copy(
            src_ref=plane_send.at[source],
            dst_ref=plane_recv.at[source],
            send_sem=plane_send_sem.at[offset],
            recv_sem=plane_recv_sem.at[source],
            device_id=plane_device(source),
            device_id_type=MESH,
        )
        arrival.wait_recv()
    for group in range(groups):
        total = plane_recv[group].astype(jnp.float32)
        for index in range(group + groups, peers, groups):
            total = total + plane_recv[index].astype(jnp.float32)
        out_ref[group] = total


def ring_reduce_scatter(rows, weight, n, peers, plane, call_id, whole=False):
    half = rows.shape[0] // (2 * n)
    width = weight.shape[1]
    groups = 2 if len(plane) == 2 else 1
    per_peer = 2 * half // peers
    return pl.pallas_call(
        functools.partial(_ring_kernel, whole, plane),
        out_shape=jax.ShapeDtypeStruct((groups, per_peer, width), jnp.float32),
        in_specs=[pl.BlockSpec(memory_space=pltpu.VMEM)] * 2,
        out_specs=pl.BlockSpec(memory_space=pltpu.VMEM),
        scratch_shapes=[
            pltpu.VMEM((2, n - 1, half, width), jnp.bfloat16),
            pltpu.VMEM((2, n - 1, half, width), jnp.bfloat16),
            pltpu.SemaphoreType.DMA((2, n - 1)),
            pltpu.SemaphoreType.DMA((2, n - 1)),
            pltpu.VMEM((2 * half, width), jnp.float32),
            pltpu.VMEM((peers, per_peer, width), jnp.bfloat16),
            pltpu.VMEM((peers, per_peer, width), jnp.bfloat16),
            pltpu.SemaphoreType.DMA((peers,)),
            pltpu.SemaphoreType.DMA((peers,)),
        ]
        + ([pltpu.VMEM((rows.shape[0], width), jnp.float32)] if whole else []),
        compiler_params=pltpu.CompilerParams(collective_id=call_id, has_side_effects=True),
    )(rows, weight)


def _pages_kernel(pages_ref, out_ref, arrived, z_send, z_recv, p_send, p_recv):
    nz = pages_ref.shape[0]
    peers = out_ref.shape[1]
    groups = lax.axis_size("dec")
    mz = lax.axis_index("z")
    rep = lax.axis_index("rep")
    yy = lax.axis_index("y")
    dd = lax.axis_index("dec")
    mp = yy * groups + dd

    def z_device(index):
        return (rep, index, yy, dd)

    def plane_device(index):
        return (rep, mz, index // groups, lax.rem(index, groups))

    barrier = pltpu.get_barrier_semaphore()
    for offset in range(1, nz):
        pl.semaphore_signal(barrier, inc=1, device_id=z_device(lax.rem(mz + offset, nz)),
                            device_id_type=MESH)
    for offset in range(1, peers):
        pl.semaphore_signal(barrier, inc=1, device_id=plane_device(lax.rem(mp + offset, peers)),
                            device_id_type=MESH)
    pl.semaphore_wait(barrier, nz - 1 + peers - 1)
    z_copies = []
    for offset in range(1, nz):
        target = lax.rem(mz + offset, nz)
        copy = pltpu.make_async_remote_copy(
            src_ref=pages_ref.at[target],
            dst_ref=arrived.at[mz],
            send_sem=z_send.at[offset],
            recv_sem=z_recv.at[mz],
            device_id=z_device(target),
            device_id_type=MESH,
        )
        copy.start()
        z_copies.append(copy)
    forwards = []

    def forward(source, page_ref):
        for offset in range(1, peers):
            target = lax.rem(mp + offset, peers)
            copy = pltpu.make_async_remote_copy(
                src_ref=page_ref,
                dst_ref=out_ref.at[source, mp],
                send_sem=p_send.at[source, offset],
                recv_sem=p_recv.at[source, mp],
                device_id=plane_device(target),
                device_id_type=MESH,
            )
            copy.start()
            forwards.append(copy)
        out_ref[source, mp] = page_ref[...]

    forward(mz, pages_ref.at[mz])
    order = []
    for distance in range(1, nz // 2 + 1):
        for offset in (nz - distance, distance):
            if offset not in order:
                order.append(offset)
    for offset in order:
        source = lax.rem(mz + offset, nz)
        arrival = pltpu.make_async_remote_copy(
            src_ref=pages_ref.at[source],
            dst_ref=arrived.at[source],
            send_sem=z_send.at[offset],
            recv_sem=z_recv.at[source],
            device_id=z_device(source),
            device_id_type=MESH,
        )
        arrival.wait_recv()
        forward(source, arrived.at[source])
    for copy in z_copies:
        copy.wait_send()
    for copy in forwards:
        copy.wait_send()
    for source in range(nz):
        for offset in range(1, peers):
            sender = lax.rem(mp + peers - offset, peers)
            arrival = pltpu.make_async_remote_copy(
                src_ref=pages_ref.at[source],
                dst_ref=out_ref.at[source, sender],
                send_sem=p_send.at[source, offset],
                recv_sem=p_recv.at[source, sender],
                device_id=plane_device(sender),
                device_id_type=MESH,
            )
            arrival.wait_recv()


def exchange_pages(pages, peers):
    nz = pages.shape[0]
    block = pages.shape[1:]
    return pl.pallas_call(
        _pages_kernel,
        out_shape=jax.ShapeDtypeStruct((nz, peers) + block, pages.dtype),
        in_specs=[pl.BlockSpec(memory_space=pltpu.VMEM)],
        out_specs=pl.BlockSpec(memory_space=pltpu.VMEM),
        scratch_shapes=[
            pltpu.VMEM((nz,) + block, pages.dtype),
            pltpu.SemaphoreType.DMA((nz,)),
            pltpu.SemaphoreType.DMA((nz,)),
            pltpu.SemaphoreType.DMA((nz, peers)),
            pltpu.SemaphoreType.DMA((nz, peers)),
        ],
        compiler_params=pltpu.CompilerParams(collective_id=2, has_side_effects=True),
    )(pages)


def hand_over(kv_pool, page_target):
    rep_size = lax.axis_size("rep")
    owners = jnp.arange(rep_size, dtype=jnp.int32)
    selected = (page_target[None, :] == owners[:, None])[:, :, None, None, None]
    outgoing = jnp.where(selected, kv_pool[None], jnp.zeros((), kv_pool.dtype))
    incoming = lax.all_to_all(outgoing, "rep", split_axis=0, concat_axis=0, tiled=True)
    return jnp.sum(incoming, axis=0)


def on_device(
    residual,
    queries,
    kv_pool,
    prior_len,
    page_table,
    page_target,
    out_weight,
    moe_gain,
    expert_ids,
    expert_gates,
    w_gate,
    w_up,
    w_down,
):
    tp_size = lax.axis_size("z") * lax.axis_size("y")
    dec_size = lax.axis_size("dec")
    dec_index = lax.axis_index("dec")
    slots_dev, kv_heads, page_rows, both_dim = kv_pool.shape
    head_dim = both_dim // 2
    heads_dev = queries.shape[3] // head_dim
    group_size = QH // KVH
    kv_dev = max(1, heads_dev // group_size)
    copies = max(1, group_size // heads_dev)
    per_kv = heads_dev // kv_dev
    requests = prior_len.shape[0]
    tok_dev = queries.shape[2]
    half_rows = queries.shape[0] * tok_dev // requests
    pages_max = page_table.shape[1]
    team_size = tp_size * dec_size
    z_size = lax.axis_size("z")
    plane_size = team_size // z_size
    received = exchange_pages(kv_pool.reshape(z_size * kv_dev, page_rows, both_dim), plane_size)
    received = received.reshape(team_size * slots_dev, kv_dev, page_rows, both_dim)
    gathered_pages = received[page_table % (team_size * slots_dev)]
    keys_part = gathered_pages[..., :head_dim]
    values_part = gathered_pages[..., head_dim:]
    query_rows = queries.reshape(requests, half_rows, kv_dev, per_kv, head_dim)
    key_count = pages_max * page_rows
    scores = jnp.einsum(
        "rukgd,rpkwd->rukgpw", query_rows, keys_part, preferred_element_type=jnp.float32
    )
    scores = scores.reshape(requests, half_rows, kv_dev, per_kv, key_count) * head_dim ** (-0.5)
    position = jnp.arange(key_count, dtype=jnp.int32)
    local_row = jnp.arange(half_rows, dtype=jnp.int32)
    offset = (local_row // tok_dev * dec_size + dec_index) * tok_dev + local_row % tok_dev
    last_seen = prior_len[:, None] + offset[None, :]
    visible = (position[None, None, :] <= last_seen[:, :, None])[:, :, None, None, :]
    scores = jnp.where(visible, scores, -1e30)
    row_top = jnp.max(scores, axis=-1, keepdims=True)
    raw_weights = jnp.where(visible, jnp.exp(scores - row_top), 0.0)
    totals = jnp.sum(raw_weights, axis=-1)
    weights_low = raw_weights.astype(jnp.bfloat16).reshape(
        requests, half_rows, kv_dev, per_kv, pages_max, page_rows
    )
    weighted = jnp.einsum(
        "rukgpw,rpkwd->rukgd", weights_low, values_part, preferred_element_type=jnp.float32
    )
    attended = (
        (weighted / totals[..., None])
        .astype(jnp.bfloat16)
        .reshape(requests * half_rows, heads_dev * head_dim)
    )
    y_size = lax.axis_size("y")
    width = out_weight.shape[1]
    projected = ring_reduce_scatter(attended, out_weight, z_size, y_size, ("y",), 0)[0]
    mid_state = residual.astype(jnp.float32) + projected
    routed_dev = tok_dev * TOPK // EXPERTS
    row_lists = []
    gate_lists = []
    for expert in range(EXP_WIN):
        names_it = expert_ids == expert
        chosen_rows = jnp.nonzero(jnp.any(names_it, axis=-1), size=routed_dev)[0].astype(jnp.int32)
        row_lists.append(chosen_rows)
        gate_lists.append(jnp.sum(jnp.where(names_it, expert_gates, 0.0), axis=-1)[chosen_rows])
    picked_rows = jnp.stack(row_lists, axis=0)
    picked_gates = jnp.stack(gate_lists, axis=0)
    inverse = lax.rsqrt(jnp.mean(mid_state * mid_state, axis=-1, keepdims=True) + 1e-05)
    normed_all = (mid_state * inverse * moe_gain).astype(jnp.bfloat16)
    width = normed_all.shape[1]
    by_expert = normed_all[picked_rows]
    outgoing = jnp.broadcast_to(by_expert[None], (tp_size, dec_size, routed_dev, width))
    outgoing = outgoing.reshape(team_size, routed_dev, width)
    row_piece = lax.all_to_all(outgoing, ("z", "y", "dec"), split_axis=0, concat_axis=0, tiled=True)
    row_piece = row_piece.reshape(team_size * routed_dev, width)
    gate_part = jnp.dot(row_piece, w_gate[0].T, preferred_element_type=jnp.float32)
    up_part = jnp.dot(row_piece, w_up[0].T, preferred_element_type=jnp.float32)
    hidden = (jax.nn.silu(gate_part) * up_part).astype(jnp.bfloat16)
    expert_out = ring_reduce_scatter(
        hidden, w_down[0], z_size, y_size * dec_size, ("y", "dec"), 1, whole=True
    )
    mixture = jnp.zeros_like(mid_state)
    for expert in range(EXP_WIN):
        mixture = mixture.at[picked_rows[expert]].add(
            expert_out[expert] * picked_gates[expert][:, None]
        )
    layer_out = (mid_state + mixture).astype(jnp.bfloat16)
    pool_later, _ = lax.optimization_barrier((kv_pool, attended))
    decode_pages = hand_over(pool_later, page_target)
    return (layer_out, decode_pages)


def fine_mesh(mesh):
    tp_devices = mesh.devices[0, :, 0]
    y_size = len({device.coords[1] for device in tp_devices})
    shape = (mesh.shape["rep"], mesh.shape["tp"] // y_size, y_size, mesh.shape["dec"])
    return jax.sharding.Mesh(mesh.devices.reshape(shape), ("rep", "z", "y", "dec"))


def solution(mesh):
    team = ("rep", "z", "y", "dec")
    return jax.shard_map(
        on_device,
        mesh=fine_mesh(mesh),
        in_specs=(
            P(team, None),
            P("rep", "dec", None, ("z", "y")),
            P(team, None, None, None),
            P("rep"),
            P("rep", None),
            P(team),
            P(("z", "y"), None),
            P(),
            P(team, None),
            P(team, None),
            P("dec", ("z", "y"), None),
            P("dec", ("z", "y"), None),
            P("dec", ("z", "y"), None),
        ),
        out_specs=(P(team, None), P(team, None, None, None)),
        check_vma=False,
    )
```

```python
import functools

import jax
import jax.numpy as jnp
from jax import lax
from jax.sharding import PartitionSpec as P
from jax.experimental import pallas as pl
from jax.experimental.pallas import tpu as pltpu

QH = 32
KVH = 8
EXPERTS = 8
TOPK = 2
EXP_WIN = 2


MESH = pl.DeviceIdType.MESH

def _ring_kernel(whole, plane, rows_ref, weight_ref, out_ref, recv_buf, send_buf, send_sem, recv_sem,
                 ring_out, plane_send, plane_recv, plane_send_sem, plane_recv_sem, *product):
    n = recv_buf.shape[1] + 1
    half = recv_buf.shape[2]
    peers = plane_send.shape[0]
    groups = out_ref.shape[0]
    per_peer = plane_send.shape[1]
    me = lax.axis_index("z")
    rep = lax.axis_index("rep")
    yy = lax.axis_index("y")
    dd = lax.axis_index("dec")
    right = lax.rem(me + 1, n)
    left = lax.rem(me + n - 1, n)
    if len(plane) == 2:
        me_plane = yy * groups + dd

        def plane_device(index):
            return (rep, me, index // groups, lax.rem(index, groups))
    else:
        me_plane = yy

        def plane_device(index):
            return (rep, me, index, dd)

    if whole:
        product[0][...] = jnp.dot(rows_ref[...], weight_ref[...], preferred_element_type=jnp.float32)

    def block_part(block, way):
        start = pl.multiple_of(block * (2 * half) + way * half, half)
        if whole:
            return product[0][pl.ds(start, half), :]
        piece = rows_ref[pl.ds(start, half), :]
        return jnp.dot(piece, weight_ref[...], preferred_element_type=jnp.float32)

    barrier = pltpu.get_barrier_semaphore()
    for neighbour in (left, right):
        pl.semaphore_signal(barrier, inc=1, device_id=(rep, neighbour, yy, dd), device_id_type=MESH)
    for offset in range(1, peers):
        target = lax.rem(me_plane + offset, peers)
        pl.semaphore_signal(barrier, inc=1, device_id=plane_device(target), device_id_type=MESH)
    pl.semaphore_wait(barrier, 2 + peers - 1)
    for way in range(2):
        if way == 0:
            block = lax.rem(me + n - 1, n)
        else:
            block = lax.rem(me + 1, n)
        send_buf[way, 0] = block_part(block, way).astype(send_buf.dtype)
    for step in range(n - 1):
        copies = []
        for way in range(2):
            target = right if way == 0 else left
            copy = pltpu.make_async_remote_copy(
                src_ref=send_buf.at[way, step],
                dst_ref=recv_buf.at[way, step],
                send_sem=send_sem.at[way, step],
                recv_sem=recv_sem.at[way, step],
                device_id=(rep, target, yy, dd),
                device_id_type=MESH,
            )
            copy.start()
            copies.append(copy)
        for way in range(2):
            if way == 0:
                block = lax.rem(me + 2 * n - 2 - step, n)
            else:
                block = lax.rem(me + 2 + step, n)
            own = block_part(block, way)
            copies[way].wait()
            total = recv_buf[way, step].astype(jnp.float32) + own
            if step < n - 2:
                send_buf[way, step + 1] = total.astype(send_buf.dtype)
            else:
                ring_out[pl.ds(way * half, half), :] = total
    for index in range(peers):
        plane_send[index] = ring_out[pl.ds(index * per_peer, per_peer), :].astype(plane_send.dtype)
    sent = []
    for offset in range(1, peers):
        target = lax.rem(me_plane + offset, peers)
        copy = pltpu.make_async_remote_copy(
            src_ref=plane_send.at[target],
            dst_ref=plane_recv.at[me_plane],
            send_sem=plane_send_sem.at[offset],
            recv_sem=plane_recv_sem.at[me_plane],
            device_id=plane_device(target),
            device_id_type=MESH,
        )
        copy.start()
        sent.append(copy)
    plane_recv[me_plane] = plane_send[me_plane]
    for copy in sent:
        copy.wait_send()
    for offset in range(1, peers):
        source = lax.rem(me_plane + peers - offset, peers)
        arrival = pltpu.make_async_remote_copy(
            src_ref=plane_send.at[source],
            dst_ref=plane_recv.at[source],
            send_sem=plane_send_sem.at[offset],
            recv_sem=plane_recv_sem.at[source],
            device_id=plane_device(source),
            device_id_type=MESH,
        )
        arrival.wait_recv()
    for group in range(groups):
        total = plane_recv[group].astype(jnp.float32)
        for index in range(group + groups, peers, groups):
            total = total + plane_recv[index].astype(jnp.float32)
        out_ref[group] = total


def ring_reduce_scatter(rows, weight, n, peers, plane, call_id, whole=False):
    half = rows.shape[0] // (2 * n)
    width = weight.shape[1]
    groups = 2 if len(plane) == 2 else 1
    per_peer = 2 * half // peers
    return pl.pallas_call(
        functools.partial(_ring_kernel, whole, plane),
        out_shape=jax.ShapeDtypeStruct((groups, per_peer, width), jnp.float32),
        in_specs=[pl.BlockSpec(memory_space=pltpu.VMEM)] * 2,
        out_specs=pl.BlockSpec(memory_space=pltpu.VMEM),
        scratch_shapes=[
            pltpu.VMEM((2, n - 1, half, width), jnp.bfloat16),
            pltpu.VMEM((2, n - 1, half, width), jnp.bfloat16),
            pltpu.SemaphoreType.DMA((2, n - 1)),
            pltpu.SemaphoreType.DMA((2, n - 1)),
            pltpu.VMEM((2 * half, width), jnp.float32),
            pltpu.VMEM((peers, per_peer, width), jnp.bfloat16),
            pltpu.VMEM((peers, per_peer, width), jnp.bfloat16),
            pltpu.SemaphoreType.DMA((peers,)),
            pltpu.SemaphoreType.DMA((peers,)),
        ]
        + ([pltpu.VMEM((rows.shape[0], width), jnp.float32)] if whole else []),
        compiler_params=pltpu.CompilerParams(collective_id=call_id, has_side_effects=True),
    )(rows, weight)


def _pages_kernel(pages_ref, out_ref, arrived, z_send, z_recv, p_send, p_recv):
    nz = pages_ref.shape[0]
    peers = out_ref.shape[1]
    groups = lax.axis_size("dec")
    mz = lax.axis_index("z")
    rep = lax.axis_index("rep")
    yy = lax.axis_index("y")
    dd = lax.axis_index("dec")
    mp = yy * groups + dd

    def z_device(index):
        return (rep, index, yy, dd)

    def plane_device(index):
        return (rep, mz, index // groups, lax.rem(index, groups))

    barrier = pltpu.get_barrier_semaphore()
    for offset in range(1, nz):
        pl.semaphore_signal(barrier, inc=1, device_id=z_device(lax.rem(mz + offset, nz)),
                            device_id_type=MESH)
    for offset in range(1, peers):
        pl.semaphore_signal(barrier, inc=1, device_id=plane_device(lax.rem(mp + offset, peers)),
                            device_id_type=MESH)
    pl.semaphore_wait(barrier, nz - 1 + peers - 1)
    z_copies = []
    for offset in range(1, nz):
        target = lax.rem(mz + offset, nz)
        copy = pltpu.make_async_remote_copy(
            src_ref=pages_ref.at[target],
            dst_ref=arrived.at[mz],
            send_sem=z_send.at[offset],
            recv_sem=z_recv.at[mz],
            device_id=z_device(target),
            device_id_type=MESH,
        )
        copy.start()
        z_copies.append(copy)
    forwards = []

    def forward(source, page_ref):
        for offset in range(1, peers):
            target = lax.rem(mp + offset, peers)
            copy = pltpu.make_async_remote_copy(
                src_ref=page_ref,
                dst_ref=out_ref.at[source, mp],
                send_sem=p_send.at[source, offset],
                recv_sem=p_recv.at[source, mp],
                device_id=plane_device(target),
                device_id_type=MESH,
            )
            copy.start()
            forwards.append(copy)
        out_ref[source, mp] = page_ref[...]

    forward(mz, pages_ref.at[mz])
    order = []
    for distance in range(1, nz // 2 + 1):
        for offset in (nz - distance, distance):
            if offset not in order:
                order.append(offset)
    for offset in order:
        source = lax.rem(mz + offset, nz)
        arrival = pltpu.make_async_remote_copy(
            src_ref=pages_ref.at[source],
            dst_ref=arrived.at[source],
            send_sem=z_send.at[offset],
            recv_sem=z_recv.at[source],
            device_id=z_device(source),
            device_id_type=MESH,
        )
        arrival.wait_recv()
        forward(source, arrived.at[source])
    for copy in z_copies:
        copy.wait_send()
    for copy in forwards:
        copy.wait_send()
    for source in range(nz):
        for offset in range(1, peers):
            sender = lax.rem(mp + peers - offset, peers)
            arrival = pltpu.make_async_remote_copy(
                src_ref=pages_ref.at[source],
                dst_ref=out_ref.at[source, sender],
                send_sem=p_send.at[source, offset],
                recv_sem=p_recv.at[source, sender],
                device_id=plane_device(sender),
                device_id_type=MESH,
            )
            arrival.wait_recv()


def exchange_pages(pages, peers):
    nz = pages.shape[0]
    block = pages.shape[1:]
    return pl.pallas_call(
        _pages_kernel,
        out_shape=jax.ShapeDtypeStruct((nz, peers) + block, pages.dtype),
        in_specs=[pl.BlockSpec(memory_space=pltpu.VMEM)],
        out_specs=pl.BlockSpec(memory_space=pltpu.VMEM),
        scratch_shapes=[
            pltpu.VMEM((nz,) + block, pages.dtype),
            pltpu.SemaphoreType.DMA((nz,)),
            pltpu.SemaphoreType.DMA((nz,)),
            pltpu.SemaphoreType.DMA((nz, peers)),
            pltpu.SemaphoreType.DMA((nz, peers)),
        ],
        compiler_params=pltpu.CompilerParams(collective_id=2, has_side_effects=True),
    )(pages)


def _rows_kernel(rows_ref, out_ref, plane_rows, p_send, p_recv, send_sem, recv_sem):
    nz = out_ref.shape[0]
    peers = out_ref.shape[1]
    part = peers // 2
    groups = lax.axis_size("dec")
    mz = lax.axis_index("z")
    rep = lax.axis_index("rep")
    yy = lax.axis_index("y")
    dd = lax.axis_index("dec")
    mp = yy * groups + dd
    right = lax.rem(mz + 1, nz)
    left = lax.rem(mz + nz - 1, nz)

    def plane_device(index):
        return (rep, mz, index // groups, lax.rem(index, groups))

    barrier = pltpu.get_barrier_semaphore()
    for neighbour in (left, right):
        pl.semaphore_signal(barrier, inc=1, device_id=(rep, neighbour, yy, dd), device_id_type=MESH)
    for offset in range(1, peers):
        pl.semaphore_signal(barrier, inc=1, device_id=plane_device(lax.rem(mp + offset, peers)),
                            device_id_type=MESH)
    pl.semaphore_wait(barrier, 2 + peers - 1)
    sent = []
    for offset in range(1, peers):
        target = lax.rem(mp + offset, peers)
        copy = pltpu.make_async_remote_copy(
            src_ref=rows_ref.at[lax.rem(target, groups)],
            dst_ref=plane_rows.at[mp],
            send_sem=p_send.at[offset],
            recv_sem=p_recv.at[mp],
            device_id=plane_device(target),
            device_id_type=MESH,
        )
        copy.start()
        sent.append(copy)
    plane_rows[mp] = rows_ref[dd]
    for copy in sent:
        copy.wait_send()
    for offset in range(1, peers):
        sender = lax.rem(mp + peers - offset, peers)
        arrival = pltpu.make_async_remote_copy(
            src_ref=rows_ref.at[0],
            dst_ref=plane_rows.at[sender],
            send_sem=p_send.at[offset],
            recv_sem=p_recv.at[sender],
            device_id=plane_device(sender),
            device_id_type=MESH,
        )
        arrival.wait_recv()
    out_ref[mz] = plane_rows[...]
    for step in range(nz - 1):
        copies = []
        for way in range(2):
            if way == 0:
                target, source = right, lax.rem(mz + nz - step, nz)
            else:
                target, source = left, lax.rem(mz + step, nz)
            if step == 0:
                src = plane_rows.at[pl.ds(way * part, part)]
            else:
                src = out_ref.at[source, pl.ds(way * part, part)]
            copy = pltpu.make_async_remote_copy(
                src_ref=src,
                dst_ref=out_ref.at[source, pl.ds(way * part, part)],
                send_sem=send_sem.at[way, step],
                recv_sem=recv_sem.at[way, step],
                device_id=(rep, target, yy, dd),
                device_id_type=MESH,
            )
            copy.start()
            copies.append(copy)
        for copy in copies:
            copy.wait()


def gather_rows(rows, nz, peers):
    block = rows.shape[1:]
    return pl.pallas_call(
        _rows_kernel,
        out_shape=jax.ShapeDtypeStruct((nz, peers) + block, rows.dtype),
        in_specs=[pl.BlockSpec(memory_space=pltpu.VMEM)],
        out_specs=pl.BlockSpec(memory_space=pltpu.VMEM),
        scratch_shapes=[
            pltpu.VMEM((peers,) + block, rows.dtype),
            pltpu.SemaphoreType.DMA((peers,)),
            pltpu.SemaphoreType.DMA((peers,)),
            pltpu.SemaphoreType.DMA((2, nz - 1)),
            pltpu.SemaphoreType.DMA((2, nz - 1)),
        ],
        compiler_params=pltpu.CompilerParams(collective_id=3, has_side_effects=True),
    )(rows)


def hand_over(kv_pool, page_target):
    rep_size = lax.axis_size("rep")
    owners = jnp.arange(rep_size, dtype=jnp.int32)
    selected = (page_target[None, :] == owners[:, None])[:, :, None, None, None]
    outgoing = jnp.where(selected, kv_pool[None], jnp.zeros((), kv_pool.dtype))
    incoming = lax.all_to_all(outgoing, "rep", split_axis=0, concat_axis=0, tiled=True)
    return jnp.sum(incoming, axis=0)


def on_device(
    residual,
    queries,
    kv_pool,
    prior_len,
    page_table,
    page_target,
    out_weight,
    moe_gain,
    expert_ids,
    expert_gates,
    w_gate,
    w_up,
    w_down,
):
    tp_size = lax.axis_size("z") * lax.axis_size("y")
    dec_size = lax.axis_size("dec")
    dec_index = lax.axis_index("dec")
    slots_dev, kv_heads, page_rows, both_dim = kv_pool.shape
    head_dim = both_dim // 2
    heads_dev = queries.shape[3] // head_dim
    group_size = QH // KVH
    kv_dev = max(1, heads_dev // group_size)
    copies = max(1, group_size // heads_dev)
    per_kv = heads_dev // kv_dev
    requests = prior_len.shape[0]
    tok_dev = queries.shape[2]
    half_rows = queries.shape[0] * tok_dev // requests
    pages_max = page_table.shape[1]
    team_size = tp_size * dec_size
    z_size = lax.axis_size("z")
    plane_size = team_size // z_size
    received = exchange_pages(kv_pool.reshape(z_size * kv_dev, page_rows, both_dim), plane_size)
    received = received.reshape(team_size * slots_dev, kv_dev, page_rows, both_dim)
    gathered_pages = received[page_table % (team_size * slots_dev)]
    keys_part = gathered_pages[..., :head_dim]
    values_part = gathered_pages[..., head_dim:]
    query_rows = queries.reshape(requests, half_rows, kv_dev, per_kv, head_dim)
    key_count = pages_max * page_rows
    scores = jnp.einsum(
        "rukgd,rpkwd->rukgpw", query_rows, keys_part, preferred_element_type=jnp.float32
    )
    scores = scores.reshape(requests, half_rows, kv_dev, per_kv, key_count) * head_dim ** (-0.5)
    position = jnp.arange(key_count, dtype=jnp.int32)
    local_row = jnp.arange(half_rows, dtype=jnp.int32)
    offset = (local_row // tok_dev * dec_size + dec_index) * tok_dev + local_row % tok_dev
    last_seen = prior_len[:, None] + offset[None, :]
    visible = (position[None, None, :] <= last_seen[:, :, None])[:, :, None, None, :]
    scores = jnp.where(visible, scores, -1e30)
    row_top = jnp.max(scores, axis=-1, keepdims=True)
    raw_weights = jnp.where(visible, jnp.exp(scores - row_top), 0.0)
    totals = jnp.sum(raw_weights, axis=-1)
    weights_low = raw_weights.astype(jnp.bfloat16).reshape(
        requests, half_rows, kv_dev, per_kv, pages_max, page_rows
    )
    weighted = jnp.einsum(
        "rukgpw,rpkwd->rukgd", weights_low, values_part, preferred_element_type=jnp.float32
    )
    attended = (
        (weighted / totals[..., None])
        .astype(jnp.bfloat16)
        .reshape(requests * half_rows, heads_dev * head_dim)
    )
    y_size = lax.axis_size("y")
    width = out_weight.shape[1]
    projected = ring_reduce_scatter(attended, out_weight, z_size, y_size, ("y",), 0)[0]
    mid_state = residual.astype(jnp.float32) + projected
    routed_dev = tok_dev * TOPK // EXPERTS
    row_lists = []
    gate_lists = []
    for expert in range(EXP_WIN):
        names_it = expert_ids == expert
        chosen_rows = jnp.nonzero(jnp.any(names_it, axis=-1), size=routed_dev)[0].astype(jnp.int32)
        row_lists.append(chosen_rows)
        gate_lists.append(jnp.sum(jnp.where(names_it, expert_gates, 0.0), axis=-1)[chosen_rows])
    picked_rows = jnp.stack(row_lists, axis=0)
    picked_gates = jnp.stack(gate_lists, axis=0)
    inverse = lax.rsqrt(jnp.mean(mid_state * mid_state, axis=-1, keepdims=True) + 1e-05)
    normed_all = (mid_state * inverse * moe_gain).astype(jnp.bfloat16)
    width = normed_all.shape[1]
    by_expert = normed_all[picked_rows]
    row_piece = gather_rows(by_expert, z_size, plane_size)
    row_piece = row_piece.reshape(team_size * routed_dev, width)
    gate_part = jnp.dot(row_piece, w_gate[0].T, preferred_element_type=jnp.float32)
    up_part = jnp.dot(row_piece, w_up[0].T, preferred_element_type=jnp.float32)
    hidden = (jax.nn.silu(gate_part) * up_part).astype(jnp.bfloat16)
    expert_out = ring_reduce_scatter(
        hidden, w_down[0], z_size, y_size * dec_size, ("y", "dec"), 1, whole=True
    )
    mixture = jnp.zeros_like(mid_state)
    for expert in range(EXP_WIN):
        mixture = mixture.at[picked_rows[expert]].add(
            expert_out[expert] * picked_gates[expert][:, None]
        )
    layer_out = (mid_state + mixture).astype(jnp.bfloat16)
    pool_later, _ = lax.optimization_barrier((kv_pool, attended))
    decode_pages = hand_over(pool_later, page_target)
    return (layer_out, decode_pages)


def fine_mesh(mesh):
    tp_devices = mesh.devices[0, :, 0]
    y_size = len({device.coords[1] for device in tp_devices})
    shape = (mesh.shape["rep"], mesh.shape["tp"] // y_size, y_size, mesh.shape["dec"])
    return jax.sharding.Mesh(mesh.devices.reshape(shape), ("rep", "z", "y", "dec"))


def solution(mesh):
    team = ("rep", "z", "y", "dec")
    return jax.shard_map(
        on_device,
        mesh=fine_mesh(mesh),
        in_specs=(
            P(team, None),
            P("rep", "dec", None, ("z", "y")),
            P(team, None, None, None),
            P("rep"),
            P("rep", None),
            P(team),
            P(("z", "y"), None),
            P(),
            P(team, None),
            P(team, None),
            P("dec", ("z", "y"), None),
            P("dec", ("z", "y"), None),
            P("dec", ("z", "y"), None),
        ),
        out_specs=(P(team, None), P(team, None, None, None)),
        check_vma=False,
    )
```

```python
import functools

import jax
import jax.numpy as jnp
from jax import lax
from jax.sharding import PartitionSpec as P
from jax.experimental import pallas as pl
from jax.experimental.pallas import tpu as pltpu

QH = 32
KVH = 8
EXPERTS = 8
TOPK = 2
EXP_WIN = 2


MESH = pl.DeviceIdType.MESH

def _ring_kernel(whole, plane, rows_ref, weight_ref, out_ref, recv_buf, send_buf, send_sem, recv_sem,
                 ring_out, plane_send, plane_recv, plane_send_sem, plane_recv_sem, *product):
    n = recv_buf.shape[1] + 1
    half = recv_buf.shape[2]
    peers = plane_send.shape[0]
    groups = out_ref.shape[0]
    per_peer = plane_send.shape[1]
    me = lax.axis_index("z")
    rep = lax.axis_index("rep")
    yy = lax.axis_index("y")
    dd = lax.axis_index("dec")
    right = lax.rem(me + 1, n)
    left = lax.rem(me + n - 1, n)
    if len(plane) == 2:
        me_plane = yy * groups + dd

        def plane_device(index):
            return (rep, me, index // groups, lax.rem(index, groups))
    else:
        me_plane = yy

        def plane_device(index):
            return (rep, me, index, dd)

    if whole:
        product[0][...] = jnp.dot(rows_ref[...], weight_ref[...], preferred_element_type=jnp.float32)

    def block_part(block, way):
        start = pl.multiple_of(block * (2 * half) + way * half, half)
        if whole:
            return product[0][pl.ds(start, half), :]
        piece = rows_ref[pl.ds(start, half), :]
        return jnp.dot(piece, weight_ref[...], preferred_element_type=jnp.float32)

    barrier = pltpu.get_barrier_semaphore()
    for neighbour in (left, right):
        pl.semaphore_signal(barrier, inc=1, device_id=(rep, neighbour, yy, dd), device_id_type=MESH)
    for offset in range(1, peers):
        target = lax.rem(me_plane + offset, peers)
        pl.semaphore_signal(barrier, inc=1, device_id=plane_device(target), device_id_type=MESH)
    pl.semaphore_wait(barrier, 2 + peers - 1)
    for way in range(2):
        if way == 0:
            block = lax.rem(me + n - 1, n)
        else:
            block = lax.rem(me + 1, n)
        send_buf[way, 0] = block_part(block, way).astype(send_buf.dtype)
    for step in range(n - 1):
        copies = []
        for way in range(2):
            target = right if way == 0 else left
            copy = pltpu.make_async_remote_copy(
                src_ref=send_buf.at[way, step],
                dst_ref=recv_buf.at[way, step],
                send_sem=send_sem.at[way, step],
                recv_sem=recv_sem.at[way, step],
                device_id=(rep, target, yy, dd),
                device_id_type=MESH,
            )
            copy.start()
            copies.append(copy)
        for way in range(2):
            if way == 0:
                block = lax.rem(me + 2 * n - 2 - step, n)
            else:
                block = lax.rem(me + 2 + step, n)
            own = block_part(block, way)
            copies[way].wait()
            total = recv_buf[way, step].astype(jnp.float32) + own
            if step < n - 2:
                send_buf[way, step + 1] = total.astype(send_buf.dtype)
            else:
                ring_out[pl.ds(way * half, half), :] = total
    for index in range(peers):
        plane_send[index] = ring_out[pl.ds(index * per_peer, per_peer), :].astype(plane_send.dtype)
    sent = []
    for offset in range(1, peers):
        target = lax.rem(me_plane + offset, peers)
        copy = pltpu.make_async_remote_copy(
            src_ref=plane_send.at[target],
            dst_ref=plane_recv.at[me_plane],
            send_sem=plane_send_sem.at[offset],
            recv_sem=plane_recv_sem.at[me_plane],
            device_id=plane_device(target),
            device_id_type=MESH,
        )
        copy.start()
        sent.append(copy)
    plane_recv[me_plane] = plane_send[me_plane]
    for copy in sent:
        copy.wait_send()
    for offset in range(1, peers):
        source = lax.rem(me_plane + peers - offset, peers)
        arrival = pltpu.make_async_remote_copy(
            src_ref=plane_send.at[source],
            dst_ref=plane_recv.at[source],
            send_sem=plane_send_sem.at[offset],
            recv_sem=plane_recv_sem.at[source],
            device_id=plane_device(source),
            device_id_type=MESH,
        )
        arrival.wait_recv()
    for group in range(groups):
        total = plane_recv[group].astype(jnp.float32)
        for index in range(group + groups, peers, groups):
            total = total + plane_recv[index].astype(jnp.float32)
        out_ref[group] = total


def ring_reduce_scatter(rows, weight, n, peers, plane, call_id, whole=False):
    half = rows.shape[0] // (2 * n)
    width = weight.shape[1]
    groups = 2 if len(plane) == 2 else 1
    per_peer = 2 * half // peers
    return pl.pallas_call(
        functools.partial(_ring_kernel, whole, plane),
        out_shape=jax.ShapeDtypeStruct((groups, per_peer, width), jnp.float32),
        in_specs=[pl.BlockSpec(memory_space=pltpu.VMEM)] * 2,
        out_specs=pl.BlockSpec(memory_space=pltpu.VMEM),
        scratch_shapes=[
            pltpu.VMEM((2, n - 1, half, width), jnp.bfloat16),
            pltpu.VMEM((2, n - 1, half, width), jnp.bfloat16),
            pltpu.SemaphoreType.DMA((2, n - 1)),
            pltpu.SemaphoreType.DMA((2, n - 1)),
            pltpu.VMEM((2 * half, width), jnp.float32),
            pltpu.VMEM((peers, per_peer, width), jnp.bfloat16),
            pltpu.VMEM((peers, per_peer, width), jnp.bfloat16),
            pltpu.SemaphoreType.DMA((peers,)),
            pltpu.SemaphoreType.DMA((peers,)),
        ]
        + ([pltpu.VMEM((rows.shape[0], width), jnp.float32)] if whole else []),
        compiler_params=pltpu.CompilerParams(collective_id=call_id, has_side_effects=True),
    )(rows, weight)


def _pages_kernel(pages_ref, out_ref, arrived, z_send, z_recv, p_send, p_recv):
    nz = pages_ref.shape[0]
    peers = out_ref.shape[1]
    groups = lax.axis_size("dec")
    mz = lax.axis_index("z")
    rep = lax.axis_index("rep")
    yy = lax.axis_index("y")
    dd = lax.axis_index("dec")
    mp = yy * groups + dd

    def z_device(index):
        return (rep, index, yy, dd)

    def plane_device(index):
        return (rep, mz, index // groups, lax.rem(index, groups))

    barrier = pltpu.get_barrier_semaphore()
    for offset in range(1, nz):
        pl.semaphore_signal(barrier, inc=1, device_id=z_device(lax.rem(mz + offset, nz)),
                            device_id_type=MESH)
    for offset in range(1, peers):
        pl.semaphore_signal(barrier, inc=1, device_id=plane_device(lax.rem(mp + offset, peers)),
                            device_id_type=MESH)
    pl.semaphore_wait(barrier, nz - 1 + peers - 1)
    z_copies = []
    for offset in range(1, nz):
        target = lax.rem(mz + offset, nz)
        copy = pltpu.make_async_remote_copy(
            src_ref=pages_ref.at[target],
            dst_ref=arrived.at[mz],
            send_sem=z_send.at[offset],
            recv_sem=z_recv.at[mz],
            device_id=z_device(target),
            device_id_type=MESH,
        )
        copy.start()
        z_copies.append(copy)
    forwards = []

    def forward(source, page_ref):
        for offset in range(1, peers):
            target = lax.rem(mp + offset, peers)
            copy = pltpu.make_async_remote_copy(
                src_ref=page_ref,
                dst_ref=out_ref.at[source, mp],
                send_sem=p_send.at[source, offset],
                recv_sem=p_recv.at[source, mp],
                device_id=plane_device(target),
                device_id_type=MESH,
            )
            copy.start()
            forwards.append(copy)
        out_ref[source, mp] = page_ref[...]

    forward(mz, pages_ref.at[mz])
    order = []
    for distance in range(1, nz // 2 + 1):
        for offset in (nz - distance, distance):
            if offset not in order:
                order.append(offset)
    for offset in order:
        source = lax.rem(mz + offset, nz)
        arrival = pltpu.make_async_remote_copy(
            src_ref=pages_ref.at[source],
            dst_ref=arrived.at[source],
            send_sem=z_send.at[offset],
            recv_sem=z_recv.at[source],
            device_id=z_device(source),
            device_id_type=MESH,
        )
        arrival.wait_recv()
        forward(source, arrived.at[source])
    for copy in z_copies:
        copy.wait_send()
    for copy in forwards:
        copy.wait_send()
    for source in range(nz):
        for offset in range(1, peers):
            sender = lax.rem(mp + peers - offset, peers)
            arrival = pltpu.make_async_remote_copy(
                src_ref=pages_ref.at[source],
                dst_ref=out_ref.at[source, sender],
                send_sem=p_send.at[source, offset],
                recv_sem=p_recv.at[source, sender],
                device_id=plane_device(sender),
                device_id_type=MESH,
            )
            arrival.wait_recv()


def exchange_pages(pages, peers):
    nz = pages.shape[0]
    block = pages.shape[1:]
    return pl.pallas_call(
        _pages_kernel,
        out_shape=jax.ShapeDtypeStruct((nz, peers) + block, pages.dtype),
        in_specs=[pl.BlockSpec(memory_space=pltpu.VMEM)],
        out_specs=pl.BlockSpec(memory_space=pltpu.VMEM),
        scratch_shapes=[
            pltpu.VMEM((nz,) + block, pages.dtype),
            pltpu.SemaphoreType.DMA((nz,)),
            pltpu.SemaphoreType.DMA((nz,)),
            pltpu.SemaphoreType.DMA((nz, peers)),
            pltpu.SemaphoreType.DMA((nz, peers)),
        ],
        compiler_params=pltpu.CompilerParams(collective_id=2, has_side_effects=True),
    )(pages)


def _rows_kernel(rows_ref, out_ref, plane_rows, p_send, p_recv, send_sem, recv_sem):
    nz = out_ref.shape[0]
    peers = plane_rows.shape[0]
    each = plane_rows.shape[1]
    part = out_ref.shape[1] // 2
    groups = lax.axis_size("dec")
    mz = lax.axis_index("z")
    rep = lax.axis_index("rep")
    yy = lax.axis_index("y")
    dd = lax.axis_index("dec")
    mp = yy * groups + dd
    right = lax.rem(mz + 1, nz)
    left = lax.rem(mz + nz - 1, nz)

    def plane_device(index):
        return (rep, mz, index // groups, lax.rem(index, groups))

    barrier = pltpu.get_barrier_semaphore()
    for neighbour in (left, right):
        pl.semaphore_signal(barrier, inc=1, device_id=(rep, neighbour, yy, dd), device_id_type=MESH)
    for offset in range(1, peers):
        pl.semaphore_signal(barrier, inc=1, device_id=plane_device(lax.rem(mp + offset, peers)),
                            device_id_type=MESH)
    pl.semaphore_wait(barrier, 2 + peers - 1)
    sent = []
    for offset in range(1, peers):
        target = lax.rem(mp + offset, peers)
        copy = pltpu.make_async_remote_copy(
            src_ref=rows_ref.at[lax.rem(target, groups)],
            dst_ref=plane_rows.at[mp],
            send_sem=p_send.at[offset],
            recv_sem=p_recv.at[mp],
            device_id=plane_device(target),
            device_id_type=MESH,
        )
        copy.start()
        sent.append(copy)
    plane_rows[mp] = rows_ref[dd]
    for copy in sent:
        copy.wait_send()
    for offset in range(1, peers):
        sender = lax.rem(mp + peers - offset, peers)
        arrival = pltpu.make_async_remote_copy(
            src_ref=rows_ref.at[0],
            dst_ref=plane_rows.at[sender],
            send_sem=p_send.at[offset],
            recv_sem=p_recv.at[sender],
            device_id=plane_device(sender),
            device_id_type=MESH,
        )
        arrival.wait_recv()
    for index in range(peers):
        out_ref[mz, pl.ds(index * each, each), :] = plane_rows[index]
    for step in range(nz - 1):
        copies = []
        for way in range(2):
            if way == 0:
                target, source = right, lax.rem(mz + nz - step, nz)
            else:
                target, source = left, lax.rem(mz + step, nz)
            src = out_ref.at[source, pl.ds(way * part, part)]
            copy = pltpu.make_async_remote_copy(
                src_ref=src,
                dst_ref=out_ref.at[source, pl.ds(way * part, part)],
                send_sem=send_sem.at[way, step],
                recv_sem=recv_sem.at[way, step],
                device_id=(rep, target, yy, dd),
                device_id_type=MESH,
            )
            copy.start()
            copies.append(copy)
        for copy in copies:
            copy.wait()


def gather_rows(rows, nz, peers):
    block = rows.shape[1:]
    return pl.pallas_call(
        _rows_kernel,
        out_shape=jax.ShapeDtypeStruct((nz, peers * block[0], block[1]), rows.dtype),
        in_specs=[pl.BlockSpec(memory_space=pltpu.VMEM)],
        out_specs=pl.BlockSpec(memory_space=pltpu.VMEM),
        scratch_shapes=[
            pltpu.VMEM((peers,) + block, rows.dtype),
            pltpu.SemaphoreType.DMA((peers,)),
            pltpu.SemaphoreType.DMA((peers,)),
            pltpu.SemaphoreType.DMA((2, nz - 1)),
            pltpu.SemaphoreType.DMA((2, nz - 1)),
        ],
        compiler_params=pltpu.CompilerParams(collective_id=3, has_side_effects=True),
    )(rows)


def hand_over(kv_pool, page_target):
    rep_size = lax.axis_size("rep")
    owners = jnp.arange(rep_size, dtype=jnp.int32)
    selected = (page_target[None, :] == owners[:, None])[:, :, None, None, None]
    outgoing = jnp.where(selected, kv_pool[None], jnp.zeros((), kv_pool.dtype))
    incoming = lax.all_to_all(outgoing, "rep", split_axis=0, concat_axis=0, tiled=True)
    return jnp.sum(incoming, axis=0)


def on_device(
    residual,
    queries,
    kv_pool,
    prior_len,
    page_table,
    page_target,
    out_weight,
    moe_gain,
    expert_ids,
    expert_gates,
    w_gate,
    w_up,
    w_down,
):
    tp_size = lax.axis_size("z") * lax.axis_size("y")
    dec_size = lax.axis_size("dec")
    dec_index = lax.axis_index("dec")
    slots_dev, kv_heads, page_rows, both_dim = kv_pool.shape
    head_dim = both_dim // 2
    heads_dev = queries.shape[3] // head_dim
    group_size = QH // KVH
    kv_dev = max(1, heads_dev // group_size)
    copies = max(1, group_size // heads_dev)
    per_kv = heads_dev // kv_dev
    requests = prior_len.shape[0]
    tok_dev = queries.shape[2]
    half_rows = queries.shape[0] * tok_dev // requests
    pages_max = page_table.shape[1]
    team_size = tp_size * dec_size
    z_size = lax.axis_size("z")
    plane_size = team_size // z_size
    received = exchange_pages(kv_pool.reshape(z_size * kv_dev, page_rows, both_dim), plane_size)
    received = received.reshape(team_size * slots_dev, kv_dev, page_rows, both_dim)
    gathered_pages = received[page_table % (team_size * slots_dev)]
    keys_part = gathered_pages[..., :head_dim]
    values_part = gathered_pages[..., head_dim:]
    query_rows = queries.reshape(requests, half_rows, kv_dev, per_kv, head_dim)
    key_count = pages_max * page_rows
    scores = jnp.einsum(
        "rukgd,rpkwd->rukgpw", query_rows, keys_part, preferred_element_type=jnp.float32
    )
    scores = scores.reshape(requests, half_rows, kv_dev, per_kv, key_count) * head_dim ** (-0.5)
    position = jnp.arange(key_count, dtype=jnp.int32)
    local_row = jnp.arange(half_rows, dtype=jnp.int32)
    offset = (local_row // tok_dev * dec_size + dec_index) * tok_dev + local_row % tok_dev
    last_seen = prior_len[:, None] + offset[None, :]
    visible = (position[None, None, :] <= last_seen[:, :, None])[:, :, None, None, :]
    scores = jnp.where(visible, scores, -1e30)
    row_top = jnp.max(scores, axis=-1, keepdims=True)
    raw_weights = jnp.where(visible, jnp.exp(scores - row_top), 0.0)
    totals = jnp.sum(raw_weights, axis=-1)
    weights_low = raw_weights.astype(jnp.bfloat16).reshape(
        requests, half_rows, kv_dev, per_kv, pages_max, page_rows
    )
    weighted = jnp.einsum(
        "rukgpw,rpkwd->rukgd", weights_low, values_part, preferred_element_type=jnp.float32
    )
    attended = (
        (weighted / totals[..., None])
        .astype(jnp.bfloat16)
        .reshape(requests * half_rows, heads_dev * head_dim)
    )
    y_size = lax.axis_size("y")
    width = out_weight.shape[1]
    projected = ring_reduce_scatter(attended, out_weight, z_size, y_size, ("y",), 0)[0]
    mid_state = residual.astype(jnp.float32) + projected
    routed_dev = tok_dev * TOPK // EXPERTS
    row_lists = []
    gate_lists = []
    for expert in range(EXP_WIN):
        names_it = expert_ids == expert
        chosen_rows = jnp.nonzero(jnp.any(names_it, axis=-1), size=routed_dev)[0].astype(jnp.int32)
        row_lists.append(chosen_rows)
        gate_lists.append(jnp.sum(jnp.where(names_it, expert_gates, 0.0), axis=-1)[chosen_rows])
    picked_rows = jnp.stack(row_lists, axis=0)
    picked_gates = jnp.stack(gate_lists, axis=0)
    inverse = lax.rsqrt(jnp.mean(mid_state * mid_state, axis=-1, keepdims=True) + 1e-05)
    normed_all = (mid_state * inverse * moe_gain).astype(jnp.bfloat16)
    width = normed_all.shape[1]
    by_expert = normed_all[picked_rows]
    row_piece = gather_rows(by_expert, z_size, plane_size)
    row_piece = row_piece.reshape(team_size * routed_dev, width)
    gate_part = jnp.dot(row_piece, w_gate[0].T, preferred_element_type=jnp.float32)
    up_part = jnp.dot(row_piece, w_up[0].T, preferred_element_type=jnp.float32)
    hidden = (jax.nn.silu(gate_part) * up_part).astype(jnp.bfloat16)
    expert_out = ring_reduce_scatter(
        hidden, w_down[0], z_size, y_size * dec_size, ("y", "dec"), 1, whole=True
    )
    mixture = jnp.zeros_like(mid_state)
    for expert in range(EXP_WIN):
        mixture = mixture.at[picked_rows[expert]].add(
            expert_out[expert] * picked_gates[expert][:, None]
        )
    layer_out = (mid_state + mixture).astype(jnp.bfloat16)
    pool_later, _ = lax.optimization_barrier((kv_pool, attended))
    decode_pages = hand_over(pool_later, page_target)
    return (layer_out, decode_pages)


def fine_mesh(mesh):
    tp_devices = mesh.devices[0, :, 0]
    y_size = len({device.coords[1] for device in tp_devices})
    shape = (mesh.shape["rep"], mesh.shape["tp"] // y_size, y_size, mesh.shape["dec"])
    return jax.sharding.Mesh(mesh.devices.reshape(shape), ("rep", "z", "y", "dec"))


def solution(mesh):
    team = ("rep", "z", "y", "dec")
    return jax.shard_map(
        on_device,
        mesh=fine_mesh(mesh),
        in_specs=(
            P(team, None),
            P("rep", "dec", None, ("z", "y")),
            P(team, None, None, None),
            P("rep"),
            P("rep", None),
            P(team),
            P(("z", "y"), None),
            P(),
            P(team, None),
            P(team, None),
            P("dec", ("z", "y"), None),
            P("dec", ("z", "y"), None),
            P("dec", ("z", "y"), None),
        ),
        out_specs=(P(team, None), P(team, None, None, None)),
        check_vma=False,
    )
```

```python
import functools

import jax
import jax.numpy as jnp
from jax import lax
from jax.sharding import PartitionSpec as P
from jax.experimental import pallas as pl
from jax.experimental.pallas import tpu as pltpu

QH = 32
KVH = 8
EXPERTS = 8
TOPK = 2
EXP_WIN = 2


MESH = pl.DeviceIdType.MESH

def _ring_kernel(whole, plane, rows_ref, weight_ref, out_ref, recv_buf, send_buf, send_sem, recv_sem,
                 ring_out, plane_send, plane_recv, plane_send_sem, plane_recv_sem, *product):
    n = recv_buf.shape[1] + 1
    half = recv_buf.shape[2]
    peers = plane_send.shape[0]
    groups = out_ref.shape[0]
    per_peer = plane_send.shape[1]
    me = lax.axis_index("z")
    rep = lax.axis_index("rep")
    yy = lax.axis_index("y")
    dd = lax.axis_index("dec")
    right = lax.rem(me + 1, n)
    left = lax.rem(me + n - 1, n)
    if len(plane) == 2:
        me_plane = yy * groups + dd

        def plane_device(index):
            return (rep, me, index // groups, lax.rem(index, groups))
    else:
        me_plane = yy

        def plane_device(index):
            return (rep, me, index, dd)

    if whole:
        product[0][...] = jnp.dot(rows_ref[...], weight_ref[...], preferred_element_type=jnp.float32)

    def block_part(block, way):
        start = pl.multiple_of(block * (2 * half) + way * half, half)
        if whole:
            return product[0][pl.ds(start, half), :]
        piece = rows_ref[pl.ds(start, half), :]
        return jnp.dot(piece, weight_ref[...], preferred_element_type=jnp.float32)

    barrier = pltpu.get_barrier_semaphore()
    for neighbour in (left, right):
        pl.semaphore_signal(barrier, inc=1, device_id=(rep, neighbour, yy, dd), device_id_type=MESH)
    for offset in range(1, peers):
        target = lax.rem(me_plane + offset, peers)
        pl.semaphore_signal(barrier, inc=1, device_id=plane_device(target), device_id_type=MESH)
    pl.semaphore_wait(barrier, 2 + peers - 1)
    for way in range(2):
        if way == 0:
            block = lax.rem(me + n - 1, n)
        else:
            block = lax.rem(me + 1, n)
        send_buf[way, 0] = block_part(block, way).astype(send_buf.dtype)
    for step in range(n - 1):
        copies = []
        for way in range(2):
            target = right if way == 0 else left
            copy = pltpu.make_async_remote_copy(
                src_ref=send_buf.at[way, step],
                dst_ref=recv_buf.at[way, step],
                send_sem=send_sem.at[way, step],
                recv_sem=recv_sem.at[way, step],
                device_id=(rep, target, yy, dd),
                device_id_type=MESH,
            )
            copy.start()
            copies.append(copy)
        for way in range(2):
            if way == 0:
                block = lax.rem(me + 2 * n - 2 - step, n)
            else:
                block = lax.rem(me + 2 + step, n)
            own = block_part(block, way)
            copies[way].wait()
            total = recv_buf[way, step].astype(jnp.float32) + own
            if step < n - 2:
                send_buf[way, step + 1] = total.astype(send_buf.dtype)
            else:
                ring_out[pl.ds(way * half, half), :] = total
    for index in range(peers):
        plane_send[index] = ring_out[pl.ds(index * per_peer, per_peer), :].astype(plane_send.dtype)
    sent = []
    for offset in range(1, peers):
        target = lax.rem(me_plane + offset, peers)
        copy = pltpu.make_async_remote_copy(
            src_ref=plane_send.at[target],
            dst_ref=plane_recv.at[me_plane],
            send_sem=plane_send_sem.at[offset],
            recv_sem=plane_recv_sem.at[me_plane],
            device_id=plane_device(target),
            device_id_type=MESH,
        )
        copy.start()
        sent.append(copy)
    plane_recv[me_plane] = plane_send[me_plane]
    for copy in sent:
        copy.wait_send()
    for offset in range(1, peers):
        source = lax.rem(me_plane + peers - offset, peers)
        arrival = pltpu.make_async_remote_copy(
            src_ref=plane_send.at[source],
            dst_ref=plane_recv.at[source],
            send_sem=plane_send_sem.at[offset],
            recv_sem=plane_recv_sem.at[source],
            device_id=plane_device(source),
            device_id_type=MESH,
        )
        arrival.wait_recv()
    for group in range(groups):
        total = plane_recv[group].astype(jnp.float32)
        for index in range(group + groups, peers, groups):
            total = total + plane_recv[index].astype(jnp.float32)
        out_ref[group] = total


def ring_reduce_scatter(rows, weight, n, peers, plane, call_id, whole=False):
    half = rows.shape[0] // (2 * n)
    width = weight.shape[1]
    groups = 2 if len(plane) == 2 else 1
    per_peer = 2 * half // peers
    return pl.pallas_call(
        functools.partial(_ring_kernel, whole, plane),
        out_shape=jax.ShapeDtypeStruct((groups, per_peer, width), jnp.float32),
        in_specs=[pl.BlockSpec(memory_space=pltpu.VMEM)] * 2,
        out_specs=pl.BlockSpec(memory_space=pltpu.VMEM),
        scratch_shapes=[
            pltpu.VMEM((2, n - 1, half, width), jnp.bfloat16),
            pltpu.VMEM((2, n - 1, half, width), jnp.bfloat16),
            pltpu.SemaphoreType.DMA((2, n - 1)),
            pltpu.SemaphoreType.DMA((2, n - 1)),
            pltpu.VMEM((2 * half, width), jnp.float32),
            pltpu.VMEM((peers, per_peer, width), jnp.bfloat16),
            pltpu.VMEM((peers, per_peer, width), jnp.bfloat16),
            pltpu.SemaphoreType.DMA((peers,)),
            pltpu.SemaphoreType.DMA((peers,)),
        ]
        + ([pltpu.VMEM((rows.shape[0], width), jnp.float32)] if whole else []),
        compiler_params=pltpu.CompilerParams(collective_id=call_id, has_side_effects=True),
    )(rows, weight)


def _pages_kernel(pages_ref, out_ref, arrived, z_send, z_recv, p_send, p_recv):
    nz = pages_ref.shape[0]
    peers = out_ref.shape[1]
    groups = lax.axis_size("dec")
    mz = lax.axis_index("z")
    rep = lax.axis_index("rep")
    yy = lax.axis_index("y")
    dd = lax.axis_index("dec")
    mp = yy * groups + dd

    def z_device(index):
        return (rep, index, yy, dd)

    def plane_device(index):
        return (rep, mz, index // groups, lax.rem(index, groups))

    barrier = pltpu.get_barrier_semaphore()
    for offset in range(1, nz):
        pl.semaphore_signal(barrier, inc=1, device_id=z_device(lax.rem(mz + offset, nz)),
                            device_id_type=MESH)
    for offset in range(1, peers):
        pl.semaphore_signal(barrier, inc=1, device_id=plane_device(lax.rem(mp + offset, peers)),
                            device_id_type=MESH)
    pl.semaphore_wait(barrier, nz - 1 + peers - 1)
    z_copies = []
    for offset in range(1, nz):
        target = lax.rem(mz + offset, nz)
        copy = pltpu.make_async_remote_copy(
            src_ref=pages_ref.at[target],
            dst_ref=arrived.at[mz],
            send_sem=z_send.at[offset],
            recv_sem=z_recv.at[mz],
            device_id=z_device(target),
            device_id_type=MESH,
        )
        copy.start()
        z_copies.append(copy)
    forwards = []

    def forward(source, page_ref):
        for offset in range(1, peers):
            target = lax.rem(mp + offset, peers)
            copy = pltpu.make_async_remote_copy(
                src_ref=page_ref,
                dst_ref=out_ref.at[source, mp],
                send_sem=p_send.at[source, offset],
                recv_sem=p_recv.at[source, mp],
                device_id=plane_device(target),
                device_id_type=MESH,
            )
            copy.start()
            forwards.append(copy)
        out_ref[source, mp] = page_ref[...]

    forward(mz, pages_ref.at[mz])
    order = []
    for distance in range(1, nz // 2 + 1):
        for offset in (nz - distance, distance):
            if offset not in order:
                order.append(offset)
    for offset in order:
        source = lax.rem(mz + offset, nz)
        arrival = pltpu.make_async_remote_copy(
            src_ref=pages_ref.at[source],
            dst_ref=arrived.at[source],
            send_sem=z_send.at[offset],
            recv_sem=z_recv.at[source],
            device_id=z_device(source),
            device_id_type=MESH,
        )
        arrival.wait_recv()
        forward(source, arrived.at[source])
    for copy in z_copies:
        copy.wait_send()
    for copy in forwards:
        copy.wait_send()
    for source in range(nz):
        for offset in range(1, peers):
            sender = lax.rem(mp + peers - offset, peers)
            arrival = pltpu.make_async_remote_copy(
                src_ref=pages_ref.at[source],
                dst_ref=out_ref.at[source, sender],
                send_sem=p_send.at[source, offset],
                recv_sem=p_recv.at[source, sender],
                device_id=plane_device(sender),
                device_id_type=MESH,
            )
            arrival.wait_recv()


def exchange_pages(pages, peers):
    nz = pages.shape[0]
    block = pages.shape[1:]
    return pl.pallas_call(
        _pages_kernel,
        out_shape=jax.ShapeDtypeStruct((nz, peers) + block, pages.dtype),
        in_specs=[pl.BlockSpec(memory_space=pltpu.VMEM)],
        out_specs=pl.BlockSpec(memory_space=pltpu.VMEM),
        scratch_shapes=[
            pltpu.VMEM((nz,) + block, pages.dtype),
            pltpu.SemaphoreType.DMA((nz,)),
            pltpu.SemaphoreType.DMA((nz,)),
            pltpu.SemaphoreType.DMA((nz, peers)),
            pltpu.SemaphoreType.DMA((nz, peers)),
        ],
        compiler_params=pltpu.CompilerParams(collective_id=2, has_side_effects=True),
    )(pages)


def _rows_kernel(rows_ref, out_ref, plane_rows, p_send, p_recv, send_sem, recv_sem):
    nz = out_ref.shape[0]
    peers = plane_rows.shape[0]
    each = plane_rows.shape[1]
    part = out_ref.shape[1] // 2
    groups = lax.axis_size("dec")
    mz = lax.axis_index("z")
    rep = lax.axis_index("rep")
    yy = lax.axis_index("y")
    dd = lax.axis_index("dec")
    mp = yy * groups + dd
    right = lax.rem(mz + 1, nz)
    left = lax.rem(mz + nz - 1, nz)

    def plane_device(index):
        return (rep, mz, index // groups, lax.rem(index, groups))

    barrier = pltpu.get_barrier_semaphore()
    for neighbour in (left, right):
        pl.semaphore_signal(barrier, inc=1, device_id=(rep, neighbour, yy, dd), device_id_type=MESH)
    for offset in range(1, peers):
        pl.semaphore_signal(barrier, inc=1, device_id=plane_device(lax.rem(mp + offset, peers)),
                            device_id_type=MESH)
    pl.semaphore_wait(barrier, 2 + peers - 1)
    sent = []
    for offset in range(1, peers):
        target = lax.rem(mp + offset, peers)
        copy = pltpu.make_async_remote_copy(
            src_ref=rows_ref.at[lax.rem(target, groups)],
            dst_ref=plane_rows.at[mp],
            send_sem=p_send.at[offset],
            recv_sem=p_recv.at[mp],
            device_id=plane_device(target),
            device_id_type=MESH,
        )
        copy.start()
        sent.append(copy)
    plane_rows[mp] = rows_ref[dd]
    for copy in sent:
        copy.wait_send()
    for offset in range(1, peers):
        sender = lax.rem(mp + peers - offset, peers)
        arrival = pltpu.make_async_remote_copy(
            src_ref=rows_ref.at[0],
            dst_ref=plane_rows.at[sender],
            send_sem=p_send.at[offset],
            recv_sem=p_recv.at[sender],
            device_id=plane_device(sender),
            device_id_type=MESH,
        )
        arrival.wait_recv()
    for index in range(peers):
        out_ref[mz, pl.ds(index * each, each), :] = plane_rows[index]
    for step in range(nz - 1):
        copies = []
        for way in range(2):
            if way == 0:
                target, source = right, lax.rem(mz + nz - step, nz)
            else:
                target, source = left, lax.rem(mz + step, nz)
            src = out_ref.at[source, pl.ds(way * part, part)]
            copy = pltpu.make_async_remote_copy(
                src_ref=src,
                dst_ref=out_ref.at[source, pl.ds(way * part, part)],
                send_sem=send_sem.at[way, step],
                recv_sem=recv_sem.at[way, step],
                device_id=(rep, target, yy, dd),
                device_id_type=MESH,
            )
            copy.start()
            copies.append(copy)
        for copy in copies:
            copy.wait()


def gather_rows(rows, nz, peers):
    block = rows.shape[1:]
    return pl.pallas_call(
        _rows_kernel,
        out_shape=jax.ShapeDtypeStruct((nz, peers * block[0], block[1]), rows.dtype),
        in_specs=[pl.BlockSpec(memory_space=pltpu.VMEM)],
        out_specs=pl.BlockSpec(memory_space=pltpu.VMEM),
        scratch_shapes=[
            pltpu.VMEM((peers,) + block, rows.dtype),
            pltpu.SemaphoreType.DMA((peers,)),
            pltpu.SemaphoreType.DMA((peers,)),
            pltpu.SemaphoreType.DMA((2, nz - 1)),
            pltpu.SemaphoreType.DMA((2, nz - 1)),
        ],
        compiler_params=pltpu.CompilerParams(collective_id=3, has_side_effects=True),
    )(rows)


def hand_over(kv_pool, page_target):
    rep_size = lax.axis_size("rep")
    owners = jnp.arange(rep_size, dtype=jnp.int32)
    selected = (page_target[None, :] == owners[:, None])[:, :, None, None, None]
    outgoing = jnp.where(selected, kv_pool[None], jnp.zeros((), kv_pool.dtype))
    incoming = lax.all_to_all(outgoing, "rep", split_axis=0, concat_axis=0, tiled=True)
    return jnp.sum(incoming, axis=0)


def on_device(
    residual,
    queries,
    kv_pool,
    prior_len,
    page_table,
    page_target,
    out_weight,
    moe_gain,
    expert_ids,
    expert_gates,
    w_gate,
    w_up,
    w_down,
):
    tp_size = lax.axis_size("z") * lax.axis_size("y")
    dec_size = lax.axis_size("dec")
    dec_index = lax.axis_index("dec")
    slots_dev, kv_heads, page_rows, both_dim = kv_pool.shape
    head_dim = both_dim // 2
    heads_dev = queries.shape[3] // head_dim
    group_size = QH // KVH
    kv_dev = max(1, heads_dev // group_size)
    copies = max(1, group_size // heads_dev)
    per_kv = heads_dev // kv_dev
    requests = prior_len.shape[0]
    tok_dev = queries.shape[2]
    half_rows = queries.shape[0] * tok_dev // requests
    pages_max = page_table.shape[1]
    team_size = tp_size * dec_size
    z_size = lax.axis_size("z")
    plane_size = team_size // z_size
    received = exchange_pages(kv_pool.reshape(z_size * kv_dev, page_rows, both_dim), plane_size)
    received = received.reshape(team_size * slots_dev, kv_dev, page_rows, both_dim)
    gathered_pages = received[page_table % (team_size * slots_dev)]
    keys_part = gathered_pages[..., :head_dim]
    values_part = gathered_pages[..., head_dim:]
    query_rows = queries.reshape(requests, half_rows, kv_dev, per_kv, head_dim)
    key_count = pages_max * page_rows
    scores = jnp.einsum(
        "rukgd,rpkwd->rukgpw", query_rows, keys_part, preferred_element_type=jnp.float32
    )
    scores = scores.reshape(requests, half_rows, kv_dev, per_kv, key_count) * head_dim ** (-0.5)
    position = jnp.arange(key_count, dtype=jnp.int32)
    local_row = jnp.arange(half_rows, dtype=jnp.int32)
    offset = (local_row // tok_dev * dec_size + dec_index) * tok_dev + local_row % tok_dev
    last_seen = prior_len[:, None] + offset[None, :]
    visible = (position[None, None, :] <= last_seen[:, :, None])[:, :, None, None, :]
    scores = jnp.where(visible, scores, -1e30)
    row_top = jnp.max(scores, axis=-1, keepdims=True)
    raw_weights = jnp.where(visible, jnp.exp(scores - row_top), 0.0)
    totals = jnp.sum(raw_weights, axis=-1)
    weights_low = raw_weights.astype(jnp.bfloat16).reshape(
        requests, half_rows, kv_dev, per_kv, pages_max, page_rows
    )
    weighted = jnp.einsum(
        "rukgpw,rpkwd->rukgd", weights_low, values_part, preferred_element_type=jnp.float32
    )
    attended = (
        (weighted / totals[..., None])
        .astype(jnp.bfloat16)
        .reshape(requests * half_rows, heads_dev * head_dim)
    )
    y_size = lax.axis_size("y")
    width = out_weight.shape[1]
    projected = ring_reduce_scatter(attended, out_weight, z_size, y_size, ("y",), 0)[0]
    mid_state = residual.astype(jnp.float32) + projected
    routed_dev = tok_dev * TOPK // EXPERTS
    row_lists = []
    gate_lists = []
    for expert in range(EXP_WIN):
        names_it = expert_ids == expert
        chosen_rows = jnp.nonzero(jnp.any(names_it, axis=-1), size=routed_dev)[0].astype(jnp.int32)
        row_lists.append(chosen_rows)
        gate_lists.append(jnp.sum(jnp.where(names_it, expert_gates, 0.0), axis=-1)[chosen_rows])
    picked_rows = jnp.stack(row_lists, axis=0)
    picked_gates = jnp.stack(gate_lists, axis=0)
    inverse = lax.rsqrt(jnp.mean(mid_state * mid_state, axis=-1, keepdims=True) + 1e-05)
    normed_all = (mid_state * inverse * moe_gain).astype(jnp.bfloat16)
    width = normed_all.shape[1]
    by_expert = normed_all[picked_rows]
    row_piece = gather_rows(by_expert, z_size, plane_size)
    row_piece = row_piece.reshape(team_size * routed_dev, width)
    gate_part = jnp.dot(row_piece, w_gate[0].T, preferred_element_type=jnp.float32)
    up_part = jnp.dot(row_piece, w_up[0].T, preferred_element_type=jnp.float32)
    hidden = (jax.nn.silu(gate_part) * up_part).astype(jnp.bfloat16)
    expert_out = ring_reduce_scatter(
        hidden, w_down[0], z_size, y_size * dec_size, ("y", "dec"), 1, whole=True
    )
    weighted_out = expert_out * picked_gates[..., None]
    token_index = jnp.arange(tok_dev, dtype=jnp.int32)
    hits = token_index[:, None, None] == picked_rows[None]
    mixture = jnp.sum(jnp.where(hits[..., None], weighted_out[None], 0.0), axis=(1, 2))
    layer_out = (mid_state + mixture).astype(jnp.bfloat16)
    pool_later, _ = lax.optimization_barrier((kv_pool, attended))
    decode_pages = hand_over(pool_later, page_target)
    return (layer_out, decode_pages)


def fine_mesh(mesh):
    tp_devices = mesh.devices[0, :, 0]
    y_size = len({device.coords[1] for device in tp_devices})
    shape = (mesh.shape["rep"], mesh.shape["tp"] // y_size, y_size, mesh.shape["dec"])
    return jax.sharding.Mesh(mesh.devices.reshape(shape), ("rep", "z", "y", "dec"))


def solution(mesh):
    team = ("rep", "z", "y", "dec")
    return jax.shard_map(
        on_device,
        mesh=fine_mesh(mesh),
        in_specs=(
            P(team, None),
            P("rep", "dec", None, ("z", "y")),
            P(team, None, None, None),
            P("rep"),
            P("rep", None),
            P(team),
            P(("z", "y"), None),
            P(),
            P(team, None),
            P(team, None),
            P("dec", ("z", "y"), None),
            P("dec", ("z", "y"), None),
            P("dec", ("z", "y"), None),
        ),
        out_specs=(P(team, None), P(team, None, None, None)),
        check_vma=False,
    )
```

```python
import functools

import jax
import jax.numpy as jnp
from jax import lax
from jax.sharding import PartitionSpec as P
from jax.experimental import pallas as pl
from jax.experimental.pallas import tpu as pltpu

QH = 32
KVH = 8
EXPERTS = 8
TOPK = 2
EXP_WIN = 2


MESH = pl.DeviceIdType.MESH

def _ring_kernel(whole, plane, hand, *refs):
    if hand:
        rows_ref, weight_ref, outgoing_ref, out_ref, decode_ref = refs[:5]
        rest = refs[5:]
    else:
        rows_ref, weight_ref, out_ref = refs[:3]
        rest = refs[3:]
    (recv_buf, send_buf, send_sem, recv_sem, ring_out, plane_send, plane_recv,
     plane_send_sem, plane_recv_sem) = rest[:9]
    rest = rest[9:]
    if hand:
        hand_buf, hand_send, hand_recv = rest[:3]
        rest = rest[3:]
    product = rest
    n = recv_buf.shape[1] + 1
    half = recv_buf.shape[2]
    peers = plane_send.shape[0]
    groups = out_ref.shape[0]
    per_peer = plane_send.shape[1]
    me = lax.axis_index("z")
    rep = lax.axis_index("rep")
    yy = lax.axis_index("y")
    dd = lax.axis_index("dec")
    right = lax.rem(me + 1, n)
    left = lax.rem(me + n - 1, n)
    if len(plane) == 2:
        me_plane = yy * groups + dd

        def plane_device(index):
            return (rep, me, index // groups, lax.rem(index, groups))
    else:
        me_plane = yy

        def plane_device(index):
            return (rep, me, index, dd)

    if whole:
        product[0][...] = jnp.dot(rows_ref[...], weight_ref[...], preferred_element_type=jnp.float32)

    def block_part(block, way):
        start = pl.multiple_of(block * (2 * half) + way * half, half)
        if whole:
            return product[0][pl.ds(start, half), :]
        piece = rows_ref[pl.ds(start, half), :]
        return jnp.dot(piece, weight_ref[...], preferred_element_type=jnp.float32)

    barrier = pltpu.get_barrier_semaphore()
    for neighbour in (left, right):
        pl.semaphore_signal(barrier, inc=1, device_id=(rep, neighbour, yy, dd), device_id_type=MESH)
    for offset in range(1, peers):
        target = lax.rem(me_plane + offset, peers)
        pl.semaphore_signal(barrier, inc=1, device_id=plane_device(target), device_id_type=MESH)
    reps = lax.axis_size("rep")
    if hand:
        for offset in range(1, reps):
            pl.semaphore_signal(barrier, inc=1, device_id=(lax.rem(rep + offset, reps), me, yy, dd),
                                device_id_type=MESH)
    pl.semaphore_wait(barrier, 2 + peers - 1 + (reps - 1 if hand else 0))
    handed = []
    if hand:
        for offset in range(1, reps):
            target = lax.rem(rep + offset, reps)
            copy = pltpu.make_async_remote_copy(
                src_ref=outgoing_ref.at[target],
                dst_ref=hand_buf.at[rep],
                send_sem=hand_send.at[offset],
                recv_sem=hand_recv.at[rep],
                device_id=(target, me, yy, dd),
                device_id_type=MESH,
            )
            copy.start()
            handed.append(copy)
        hand_buf[rep] = outgoing_ref[rep]
    for way in range(2):
        if way == 0:
            block = lax.rem(me + n - 1, n)
        else:
            block = lax.rem(me + 1, n)
        send_buf[way, 0] = block_part(block, way).astype(send_buf.dtype)
    for step in range(n - 1):
        copies = []
        for way in range(2):
            target = right if way == 0 else left
            copy = pltpu.make_async_remote_copy(
                src_ref=send_buf.at[way, step],
                dst_ref=recv_buf.at[way, step],
                send_sem=send_sem.at[way, step],
                recv_sem=recv_sem.at[way, step],
                device_id=(rep, target, yy, dd),
                device_id_type=MESH,
            )
            copy.start()
            copies.append(copy)
        for way in range(2):
            if way == 0:
                block = lax.rem(me + 2 * n - 2 - step, n)
            else:
                block = lax.rem(me + 2 + step, n)
            own = block_part(block, way)
            copies[way].wait()
            total = recv_buf[way, step].astype(jnp.float32) + own
            if step < n - 2:
                send_buf[way, step + 1] = total.astype(send_buf.dtype)
            else:
                ring_out[pl.ds(way * half, half), :] = total
    for index in range(peers):
        plane_send[index] = ring_out[pl.ds(index * per_peer, per_peer), :].astype(plane_send.dtype)
    sent = []
    for offset in range(1, peers):
        target = lax.rem(me_plane + offset, peers)
        copy = pltpu.make_async_remote_copy(
            src_ref=plane_send.at[target],
            dst_ref=plane_recv.at[me_plane],
            send_sem=plane_send_sem.at[offset],
            recv_sem=plane_recv_sem.at[me_plane],
            device_id=plane_device(target),
            device_id_type=MESH,
        )
        copy.start()
        sent.append(copy)
    plane_recv[me_plane] = plane_send[me_plane]
    for copy in sent:
        copy.wait_send()
    for offset in range(1, peers):
        source = lax.rem(me_plane + peers - offset, peers)
        arrival = pltpu.make_async_remote_copy(
            src_ref=plane_send.at[source],
            dst_ref=plane_recv.at[source],
            send_sem=plane_send_sem.at[offset],
            recv_sem=plane_recv_sem.at[source],
            device_id=plane_device(source),
            device_id_type=MESH,
        )
        arrival.wait_recv()
    for group in range(groups):
        total = plane_recv[group].astype(jnp.float32)
        for index in range(group + groups, peers, groups):
            total = total + plane_recv[index].astype(jnp.float32)
        out_ref[group] = total
    if hand:
        for copy in handed:
            copy.wait_send()
        for offset in range(1, reps):
            source = lax.rem(rep + reps - offset, reps)
            arrival = pltpu.make_async_remote_copy(
                src_ref=outgoing_ref.at[source],
                dst_ref=hand_buf.at[source],
                send_sem=hand_send.at[offset],
                recv_sem=hand_recv.at[source],
                device_id=(source, me, yy, dd),
                device_id_type=MESH,
            )
            arrival.wait_recv()
        total = hand_buf[0].astype(jnp.float32)
        for index in range(1, reps):
            total = total + hand_buf[index].astype(jnp.float32)
        decode_ref[...] = total.astype(decode_ref.dtype)


def ring_reduce_scatter(rows, weight, n, peers, plane, call_id, whole=False, outgoing=None):
    half = rows.shape[0] // (2 * n)
    width = weight.shape[1]
    groups = 2 if len(plane) == 2 else 1
    per_peer = 2 * half // peers
    hand = outgoing is not None
    operands = (rows, weight) + ((outgoing,) if hand else ())
    out_shape = jax.ShapeDtypeStruct((groups, per_peer, width), jnp.float32)
    if hand:
        out_shape = (out_shape, jax.ShapeDtypeStruct(outgoing.shape[1:], outgoing.dtype))
    return pl.pallas_call(
        functools.partial(_ring_kernel, whole, plane, hand),
        out_shape=out_shape,
        in_specs=[pl.BlockSpec(memory_space=pltpu.VMEM)] * len(operands),
        out_specs=(
            (pl.BlockSpec(memory_space=pltpu.VMEM),) * 2 if hand else pl.BlockSpec(memory_space=pltpu.VMEM)
        ),
        scratch_shapes=[
            pltpu.VMEM((2, n - 1, half, width), jnp.bfloat16),
            pltpu.VMEM((2, n - 1, half, width), jnp.bfloat16),
            pltpu.SemaphoreType.DMA((2, n - 1)),
            pltpu.SemaphoreType.DMA((2, n - 1)),
            pltpu.VMEM((2 * half, width), jnp.float32),
            pltpu.VMEM((peers, per_peer, width), jnp.bfloat16),
            pltpu.VMEM((peers, per_peer, width), jnp.bfloat16),
            pltpu.SemaphoreType.DMA((peers,)),
            pltpu.SemaphoreType.DMA((peers,)),
        ]
        + (
            [
                pltpu.VMEM(outgoing.shape, outgoing.dtype),
                pltpu.SemaphoreType.DMA((outgoing.shape[0],)),
                pltpu.SemaphoreType.DMA((outgoing.shape[0],)),
            ]
            if hand
            else []
        )
        + ([pltpu.VMEM((rows.shape[0], width), jnp.float32)] if whole else []),
        compiler_params=pltpu.CompilerParams(collective_id=call_id, has_side_effects=True),
    )(*operands)


def _pages_kernel(pages_ref, out_ref, arrived, z_send, z_recv, p_send, p_recv):
    nz = pages_ref.shape[0]
    peers = out_ref.shape[1]
    groups = lax.axis_size("dec")
    mz = lax.axis_index("z")
    rep = lax.axis_index("rep")
    yy = lax.axis_index("y")
    dd = lax.axis_index("dec")
    mp = yy * groups + dd

    def z_device(index):
        return (rep, index, yy, dd)

    def plane_device(index):
        return (rep, mz, index // groups, lax.rem(index, groups))

    barrier = pltpu.get_barrier_semaphore()
    for offset in range(1, nz):
        pl.semaphore_signal(barrier, inc=1, device_id=z_device(lax.rem(mz + offset, nz)),
                            device_id_type=MESH)
    for offset in range(1, peers):
        pl.semaphore_signal(barrier, inc=1, device_id=plane_device(lax.rem(mp + offset, peers)),
                            device_id_type=MESH)
    pl.semaphore_wait(barrier, nz - 1 + peers - 1)
    z_copies = []
    for offset in range(1, nz):
        target = lax.rem(mz + offset, nz)
        copy = pltpu.make_async_remote_copy(
            src_ref=pages_ref.at[target],
            dst_ref=arrived.at[mz],
            send_sem=z_send.at[offset],
            recv_sem=z_recv.at[mz],
            device_id=z_device(target),
            device_id_type=MESH,
        )
        copy.start()
        z_copies.append(copy)
    forwards = []

    def forward(source, page_ref):
        for offset in range(1, peers):
            target = lax.rem(mp + offset, peers)
            copy = pltpu.make_async_remote_copy(
                src_ref=page_ref,
                dst_ref=out_ref.at[source, mp],
                send_sem=p_send.at[source, offset],
                recv_sem=p_recv.at[source, mp],
                device_id=plane_device(target),
                device_id_type=MESH,
            )
            copy.start()
            forwards.append(copy)
        out_ref[source, mp] = page_ref[...]

    forward(mz, pages_ref.at[mz])
    order = []
    for distance in range(1, nz // 2 + 1):
        for offset in (nz - distance, distance):
            if offset not in order:
                order.append(offset)
    for offset in order:
        source = lax.rem(mz + offset, nz)
        arrival = pltpu.make_async_remote_copy(
            src_ref=pages_ref.at[source],
            dst_ref=arrived.at[source],
            send_sem=z_send.at[offset],
            recv_sem=z_recv.at[source],
            device_id=z_device(source),
            device_id_type=MESH,
        )
        arrival.wait_recv()
        forward(source, arrived.at[source])
    for copy in z_copies:
        copy.wait_send()
    for copy in forwards:
        copy.wait_send()
    for source in range(nz):
        for offset in range(1, peers):
            sender = lax.rem(mp + peers - offset, peers)
            arrival = pltpu.make_async_remote_copy(
                src_ref=pages_ref.at[source],
                dst_ref=out_ref.at[source, sender],
                send_sem=p_send.at[source, offset],
                recv_sem=p_recv.at[source, sender],
                device_id=plane_device(sender),
                device_id_type=MESH,
            )
            arrival.wait_recv()


def exchange_pages(pages, peers):
    nz = pages.shape[0]
    block = pages.shape[1:]
    return pl.pallas_call(
        _pages_kernel,
        out_shape=jax.ShapeDtypeStruct((nz, peers) + block, pages.dtype),
        in_specs=[pl.BlockSpec(memory_space=pltpu.VMEM)],
        out_specs=pl.BlockSpec(memory_space=pltpu.VMEM),
        scratch_shapes=[
            pltpu.VMEM((nz,) + block, pages.dtype),
            pltpu.SemaphoreType.DMA((nz,)),
            pltpu.SemaphoreType.DMA((nz,)),
            pltpu.SemaphoreType.DMA((nz, peers)),
            pltpu.SemaphoreType.DMA((nz, peers)),
        ],
        compiler_params=pltpu.CompilerParams(collective_id=2, has_side_effects=True),
    )(pages)


def _rows_kernel(rows_ref, out_ref, plane_rows, p_send, p_recv, send_sem, recv_sem):
    nz = out_ref.shape[0]
    peers = plane_rows.shape[0]
    each = plane_rows.shape[1]
    part = out_ref.shape[1] // 2
    groups = lax.axis_size("dec")
    mz = lax.axis_index("z")
    rep = lax.axis_index("rep")
    yy = lax.axis_index("y")
    dd = lax.axis_index("dec")
    mp = yy * groups + dd
    right = lax.rem(mz + 1, nz)
    left = lax.rem(mz + nz - 1, nz)

    def plane_device(index):
        return (rep, mz, index // groups, lax.rem(index, groups))

    barrier = pltpu.get_barrier_semaphore()
    for neighbour in (left, right):
        pl.semaphore_signal(barrier, inc=1, device_id=(rep, neighbour, yy, dd), device_id_type=MESH)
    for offset in range(1, peers):
        pl.semaphore_signal(barrier, inc=1, device_id=plane_device(lax.rem(mp + offset, peers)),
                            device_id_type=MESH)
    pl.semaphore_wait(barrier, 2 + peers - 1)
    sent = []
    for offset in range(1, peers):
        target = lax.rem(mp + offset, peers)
        copy = pltpu.make_async_remote_copy(
            src_ref=rows_ref.at[lax.rem(target, groups)],
            dst_ref=plane_rows.at[mp],
            send_sem=p_send.at[offset],
            recv_sem=p_recv.at[mp],
            device_id=plane_device(target),
            device_id_type=MESH,
        )
        copy.start()
        sent.append(copy)
    plane_rows[mp] = rows_ref[dd]
    for copy in sent:
        copy.wait_send()
    for offset in range(1, peers):
        sender = lax.rem(mp + peers - offset, peers)
        arrival = pltpu.make_async_remote_copy(
            src_ref=rows_ref.at[0],
            dst_ref=plane_rows.at[sender],
            send_sem=p_send.at[offset],
            recv_sem=p_recv.at[sender],
            device_id=plane_device(sender),
            device_id_type=MESH,
        )
        arrival.wait_recv()
    for index in range(peers):
        out_ref[mz, pl.ds(index * each, each), :] = plane_rows[index]
    for step in range(nz - 1):
        copies = []
        for way in range(2):
            if way == 0:
                target, source = right, lax.rem(mz + nz - step, nz)
            else:
                target, source = left, lax.rem(mz + step, nz)
            src = out_ref.at[source, pl.ds(way * part, part)]
            copy = pltpu.make_async_remote_copy(
                src_ref=src,
                dst_ref=out_ref.at[source, pl.ds(way * part, part)],
                send_sem=send_sem.at[way, step],
                recv_sem=recv_sem.at[way, step],
                device_id=(rep, target, yy, dd),
                device_id_type=MESH,
            )
            copy.start()
            copies.append(copy)
        for copy in copies:
            copy.wait()


def gather_rows(rows, nz, peers):
    block = rows.shape[1:]
    return pl.pallas_call(
        _rows_kernel,
        out_shape=jax.ShapeDtypeStruct((nz, peers * block[0], block[1]), rows.dtype),
        in_specs=[pl.BlockSpec(memory_space=pltpu.VMEM)],
        out_specs=pl.BlockSpec(memory_space=pltpu.VMEM),
        scratch_shapes=[
            pltpu.VMEM((peers,) + block, rows.dtype),
            pltpu.SemaphoreType.DMA((peers,)),
            pltpu.SemaphoreType.DMA((peers,)),
            pltpu.SemaphoreType.DMA((2, nz - 1)),
            pltpu.SemaphoreType.DMA((2, nz - 1)),
        ],
        compiler_params=pltpu.CompilerParams(collective_id=3, has_side_effects=True),
    )(rows)


def hand_over(kv_pool, page_target):
    rep_size = lax.axis_size("rep")
    owners = jnp.arange(rep_size, dtype=jnp.int32)
    selected = (page_target[None, :] == owners[:, None])[:, :, None, None, None]
    outgoing = jnp.where(selected, kv_pool[None], jnp.zeros((), kv_pool.dtype))
    incoming = lax.all_to_all(outgoing, "rep", split_axis=0, concat_axis=0, tiled=True)
    return jnp.sum(incoming, axis=0)


def on_device(
    residual,
    queries,
    kv_pool,
    prior_len,
    page_table,
    page_target,
    out_weight,
    moe_gain,
    expert_ids,
    expert_gates,
    w_gate,
    w_up,
    w_down,
):
    tp_size = lax.axis_size("z") * lax.axis_size("y")
    dec_size = lax.axis_size("dec")
    dec_index = lax.axis_index("dec")
    slots_dev, kv_heads, page_rows, both_dim = kv_pool.shape
    head_dim = both_dim // 2
    heads_dev = queries.shape[3] // head_dim
    group_size = QH // KVH
    kv_dev = max(1, heads_dev // group_size)
    copies = max(1, group_size // heads_dev)
    per_kv = heads_dev // kv_dev
    requests = prior_len.shape[0]
    tok_dev = queries.shape[2]
    half_rows = queries.shape[0] * tok_dev // requests
    pages_max = page_table.shape[1]
    team_size = tp_size * dec_size
    z_size = lax.axis_size("z")
    plane_size = team_size // z_size
    received = exchange_pages(kv_pool.reshape(z_size * kv_dev, page_rows, both_dim), plane_size)
    received = received.reshape(team_size * slots_dev, kv_dev, page_rows, both_dim)
    gathered_pages = received[page_table % (team_size * slots_dev)]
    keys_part = gathered_pages[..., :head_dim]
    values_part = gathered_pages[..., head_dim:]
    query_rows = queries.reshape(requests, half_rows, kv_dev, per_kv, head_dim)
    key_count = pages_max * page_rows
    scores = jnp.einsum(
        "rukgd,rpkwd->rukgpw", query_rows, keys_part, preferred_element_type=jnp.float32
    )
    scores = scores.reshape(requests, half_rows, kv_dev, per_kv, key_count) * head_dim ** (-0.5)
    position = jnp.arange(key_count, dtype=jnp.int32)
    local_row = jnp.arange(half_rows, dtype=jnp.int32)
    offset = (local_row // tok_dev * dec_size + dec_index) * tok_dev + local_row % tok_dev
    last_seen = prior_len[:, None] + offset[None, :]
    visible = (position[None, None, :] <= last_seen[:, :, None])[:, :, None, None, :]
    scores = jnp.where(visible, scores, -1e30)
    row_top = jnp.max(scores, axis=-1, keepdims=True)
    raw_weights = jnp.where(visible, jnp.exp(scores - row_top), 0.0)
    totals = jnp.sum(raw_weights, axis=-1)
    weights_low = raw_weights.astype(jnp.bfloat16).reshape(
        requests, half_rows, kv_dev, per_kv, pages_max, page_rows
    )
    weighted = jnp.einsum(
        "rukgpw,rpkwd->rukgd", weights_low, values_part, preferred_element_type=jnp.float32
    )
    attended = (
        (weighted / totals[..., None])
        .astype(jnp.bfloat16)
        .reshape(requests * half_rows, heads_dev * head_dim)
    )
    y_size = lax.axis_size("y")
    width = out_weight.shape[1]
    rep_size = lax.axis_size("rep")
    owners = jnp.arange(rep_size, dtype=jnp.int32)
    chosen = (page_target[None, :] == owners[:, None])[:, :, None, None, None]
    outgoing = jnp.where(chosen, kv_pool[None], jnp.zeros((), kv_pool.dtype))
    outgoing = outgoing.reshape((rep_size,) + kv_pool.shape[1:])
    projected, handed = ring_reduce_scatter(
        attended, out_weight, z_size, y_size, ("y",), 0, outgoing=outgoing
    )
    projected = projected[0]
    decode_pages = handed.reshape(kv_pool.shape)
    mid_state = residual.astype(jnp.float32) + projected
    routed_dev = tok_dev * TOPK // EXPERTS
    row_lists = []
    gate_lists = []
    for expert in range(EXP_WIN):
        names_it = expert_ids == expert
        chosen_rows = jnp.nonzero(jnp.any(names_it, axis=-1), size=routed_dev)[0].astype(jnp.int32)
        row_lists.append(chosen_rows)
        gate_lists.append(jnp.sum(jnp.where(names_it, expert_gates, 0.0), axis=-1)[chosen_rows])
    picked_rows = jnp.stack(row_lists, axis=0)
    picked_gates = jnp.stack(gate_lists, axis=0)
    inverse = lax.rsqrt(jnp.mean(mid_state * mid_state, axis=-1, keepdims=True) + 1e-05)
    normed_all = (mid_state * inverse * moe_gain).astype(jnp.bfloat16)
    width = normed_all.shape[1]
    by_expert = normed_all[picked_rows]
    row_piece = gather_rows(by_expert, z_size, plane_size)
    row_piece = row_piece.reshape(team_size * routed_dev, width)
    gate_part = jnp.dot(row_piece, w_gate[0].T, preferred_element_type=jnp.float32)
    up_part = jnp.dot(row_piece, w_up[0].T, preferred_element_type=jnp.float32)
    hidden = (jax.nn.silu(gate_part) * up_part).astype(jnp.bfloat16)
    expert_out = ring_reduce_scatter(
        hidden, w_down[0], z_size, y_size * dec_size, ("y", "dec"), 1, whole=True
    )
    mixture = jnp.zeros_like(mid_state)
    for expert in range(EXP_WIN):
        mixture = mixture.at[picked_rows[expert]].add(
            expert_out[expert] * picked_gates[expert][:, None]
        )
    layer_out = (mid_state + mixture).astype(jnp.bfloat16)
    return (layer_out, decode_pages)


def fine_mesh(mesh):
    tp_devices = mesh.devices[0, :, 0]
    y_size = len({device.coords[1] for device in tp_devices})
    shape = (mesh.shape["rep"], mesh.shape["tp"] // y_size, y_size, mesh.shape["dec"])
    return jax.sharding.Mesh(mesh.devices.reshape(shape), ("rep", "z", "y", "dec"))


def solution(mesh):
    team = ("rep", "z", "y", "dec")
    return jax.shard_map(
        on_device,
        mesh=fine_mesh(mesh),
        in_specs=(
            P(team, None),
            P("rep", "dec", None, ("z", "y")),
            P(team, None, None, None),
            P("rep"),
            P("rep", None),
            P(team),
            P(("z", "y"), None),
            P(),
            P(team, None),
            P(team, None),
            P("dec", ("z", "y"), None),
            P("dec", ("z", "y"), None),
            P("dec", ("z", "y"), None),
        ),
        out_specs=(P(team, None), P(team, None, None, None)),
        check_vma=False,
    )
```

```python
import functools

import jax
import jax.numpy as jnp
from jax import lax
from jax.sharding import PartitionSpec as P
from jax.experimental import pallas as pl
from jax.experimental.pallas import tpu as pltpu

QH = 32
KVH = 8
EXPERTS = 8
TOPK = 2
EXP_WIN = 2


MESH = pl.DeviceIdType.MESH

def _ring_kernel(whole, plane, hand, *refs):
    if hand:
        rows_ref, weight_ref, outgoing_ref, out_ref, decode_ref = refs[:5]
        rest = refs[5:]
    else:
        rows_ref, weight_ref, out_ref = refs[:3]
        rest = refs[3:]
    (recv_buf, send_buf, send_sem, recv_sem, ring_out, plane_send, plane_recv,
     plane_send_sem, plane_recv_sem) = rest[:9]
    rest = rest[9:]
    if hand:
        hand_buf, hand_send, hand_recv = rest[:3]
        rest = rest[3:]
    product = rest
    n = recv_buf.shape[1] + 1
    half = recv_buf.shape[2]
    peers = plane_send.shape[0]
    groups = out_ref.shape[0]
    per_peer = plane_send.shape[1]
    me = lax.axis_index("z")
    rep = lax.axis_index("rep")
    yy = lax.axis_index("y")
    dd = lax.axis_index("dec")
    right = lax.rem(me + 1, n)
    left = lax.rem(me + n - 1, n)
    if len(plane) == 2:
        me_plane = yy * groups + dd

        def plane_device(index):
            return (rep, me, index // groups, lax.rem(index, groups))
    else:
        me_plane = yy

        def plane_device(index):
            return (rep, me, index, dd)

    if whole:
        product[0][...] = jnp.dot(rows_ref[...], weight_ref[...], preferred_element_type=jnp.float32)

    def block_part(block, way):
        start = pl.multiple_of(block * (2 * half) + way * half, half)
        if whole:
            return product[0][pl.ds(start, half), :]
        piece = rows_ref[pl.ds(start, half), :]
        return jnp.dot(piece, weight_ref[...], preferred_element_type=jnp.float32)

    barrier = pltpu.get_barrier_semaphore()
    for neighbour in (left, right):
        pl.semaphore_signal(barrier, inc=1, device_id=(rep, neighbour, yy, dd), device_id_type=MESH)
    for offset in range(1, peers):
        target = lax.rem(me_plane + offset, peers)
        pl.semaphore_signal(barrier, inc=1, device_id=plane_device(target), device_id_type=MESH)
    reps = lax.axis_size("rep")
    if hand:
        for offset in range(1, reps):
            pl.semaphore_signal(barrier, inc=1, device_id=(lax.rem(rep + offset, reps), me, yy, dd),
                                device_id_type=MESH)
    pl.semaphore_wait(barrier, 2 + peers - 1 + (reps - 1 if hand else 0))
    handed = []
    if hand:
        for offset in range(1, reps):
            target = lax.rem(rep + offset, reps)
            copy = pltpu.make_async_remote_copy(
                src_ref=outgoing_ref.at[target],
                dst_ref=hand_buf.at[rep],
                send_sem=hand_send.at[offset],
                recv_sem=hand_recv.at[rep],
                device_id=(target, me, yy, dd),
                device_id_type=MESH,
            )
            copy.start()
            handed.append(copy)
        hand_buf[rep] = outgoing_ref[rep]
    for way in range(2):
        if way == 0:
            block = lax.rem(me + n - 1, n)
        else:
            block = lax.rem(me + 1, n)
        send_buf[way, 0] = block_part(block, way).astype(send_buf.dtype)
    for step in range(n - 1):
        copies = []
        for way in range(2):
            target = right if way == 0 else left
            copy = pltpu.make_async_remote_copy(
                src_ref=send_buf.at[way, step],
                dst_ref=recv_buf.at[way, step],
                send_sem=send_sem.at[way, step],
                recv_sem=recv_sem.at[way, step],
                device_id=(rep, target, yy, dd),
                device_id_type=MESH,
            )
            copy.start()
            copies.append(copy)
        for way in range(2):
            if way == 0:
                block = lax.rem(me + 2 * n - 2 - step, n)
            else:
                block = lax.rem(me + 2 + step, n)
            own = block_part(block, way)
            copies[way].wait()
            total = recv_buf[way, step].astype(jnp.float32) + own
            if step < n - 2:
                send_buf[way, step + 1] = total.astype(send_buf.dtype)
            else:
                ring_out[pl.ds(way * half, half), :] = total
    for index in range(peers):
        plane_send[index] = ring_out[pl.ds(index * per_peer, per_peer), :].astype(plane_send.dtype)
    sent = []
    for offset in range(1, peers):
        target = lax.rem(me_plane + offset, peers)
        copy = pltpu.make_async_remote_copy(
            src_ref=plane_send.at[target],
            dst_ref=plane_recv.at[me_plane],
            send_sem=plane_send_sem.at[offset],
            recv_sem=plane_recv_sem.at[me_plane],
            device_id=plane_device(target),
            device_id_type=MESH,
        )
        copy.start()
        sent.append(copy)
    plane_recv[me_plane] = plane_send[me_plane]
    for copy in sent:
        copy.wait_send()
    for offset in range(1, peers):
        source = lax.rem(me_plane + peers - offset, peers)
        arrival = pltpu.make_async_remote_copy(
            src_ref=plane_send.at[source],
            dst_ref=plane_recv.at[source],
            send_sem=plane_send_sem.at[offset],
            recv_sem=plane_recv_sem.at[source],
            device_id=plane_device(source),
            device_id_type=MESH,
        )
        arrival.wait_recv()
    for group in range(groups):
        total = plane_recv[group].astype(jnp.float32)
        for index in range(group + groups, peers, groups):
            total = total + plane_recv[index].astype(jnp.float32)
        out_ref[group] = total
    if hand:
        for copy in handed:
            copy.wait_send()
        for offset in range(1, reps):
            source = lax.rem(rep + reps - offset, reps)
            arrival = pltpu.make_async_remote_copy(
                src_ref=outgoing_ref.at[source],
                dst_ref=hand_buf.at[source],
                send_sem=hand_send.at[offset],
                recv_sem=hand_recv.at[source],
                device_id=(source, me, yy, dd),
                device_id_type=MESH,
            )
            arrival.wait_recv()
        total = hand_buf[0].astype(jnp.float32)
        for index in range(1, reps):
            total = total + hand_buf[index].astype(jnp.float32)
        decode_ref[...] = total.astype(decode_ref.dtype)


def ring_reduce_scatter(rows, weight, n, peers, plane, call_id, whole=False, outgoing=None):
    half = rows.shape[0] // (2 * n)
    width = weight.shape[1]
    groups = 2 if len(plane) == 2 else 1
    per_peer = 2 * half // peers
    hand = outgoing is not None
    operands = (rows, weight) + ((outgoing,) if hand else ())
    out_shape = jax.ShapeDtypeStruct((groups, per_peer, width), jnp.float32)
    if hand:
        out_shape = (out_shape, jax.ShapeDtypeStruct(outgoing.shape[1:], outgoing.dtype))
    return pl.pallas_call(
        functools.partial(_ring_kernel, whole, plane, hand),
        out_shape=out_shape,
        in_specs=[pl.BlockSpec(memory_space=pltpu.VMEM)] * len(operands),
        out_specs=(
            (pl.BlockSpec(memory_space=pltpu.VMEM),) * 2 if hand else pl.BlockSpec(memory_space=pltpu.VMEM)
        ),
        scratch_shapes=[
            pltpu.VMEM((2, n - 1, half, width), jnp.bfloat16),
            pltpu.VMEM((2, n - 1, half, width), jnp.bfloat16),
            pltpu.SemaphoreType.DMA((2, n - 1)),
            pltpu.SemaphoreType.DMA((2, n - 1)),
            pltpu.VMEM((2 * half, width), jnp.float32),
            pltpu.VMEM((peers, per_peer, width), jnp.bfloat16),
            pltpu.VMEM((peers, per_peer, width), jnp.bfloat16),
            pltpu.SemaphoreType.DMA((peers,)),
            pltpu.SemaphoreType.DMA((peers,)),
        ]
        + (
            [
                pltpu.VMEM(outgoing.shape, outgoing.dtype),
                pltpu.SemaphoreType.DMA((outgoing.shape[0],)),
                pltpu.SemaphoreType.DMA((outgoing.shape[0],)),
            ]
            if hand
            else []
        )
        + ([pltpu.VMEM((rows.shape[0], width), jnp.float32)] if whole else []),
        compiler_params=pltpu.CompilerParams(collective_id=call_id, has_side_effects=True),
    )(*operands)


def _pages_kernel(pages_ref, out_ref, arrived, z_send, z_recv, p_send, p_recv):
    nz = pages_ref.shape[0]
    peers = out_ref.shape[1]
    groups = lax.axis_size("dec")
    mz = lax.axis_index("z")
    rep = lax.axis_index("rep")
    yy = lax.axis_index("y")
    dd = lax.axis_index("dec")
    mp = yy * groups + dd

    def z_device(index):
        return (rep, index, yy, dd)

    def plane_device(index):
        return (rep, mz, index // groups, lax.rem(index, groups))

    barrier = pltpu.get_barrier_semaphore()
    for offset in range(1, nz):
        pl.semaphore_signal(barrier, inc=1, device_id=z_device(lax.rem(mz + offset, nz)),
                            device_id_type=MESH)
    for offset in range(1, peers):
        pl.semaphore_signal(barrier, inc=1, device_id=plane_device(lax.rem(mp + offset, peers)),
                            device_id_type=MESH)
    pl.semaphore_wait(barrier, nz - 1 + peers - 1)
    z_copies = []
    for offset in range(1, nz):
        target = lax.rem(mz + offset, nz)
        copy = pltpu.make_async_remote_copy(
            src_ref=pages_ref.at[target],
            dst_ref=arrived.at[mz],
            send_sem=z_send.at[offset],
            recv_sem=z_recv.at[mz],
            device_id=z_device(target),
            device_id_type=MESH,
        )
        copy.start()
        z_copies.append(copy)
    forwards = []

    def forward(source, page_ref):
        for offset in range(1, peers):
            target = lax.rem(mp + offset, peers)
            copy = pltpu.make_async_remote_copy(
                src_ref=page_ref,
                dst_ref=out_ref.at[source, mp],
                send_sem=p_send.at[source, offset],
                recv_sem=p_recv.at[source, mp],
                device_id=plane_device(target),
                device_id_type=MESH,
            )
            copy.start()
            forwards.append(copy)
        out_ref[source, mp] = page_ref[...]

    forward(mz, pages_ref.at[mz])
    order = []
    for distance in range(1, nz // 2 + 1):
        for offset in (nz - distance, distance):
            if offset not in order:
                order.append(offset)
    for offset in order:
        source = lax.rem(mz + offset, nz)
        arrival = pltpu.make_async_remote_copy(
            src_ref=pages_ref.at[source],
            dst_ref=arrived.at[source],
            send_sem=z_send.at[offset],
            recv_sem=z_recv.at[source],
            device_id=z_device(source),
            device_id_type=MESH,
        )
        arrival.wait_recv()
        forward(source, arrived.at[source])
    for copy in z_copies:
        copy.wait_send()
    for copy in forwards:
        copy.wait_send()
    for source in range(nz):
        for offset in range(1, peers):
            sender = lax.rem(mp + peers - offset, peers)
            arrival = pltpu.make_async_remote_copy(
                src_ref=pages_ref.at[source],
                dst_ref=out_ref.at[source, sender],
                send_sem=p_send.at[source, offset],
                recv_sem=p_recv.at[source, sender],
                device_id=plane_device(sender),
                device_id_type=MESH,
            )
            arrival.wait_recv()


def exchange_pages(pages, peers):
    nz = pages.shape[0]
    block = pages.shape[1:]
    return pl.pallas_call(
        _pages_kernel,
        out_shape=jax.ShapeDtypeStruct((nz, peers) + block, pages.dtype),
        in_specs=[pl.BlockSpec(memory_space=pltpu.VMEM)],
        out_specs=pl.BlockSpec(memory_space=pltpu.VMEM),
        scratch_shapes=[
            pltpu.VMEM((nz,) + block, pages.dtype),
            pltpu.SemaphoreType.DMA((nz,)),
            pltpu.SemaphoreType.DMA((nz,)),
            pltpu.SemaphoreType.DMA((nz, peers)),
            pltpu.SemaphoreType.DMA((nz, peers)),
        ],
        compiler_params=pltpu.CompilerParams(collective_id=2, has_side_effects=True),
    )(pages)


def _rows_kernel(rows_ref, out_ref, plane_rows, p_send, p_recv, send_sem, recv_sem):
    nz = out_ref.shape[0]
    peers = plane_rows.shape[0]
    each = plane_rows.shape[1]
    part = out_ref.shape[1] // 2
    groups = lax.axis_size("dec")
    mz = lax.axis_index("z")
    rep = lax.axis_index("rep")
    yy = lax.axis_index("y")
    dd = lax.axis_index("dec")
    mp = yy * groups + dd
    right = lax.rem(mz + 1, nz)
    left = lax.rem(mz + nz - 1, nz)

    def plane_device(index):
        return (rep, mz, index // groups, lax.rem(index, groups))

    barrier = pltpu.get_barrier_semaphore()
    for neighbour in (left, right):
        pl.semaphore_signal(barrier, inc=1, device_id=(rep, neighbour, yy, dd), device_id_type=MESH)
    for offset in range(1, peers):
        pl.semaphore_signal(barrier, inc=1, device_id=plane_device(lax.rem(mp + offset, peers)),
                            device_id_type=MESH)
    pl.semaphore_wait(barrier, 2 + peers - 1)
    sent = []
    for offset in range(1, peers):
        target = lax.rem(mp + offset, peers)
        copy = pltpu.make_async_remote_copy(
            src_ref=rows_ref.at[lax.rem(target, groups)],
            dst_ref=plane_rows.at[mp],
            send_sem=p_send.at[offset],
            recv_sem=p_recv.at[mp],
            device_id=plane_device(target),
            device_id_type=MESH,
        )
        copy.start()
        sent.append(copy)
    plane_rows[mp] = rows_ref[dd]
    for copy in sent:
        copy.wait_send()
    for offset in range(1, peers):
        sender = lax.rem(mp + peers - offset, peers)
        arrival = pltpu.make_async_remote_copy(
            src_ref=rows_ref.at[0],
            dst_ref=plane_rows.at[sender],
            send_sem=p_send.at[offset],
            recv_sem=p_recv.at[sender],
            device_id=plane_device(sender),
            device_id_type=MESH,
        )
        arrival.wait_recv()
    for index in range(peers):
        out_ref[mz, pl.ds(index * each, each), :] = plane_rows[index]
    for step in range(nz - 1):
        copies = []
        for way in range(2):
            if way == 0:
                target, source = right, lax.rem(mz + nz - step, nz)
            else:
                target, source = left, lax.rem(mz + step, nz)
            src = out_ref.at[source, pl.ds(way * part, part)]
            copy = pltpu.make_async_remote_copy(
                src_ref=src,
                dst_ref=out_ref.at[source, pl.ds(way * part, part)],
                send_sem=send_sem.at[way, step],
                recv_sem=recv_sem.at[way, step],
                device_id=(rep, target, yy, dd),
                device_id_type=MESH,
            )
            copy.start()
            copies.append(copy)
        for copy in copies:
            copy.wait()


def gather_rows(rows, nz, peers):
    block = rows.shape[1:]
    return pl.pallas_call(
        _rows_kernel,
        out_shape=jax.ShapeDtypeStruct((nz, peers * block[0], block[1]), rows.dtype),
        in_specs=[pl.BlockSpec(memory_space=pltpu.VMEM)],
        out_specs=pl.BlockSpec(memory_space=pltpu.VMEM),
        scratch_shapes=[
            pltpu.VMEM((peers,) + block, rows.dtype),
            pltpu.SemaphoreType.DMA((peers,)),
            pltpu.SemaphoreType.DMA((peers,)),
            pltpu.SemaphoreType.DMA((2, nz - 1)),
            pltpu.SemaphoreType.DMA((2, nz - 1)),
        ],
        compiler_params=pltpu.CompilerParams(collective_id=3, has_side_effects=True),
    )(rows)


def hand_over(kv_pool, page_target):
    rep_size = lax.axis_size("rep")
    owners = jnp.arange(rep_size, dtype=jnp.int32)
    selected = (page_target[None, :] == owners[:, None])[:, :, None, None, None]
    outgoing = jnp.where(selected, kv_pool[None], jnp.zeros((), kv_pool.dtype))
    incoming = lax.all_to_all(outgoing, "rep", split_axis=0, concat_axis=0, tiled=True)
    return jnp.sum(incoming, axis=0)


def on_device(
    residual,
    queries,
    kv_pool,
    prior_len,
    page_table,
    page_target,
    out_weight,
    moe_gain,
    expert_ids,
    expert_gates,
    w_gate,
    w_up,
    w_down,
):
    tp_size = lax.axis_size("z") * lax.axis_size("y")
    dec_size = lax.axis_size("dec")
    dec_index = lax.axis_index("dec")
    slots_dev, kv_heads, page_rows, both_dim = kv_pool.shape
    head_dim = both_dim // 2
    heads_dev = queries.shape[3] // head_dim
    group_size = QH // KVH
    kv_dev = max(1, heads_dev // group_size)
    copies = max(1, group_size // heads_dev)
    per_kv = heads_dev // kv_dev
    requests = prior_len.shape[0]
    tok_dev = queries.shape[2]
    half_rows = queries.shape[0] * tok_dev // requests
    pages_max = page_table.shape[1]
    team_size = tp_size * dec_size
    z_size = lax.axis_size("z")
    plane_size = team_size // z_size
    received = exchange_pages(kv_pool.reshape(z_size * kv_dev, page_rows, both_dim), plane_size)
    received = received.reshape(team_size * slots_dev, kv_dev, page_rows, both_dim)
    gathered_pages = received[page_table % (team_size * slots_dev)]
    keys_part = gathered_pages[..., :head_dim]
    values_part = gathered_pages[..., head_dim:]
    query_rows = queries.reshape(requests, half_rows, kv_dev, per_kv, head_dim)
    key_count = pages_max * page_rows
    scores = jnp.einsum(
        "rukgd,rpkwd->rukgpw", query_rows, keys_part, preferred_element_type=jnp.float32
    )
    scores = scores.reshape(requests, half_rows, kv_dev, per_kv, key_count) * head_dim ** (-0.5)
    position = jnp.arange(key_count, dtype=jnp.int32)
    local_row = jnp.arange(half_rows, dtype=jnp.int32)
    offset = (local_row // tok_dev * dec_size + dec_index) * tok_dev + local_row % tok_dev
    last_seen = prior_len[:, None] + offset[None, :]
    visible = (position[None, None, :] <= last_seen[:, :, None])[:, :, None, None, :]
    scores = jnp.where(visible, scores, -1e30)
    row_top = jnp.max(scores, axis=-1, keepdims=True)
    raw_weights = jnp.where(visible, jnp.exp(scores - row_top), 0.0)
    totals = jnp.sum(raw_weights, axis=-1)
    weights_low = raw_weights.astype(jnp.bfloat16).reshape(
        requests, half_rows, kv_dev, per_kv, pages_max, page_rows
    )
    weighted = jnp.einsum(
        "rukgpw,rpkwd->rukgd", weights_low, values_part, preferred_element_type=jnp.float32
    )
    attended = (
        (weighted / totals[..., None])
        .astype(jnp.bfloat16)
        .reshape(requests * half_rows, heads_dev * head_dim)
    )
    y_size = lax.axis_size("y")
    width = out_weight.shape[1]
    rep_size = lax.axis_size("rep")
    owners = jnp.arange(rep_size, dtype=jnp.int32)
    chosen = (page_target[None, :] == owners[:, None])[:, :, None, None, None]
    outgoing = jnp.where(chosen, kv_pool[None], jnp.zeros((), kv_pool.dtype))
    outgoing = outgoing.reshape((rep_size,) + kv_pool.shape[1:])
    projected, handed = ring_reduce_scatter(
        attended, out_weight, z_size, y_size, ("y",), 0, outgoing=outgoing
    )
    projected = projected[0]
    decode_pages = handed.reshape(kv_pool.shape)
    mid_state = residual.astype(jnp.float32) + projected
    routed_dev = tok_dev * TOPK // EXPERTS
    token_index = jnp.arange(tok_dev, dtype=jnp.int32)
    names_it = expert_ids[None, :, :] == jnp.arange(EXP_WIN, dtype=jnp.int32)[:, None, None]
    named = jnp.any(names_it, axis=-1)
    rank = jnp.cumsum(named.astype(jnp.int32), axis=1) - 1
    slot_hit = named[:, None, :] & (rank[:, None, :] == jnp.arange(routed_dev, dtype=jnp.int32)[None, :, None])
    picked_rows = jnp.sum(jnp.where(slot_hit, token_index, 0), axis=-1)
    gate_sum = jnp.sum(jnp.where(names_it, expert_gates[None], 0.0), axis=-1)
    picked_gates = jnp.sum(jnp.where(slot_hit, gate_sum[:, None, :], 0.0), axis=-1)
    inverse = lax.rsqrt(jnp.mean(mid_state * mid_state, axis=-1, keepdims=True) + 1e-05)
    normed_all = (mid_state * inverse * moe_gain).astype(jnp.bfloat16)
    width = normed_all.shape[1]
    by_expert = normed_all[picked_rows]
    row_piece = gather_rows(by_expert, z_size, plane_size)
    row_piece = row_piece.reshape(team_size * routed_dev, width)
    gate_part = jnp.dot(row_piece, w_gate[0].T, preferred_element_type=jnp.float32)
    up_part = jnp.dot(row_piece, w_up[0].T, preferred_element_type=jnp.float32)
    hidden = (jax.nn.silu(gate_part) * up_part).astype(jnp.bfloat16)
    expert_out = ring_reduce_scatter(
        hidden, w_down[0], z_size, y_size * dec_size, ("y", "dec"), 1, whole=True
    )
    one_hot = slot_hit.astype(jnp.float32)
    mixture = jnp.einsum(
        "eki,ekd->id", one_hot, expert_out * picked_gates[..., None], precision=lax.Precision.HIGHEST
    )
    layer_out = (mid_state + mixture).astype(jnp.bfloat16)
    return (layer_out, decode_pages)


def fine_mesh(mesh):
    tp_devices = mesh.devices[0, :, 0]
    y_size = len({device.coords[1] for device in tp_devices})
    shape = (mesh.shape["rep"], mesh.shape["tp"] // y_size, y_size, mesh.shape["dec"])
    return jax.sharding.Mesh(mesh.devices.reshape(shape), ("rep", "z", "y", "dec"))


def solution(mesh):
    team = ("rep", "z", "y", "dec")
    return jax.shard_map(
        on_device,
        mesh=fine_mesh(mesh),
        in_specs=(
            P(team, None),
            P("rep", "dec", None, ("z", "y")),
            P(team, None, None, None),
            P("rep"),
            P("rep", None),
            P(team),
            P(("z", "y"), None),
            P(),
            P(team, None),
            P(team, None),
            P("dec", ("z", "y"), None),
            P("dec", ("z", "y"), None),
            P("dec", ("z", "y"), None),
        ),
        out_specs=(P(team, None), P(team, None, None, None)),
        check_vma=False,
    )
```

```python
import functools

import jax
import jax.numpy as jnp
from jax import lax
from jax.sharding import PartitionSpec as P
from jax.experimental import pallas as pl
from jax.experimental.pallas import tpu as pltpu

QH = 32
KVH = 8
EXPERTS = 8
TOPK = 2
EXP_WIN = 2


MESH = pl.DeviceIdType.MESH

def _ring_kernel(whole, plane, hand, *refs):
    count = 3 if whole else 1
    rows_ref = refs[0]
    weight_ref = refs[1] if count == 1 else refs[1:1 + count]
    refs = refs[1 + count:]
    if hand:
        outgoing_ref, out_ref, decode_ref = refs[:3]
        rest = refs[3:]
    else:
        out_ref = refs[0]
        rest = refs[1:]
    (recv_buf, send_buf, send_sem, recv_sem, ring_out, plane_send, plane_recv,
     plane_send_sem, plane_recv_sem) = rest[:9]
    rest = rest[9:]
    if hand:
        hand_buf, hand_send, hand_recv = rest[:3]
        rest = rest[3:]
    product = rest
    n = recv_buf.shape[1] + 1
    half = recv_buf.shape[2]
    peers = plane_send.shape[0]
    groups = out_ref.shape[0]
    per_peer = plane_send.shape[1]
    me = lax.axis_index("z")
    rep = lax.axis_index("rep")
    yy = lax.axis_index("y")
    dd = lax.axis_index("dec")
    right = lax.rem(me + 1, n)
    left = lax.rem(me + n - 1, n)
    if len(plane) == 2:
        me_plane = yy * groups + dd

        def plane_device(index):
            return (rep, me, index // groups, lax.rem(index, groups))
    else:
        me_plane = yy

        def plane_device(index):
            return (rep, me, index, dd)

    if whole:
        features = rows_ref[...]
        contract = (((1,), (1,)), ((), ()))
        gate = lax.dot_general(features, weight_ref[0][...], contract, preferred_element_type=jnp.float32)
        up = lax.dot_general(features, weight_ref[1][...], contract, preferred_element_type=jnp.float32)
        hidden = (gate / (1.0 + jnp.exp(-gate)) * up).astype(features.dtype)
        product[0][...] = jnp.dot(hidden, weight_ref[2][...], preferred_element_type=jnp.float32)

    def block_part(block, way):
        start = pl.multiple_of(block * (2 * half) + way * half, half)
        if whole:
            return product[0][pl.ds(start, half), :]
        piece = rows_ref[pl.ds(start, half), :]
        return jnp.dot(piece, weight_ref[...], preferred_element_type=jnp.float32)

    barrier = pltpu.get_barrier_semaphore()
    for neighbour in (left, right):
        pl.semaphore_signal(barrier, inc=1, device_id=(rep, neighbour, yy, dd), device_id_type=MESH)
    for offset in range(1, peers):
        target = lax.rem(me_plane + offset, peers)
        pl.semaphore_signal(barrier, inc=1, device_id=plane_device(target), device_id_type=MESH)
    reps = lax.axis_size("rep")
    if hand:
        for offset in range(1, reps):
            pl.semaphore_signal(barrier, inc=1, device_id=(lax.rem(rep + offset, reps), me, yy, dd),
                                device_id_type=MESH)
    pl.semaphore_wait(barrier, 2 + peers - 1 + (reps - 1 if hand else 0))
    handed = []
    if hand:
        for offset in range(1, reps):
            target = lax.rem(rep + offset, reps)
            copy = pltpu.make_async_remote_copy(
                src_ref=outgoing_ref.at[target],
                dst_ref=hand_buf.at[rep],
                send_sem=hand_send.at[offset],
                recv_sem=hand_recv.at[rep],
                device_id=(target, me, yy, dd),
                device_id_type=MESH,
            )
            copy.start()
            handed.append(copy)
        hand_buf[rep] = outgoing_ref[rep]
    for way in range(2):
        if way == 0:
            block = lax.rem(me + n - 1, n)
        else:
            block = lax.rem(me + 1, n)
        send_buf[way, 0] = block_part(block, way).astype(send_buf.dtype)
    for step in range(n - 1):
        copies = []
        for way in range(2):
            target = right if way == 0 else left
            copy = pltpu.make_async_remote_copy(
                src_ref=send_buf.at[way, step],
                dst_ref=recv_buf.at[way, step],
                send_sem=send_sem.at[way, step],
                recv_sem=recv_sem.at[way, step],
                device_id=(rep, target, yy, dd),
                device_id_type=MESH,
            )
            copy.start()
            copies.append(copy)
        for way in range(2):
            if way == 0:
                block = lax.rem(me + 2 * n - 2 - step, n)
            else:
                block = lax.rem(me + 2 + step, n)
            own = block_part(block, way)
            copies[way].wait()
            total = recv_buf[way, step].astype(jnp.float32) + own
            if step < n - 2:
                send_buf[way, step + 1] = total.astype(send_buf.dtype)
            else:
                ring_out[pl.ds(way * half, half), :] = total
    for index in range(peers):
        plane_send[index] = ring_out[pl.ds(index * per_peer, per_peer), :].astype(plane_send.dtype)
    sent = []
    for offset in range(1, peers):
        target = lax.rem(me_plane + offset, peers)
        copy = pltpu.make_async_remote_copy(
            src_ref=plane_send.at[target],
            dst_ref=plane_recv.at[me_plane],
            send_sem=plane_send_sem.at[offset],
            recv_sem=plane_recv_sem.at[me_plane],
            device_id=plane_device(target),
            device_id_type=MESH,
        )
        copy.start()
        sent.append(copy)
    plane_recv[me_plane] = plane_send[me_plane]
    for copy in sent:
        copy.wait_send()
    for offset in range(1, peers):
        source = lax.rem(me_plane + peers - offset, peers)
        arrival = pltpu.make_async_remote_copy(
            src_ref=plane_send.at[source],
            dst_ref=plane_recv.at[source],
            send_sem=plane_send_sem.at[offset],
            recv_sem=plane_recv_sem.at[source],
            device_id=plane_device(source),
            device_id_type=MESH,
        )
        arrival.wait_recv()
    for group in range(groups):
        total = plane_recv[group].astype(jnp.float32)
        for index in range(group + groups, peers, groups):
            total = total + plane_recv[index].astype(jnp.float32)
        out_ref[group] = total
    if hand:
        for copy in handed:
            copy.wait_send()
        for offset in range(1, reps):
            source = lax.rem(rep + reps - offset, reps)
            arrival = pltpu.make_async_remote_copy(
                src_ref=outgoing_ref.at[source],
                dst_ref=hand_buf.at[source],
                send_sem=hand_send.at[offset],
                recv_sem=hand_recv.at[source],
                device_id=(source, me, yy, dd),
                device_id_type=MESH,
            )
            arrival.wait_recv()
        total = hand_buf[0].astype(jnp.float32)
        for index in range(1, reps):
            total = total + hand_buf[index].astype(jnp.float32)
        decode_ref[...] = total.astype(decode_ref.dtype)


def ring_reduce_scatter(rows, weight, n, peers, plane, call_id, whole=False, outgoing=None):
    half = rows.shape[0] // (2 * n)
    weights = tuple(weight) if isinstance(weight, (tuple, list)) else (weight,)
    width = weights[-1].shape[-1]
    groups = 2 if len(plane) == 2 else 1
    per_peer = 2 * half // peers
    hand = outgoing is not None
    operands = (rows,) + weights + ((outgoing,) if hand else ())
    out_shape = jax.ShapeDtypeStruct((groups, per_peer, width), jnp.float32)
    if hand:
        out_shape = (out_shape, jax.ShapeDtypeStruct(outgoing.shape[1:], outgoing.dtype))
    return pl.pallas_call(
        functools.partial(_ring_kernel, whole, plane, hand),
        out_shape=out_shape,
        in_specs=[pl.BlockSpec(memory_space=pltpu.VMEM)] * len(operands),
        out_specs=(
            (pl.BlockSpec(memory_space=pltpu.VMEM),) * 2 if hand else pl.BlockSpec(memory_space=pltpu.VMEM)
        ),
        scratch_shapes=[
            pltpu.VMEM((2, n - 1, half, width), jnp.bfloat16),
            pltpu.VMEM((2, n - 1, half, width), jnp.bfloat16),
            pltpu.SemaphoreType.DMA((2, n - 1)),
            pltpu.SemaphoreType.DMA((2, n - 1)),
            pltpu.VMEM((2 * half, width), jnp.float32),
            pltpu.VMEM((peers, per_peer, width), jnp.bfloat16),
            pltpu.VMEM((peers, per_peer, width), jnp.bfloat16),
            pltpu.SemaphoreType.DMA((peers,)),
            pltpu.SemaphoreType.DMA((peers,)),
        ]
        + (
            [
                pltpu.VMEM(outgoing.shape, outgoing.dtype),
                pltpu.SemaphoreType.DMA((outgoing.shape[0],)),
                pltpu.SemaphoreType.DMA((outgoing.shape[0],)),
            ]
            if hand
            else []
        )
        + ([pltpu.VMEM((rows.shape[0], width), jnp.float32)] if whole else []),
        compiler_params=pltpu.CompilerParams(collective_id=call_id, has_side_effects=True),
    )(*operands)


def _pages_kernel(pages_ref, out_ref, arrived, z_send, z_recv, p_send, p_recv):
    nz = pages_ref.shape[0]
    peers = out_ref.shape[1]
    groups = lax.axis_size("dec")
    mz = lax.axis_index("z")
    rep = lax.axis_index("rep")
    yy = lax.axis_index("y")
    dd = lax.axis_index("dec")
    mp = yy * groups + dd

    def z_device(index):
        return (rep, index, yy, dd)

    def plane_device(index):
        return (rep, mz, index // groups, lax.rem(index, groups))

    barrier = pltpu.get_barrier_semaphore()
    for offset in range(1, nz):
        pl.semaphore_signal(barrier, inc=1, device_id=z_device(lax.rem(mz + offset, nz)),
                            device_id_type=MESH)
    for offset in range(1, peers):
        pl.semaphore_signal(barrier, inc=1, device_id=plane_device(lax.rem(mp + offset, peers)),
                            device_id_type=MESH)
    pl.semaphore_wait(barrier, nz - 1 + peers - 1)
    z_copies = []
    for offset in range(1, nz):
        target = lax.rem(mz + offset, nz)
        copy = pltpu.make_async_remote_copy(
            src_ref=pages_ref.at[target],
            dst_ref=arrived.at[mz],
            send_sem=z_send.at[offset],
            recv_sem=z_recv.at[mz],
            device_id=z_device(target),
            device_id_type=MESH,
        )
        copy.start()
        z_copies.append(copy)
    forwards = []

    def forward(source, page_ref):
        for offset in range(1, peers):
            target = lax.rem(mp + offset, peers)
            copy = pltpu.make_async_remote_copy(
                src_ref=page_ref,
                dst_ref=out_ref.at[source, mp],
                send_sem=p_send.at[source, offset],
                recv_sem=p_recv.at[source, mp],
                device_id=plane_device(target),
                device_id_type=MESH,
            )
            copy.start()
            forwards.append(copy)
        out_ref[source, mp] = page_ref[...]

    forward(mz, pages_ref.at[mz])
    order = []
    for distance in range(1, nz // 2 + 1):
        for offset in (nz - distance, distance):
            if offset not in order:
                order.append(offset)
    for offset in order:
        source = lax.rem(mz + offset, nz)
        arrival = pltpu.make_async_remote_copy(
            src_ref=pages_ref.at[source],
            dst_ref=arrived.at[source],
            send_sem=z_send.at[offset],
            recv_sem=z_recv.at[source],
            device_id=z_device(source),
            device_id_type=MESH,
        )
        arrival.wait_recv()
        forward(source, arrived.at[source])
    for copy in z_copies:
        copy.wait_send()
    for copy in forwards:
        copy.wait_send()
    for source in range(nz):
        for offset in range(1, peers):
            sender = lax.rem(mp + peers - offset, peers)
            arrival = pltpu.make_async_remote_copy(
                src_ref=pages_ref.at[source],
                dst_ref=out_ref.at[source, sender],
                send_sem=p_send.at[source, offset],
                recv_sem=p_recv.at[source, sender],
                device_id=plane_device(sender),
                device_id_type=MESH,
            )
            arrival.wait_recv()


def exchange_pages(pages, peers):
    nz = pages.shape[0]
    block = pages.shape[1:]
    return pl.pallas_call(
        _pages_kernel,
        out_shape=jax.ShapeDtypeStruct((nz, peers) + block, pages.dtype),
        in_specs=[pl.BlockSpec(memory_space=pltpu.VMEM)],
        out_specs=pl.BlockSpec(memory_space=pltpu.VMEM),
        scratch_shapes=[
            pltpu.VMEM((nz,) + block, pages.dtype),
            pltpu.SemaphoreType.DMA((nz,)),
            pltpu.SemaphoreType.DMA((nz,)),
            pltpu.SemaphoreType.DMA((nz, peers)),
            pltpu.SemaphoreType.DMA((nz, peers)),
        ],
        compiler_params=pltpu.CompilerParams(collective_id=2, has_side_effects=True),
    )(pages)


def _rows_kernel(rows_ref, out_ref, plane_rows, p_send, p_recv, send_sem, recv_sem):
    nz = out_ref.shape[0]
    peers = plane_rows.shape[0]
    each = plane_rows.shape[1]
    part = out_ref.shape[1] // 2
    groups = lax.axis_size("dec")
    mz = lax.axis_index("z")
    rep = lax.axis_index("rep")
    yy = lax.axis_index("y")
    dd = lax.axis_index("dec")
    mp = yy * groups + dd
    right = lax.rem(mz + 1, nz)
    left = lax.rem(mz + nz - 1, nz)

    def plane_device(index):
        return (rep, mz, index // groups, lax.rem(index, groups))

    barrier = pltpu.get_barrier_semaphore()
    for neighbour in (left, right):
        pl.semaphore_signal(barrier, inc=1, device_id=(rep, neighbour, yy, dd), device_id_type=MESH)
    for offset in range(1, peers):
        pl.semaphore_signal(barrier, inc=1, device_id=plane_device(lax.rem(mp + offset, peers)),
                            device_id_type=MESH)
    pl.semaphore_wait(barrier, 2 + peers - 1)
    sent = []
    for offset in range(1, peers):
        target = lax.rem(mp + offset, peers)
        copy = pltpu.make_async_remote_copy(
            src_ref=rows_ref.at[lax.rem(target, groups)],
            dst_ref=plane_rows.at[mp],
            send_sem=p_send.at[offset],
            recv_sem=p_recv.at[mp],
            device_id=plane_device(target),
            device_id_type=MESH,
        )
        copy.start()
        sent.append(copy)
    plane_rows[mp] = rows_ref[dd]
    for copy in sent:
        copy.wait_send()
    for offset in range(1, peers):
        sender = lax.rem(mp + peers - offset, peers)
        arrival = pltpu.make_async_remote_copy(
            src_ref=rows_ref.at[0],
            dst_ref=plane_rows.at[sender],
            send_sem=p_send.at[offset],
            recv_sem=p_recv.at[sender],
            device_id=plane_device(sender),
            device_id_type=MESH,
        )
        arrival.wait_recv()
    for index in range(peers):
        out_ref[mz, pl.ds(index * each, each), :] = plane_rows[index]
    for step in range(nz - 1):
        copies = []
        for way in range(2):
            if way == 0:
                target, source = right, lax.rem(mz + nz - step, nz)
            else:
                target, source = left, lax.rem(mz + step, nz)
            src = out_ref.at[source, pl.ds(way * part, part)]
            copy = pltpu.make_async_remote_copy(
                src_ref=src,
                dst_ref=out_ref.at[source, pl.ds(way * part, part)],
                send_sem=send_sem.at[way, step],
                recv_sem=recv_sem.at[way, step],
                device_id=(rep, target, yy, dd),
                device_id_type=MESH,
            )
            copy.start()
            copies.append(copy)
        for copy in copies:
            copy.wait()


def gather_rows(rows, nz, peers):
    block = rows.shape[1:]
    return pl.pallas_call(
        _rows_kernel,
        out_shape=jax.ShapeDtypeStruct((nz, peers * block[0], block[1]), rows.dtype),
        in_specs=[pl.BlockSpec(memory_space=pltpu.VMEM)],
        out_specs=pl.BlockSpec(memory_space=pltpu.VMEM),
        scratch_shapes=[
            pltpu.VMEM((peers,) + block, rows.dtype),
            pltpu.SemaphoreType.DMA((peers,)),
            pltpu.SemaphoreType.DMA((peers,)),
            pltpu.SemaphoreType.DMA((2, nz - 1)),
            pltpu.SemaphoreType.DMA((2, nz - 1)),
        ],
        compiler_params=pltpu.CompilerParams(collective_id=3, has_side_effects=True),
    )(rows)


def hand_over(kv_pool, page_target):
    rep_size = lax.axis_size("rep")
    owners = jnp.arange(rep_size, dtype=jnp.int32)
    selected = (page_target[None, :] == owners[:, None])[:, :, None, None, None]
    outgoing = jnp.where(selected, kv_pool[None], jnp.zeros((), kv_pool.dtype))
    incoming = lax.all_to_all(outgoing, "rep", split_axis=0, concat_axis=0, tiled=True)
    return jnp.sum(incoming, axis=0)


def on_device(
    residual,
    queries,
    kv_pool,
    prior_len,
    page_table,
    page_target,
    out_weight,
    moe_gain,
    expert_ids,
    expert_gates,
    w_gate,
    w_up,
    w_down,
):
    tp_size = lax.axis_size("z") * lax.axis_size("y")
    dec_size = lax.axis_size("dec")
    dec_index = lax.axis_index("dec")
    slots_dev, kv_heads, page_rows, both_dim = kv_pool.shape
    head_dim = both_dim // 2
    heads_dev = queries.shape[3] // head_dim
    group_size = QH // KVH
    kv_dev = max(1, heads_dev // group_size)
    copies = max(1, group_size // heads_dev)
    per_kv = heads_dev // kv_dev
    requests = prior_len.shape[0]
    tok_dev = queries.shape[2]
    half_rows = queries.shape[0] * tok_dev // requests
    pages_max = page_table.shape[1]
    team_size = tp_size * dec_size
    z_size = lax.axis_size("z")
    plane_size = team_size // z_size
    received = exchange_pages(kv_pool.reshape(z_size * kv_dev, page_rows, both_dim), plane_size)
    received = received.reshape(team_size * slots_dev, kv_dev, page_rows, both_dim)
    gathered_pages = received[page_table % (team_size * slots_dev)]
    keys_part = gathered_pages[..., :head_dim]
    values_part = gathered_pages[..., head_dim:]
    query_rows = queries.reshape(requests, half_rows, kv_dev, per_kv, head_dim)
    key_count = pages_max * page_rows
    scores = jnp.einsum(
        "rukgd,rpkwd->rukgpw", query_rows, keys_part, preferred_element_type=jnp.float32
    )
    scores = scores.reshape(requests, half_rows, kv_dev, per_kv, key_count) * head_dim ** (-0.5)
    position = jnp.arange(key_count, dtype=jnp.int32)
    local_row = jnp.arange(half_rows, dtype=jnp.int32)
    offset = (local_row // tok_dev * dec_size + dec_index) * tok_dev + local_row % tok_dev
    last_seen = prior_len[:, None] + offset[None, :]
    visible = (position[None, None, :] <= last_seen[:, :, None])[:, :, None, None, :]
    scores = jnp.where(visible, scores, -1e30)
    row_top = jnp.max(scores, axis=-1, keepdims=True)
    raw_weights = jnp.where(visible, jnp.exp(scores - row_top), 0.0)
    totals = jnp.sum(raw_weights, axis=-1)
    weights_low = raw_weights.astype(jnp.bfloat16).reshape(
        requests, half_rows, kv_dev, per_kv, pages_max, page_rows
    )
    weighted = jnp.einsum(
        "rukgpw,rpkwd->rukgd", weights_low, values_part, preferred_element_type=jnp.float32
    )
    attended = (
        (weighted / totals[..., None])
        .astype(jnp.bfloat16)
        .reshape(requests * half_rows, heads_dev * head_dim)
    )
    y_size = lax.axis_size("y")
    width = out_weight.shape[1]
    rep_size = lax.axis_size("rep")
    owners = jnp.arange(rep_size, dtype=jnp.int32)
    chosen = (page_target[None, :] == owners[:, None])[:, :, None, None, None]
    outgoing = jnp.where(chosen, kv_pool[None], jnp.zeros((), kv_pool.dtype))
    outgoing = outgoing.reshape((rep_size,) + kv_pool.shape[1:])
    projected, handed = ring_reduce_scatter(
        attended, out_weight, z_size, y_size, ("y",), 0, outgoing=outgoing
    )
    projected = projected[0]
    decode_pages = handed.reshape(kv_pool.shape)
    mid_state = residual.astype(jnp.float32) + projected
    routed_dev = tok_dev * TOPK // EXPERTS
    token_index = jnp.arange(tok_dev, dtype=jnp.int32)
    names_it = expert_ids[None, :, :] == jnp.arange(EXP_WIN, dtype=jnp.int32)[:, None, None]
    named = jnp.any(names_it, axis=-1)
    rank = jnp.cumsum(named.astype(jnp.int32), axis=1) - 1
    slot_hit = named[:, None, :] & (rank[:, None, :] == jnp.arange(routed_dev, dtype=jnp.int32)[None, :, None])
    picked_rows = jnp.sum(jnp.where(slot_hit, token_index, 0), axis=-1)
    gate_sum = jnp.sum(jnp.where(names_it, expert_gates[None], 0.0), axis=-1)
    picked_gates = jnp.sum(jnp.where(slot_hit, gate_sum[:, None, :], 0.0), axis=-1)
    inverse = lax.rsqrt(jnp.mean(mid_state * mid_state, axis=-1, keepdims=True) + 1e-05)
    normed_all = (mid_state * inverse * moe_gain).astype(jnp.bfloat16)
    width = normed_all.shape[1]
    by_expert = normed_all[picked_rows]
    row_piece = gather_rows(by_expert, z_size, plane_size)
    row_piece = row_piece.reshape(team_size * routed_dev, width)
    expert_out = ring_reduce_scatter(
        row_piece, (w_gate[0], w_up[0], w_down[0]), z_size, y_size * dec_size, ("y", "dec"), 1,
        whole=True,
    )
    one_hot = slot_hit.astype(jnp.float32)
    mixture = jnp.einsum(
        "eki,ekd->id", one_hot, expert_out * picked_gates[..., None], precision=lax.Precision.HIGHEST
    )
    layer_out = (mid_state + mixture).astype(jnp.bfloat16)
    return (layer_out, decode_pages)


def fine_mesh(mesh):
    tp_devices = mesh.devices[0, :, 0]
    y_size = len({device.coords[1] for device in tp_devices})
    shape = (mesh.shape["rep"], mesh.shape["tp"] // y_size, y_size, mesh.shape["dec"])
    return jax.sharding.Mesh(mesh.devices.reshape(shape), ("rep", "z", "y", "dec"))


def solution(mesh):
    team = ("rep", "z", "y", "dec")
    return jax.shard_map(
        on_device,
        mesh=fine_mesh(mesh),
        in_specs=(
            P(team, None),
            P("rep", "dec", None, ("z", "y")),
            P(team, None, None, None),
            P("rep"),
            P("rep", None),
            P(team),
            P(("z", "y"), None),
            P(),
            P(team, None),
            P(team, None),
            P("dec", ("z", "y"), None),
            P("dec", ("z", "y"), None),
            P("dec", ("z", "y"), None),
        ),
        out_specs=(P(team, None), P(team, None, None, None)),
        check_vma=False,
    )
```

```python
import functools

import jax
import jax.numpy as jnp
from jax import lax
from jax.sharding import PartitionSpec as P
from jax.experimental import pallas as pl
from jax.experimental.pallas import tpu as pltpu

QH = 32
KVH = 8
EXPERTS = 8
TOPK = 2
EXP_WIN = 2


MESH = pl.DeviceIdType.MESH

def _ring_kernel(whole, plane, hand, *refs):
    count = 3 if whole else 1
    rows_ref = refs[0]
    weight_ref = refs[1] if count == 1 else refs[1:1 + count]
    refs = refs[1 + count:]
    if hand:
        outgoing_ref, out_ref, decode_ref = refs[:3]
        rest = refs[3:]
    else:
        out_ref = refs[0]
        rest = refs[1:]
    (recv_buf, send_buf, send_sem, recv_sem, ring_out, plane_send, plane_recv,
     plane_send_sem, plane_recv_sem) = rest[:9]
    rest = rest[9:]
    if hand:
        hand_buf, hand_send, hand_recv = rest[:3]
        rest = rest[3:]
    product = rest
    n = recv_buf.shape[1] + 1
    half = recv_buf.shape[2]
    peers = plane_send.shape[0]
    groups = out_ref.shape[0]
    per_peer = plane_send.shape[1]
    me = lax.axis_index("z")
    rep = lax.axis_index("rep")
    yy = lax.axis_index("y")
    dd = lax.axis_index("dec")
    right = lax.rem(me + 1, n)
    left = lax.rem(me + n - 1, n)
    if len(plane) == 2:
        me_plane = yy * groups + dd

        def plane_device(index):
            return (rep, me, index // groups, lax.rem(index, groups))
    else:
        me_plane = yy

        def plane_device(index):
            return (rep, me, index, dd)

    if whole:
        features = rows_ref[...]
        contract = (((1,), (1,)), ((), ()))
        gate = lax.dot_general(features, weight_ref[0][...], contract, preferred_element_type=jnp.float32)
        up = lax.dot_general(features, weight_ref[1][...], contract, preferred_element_type=jnp.float32)
        hidden = (gate / (1.0 + jnp.exp(-gate)) * up).astype(features.dtype)
        product[0][...] = jnp.dot(hidden, weight_ref[2][...], preferred_element_type=jnp.float32)

    def block_part(block, way):
        start = pl.multiple_of(block * (2 * half) + way * half, half)
        if whole:
            return product[0][pl.ds(start, half), :]
        piece = rows_ref[pl.ds(start, half), :]
        return jnp.dot(piece, weight_ref[...], preferred_element_type=jnp.float32)

    barrier = pltpu.get_barrier_semaphore()
    for neighbour in (left, right):
        pl.semaphore_signal(barrier, inc=1, device_id=(rep, neighbour, yy, dd), device_id_type=MESH)
    for offset in range(1, peers):
        target = lax.rem(me_plane + offset, peers)
        pl.semaphore_signal(barrier, inc=1, device_id=plane_device(target), device_id_type=MESH)
    reps = lax.axis_size("rep")
    if hand:
        for offset in range(1, reps):
            pl.semaphore_signal(barrier, inc=1, device_id=(lax.rem(rep + offset, reps), me, yy, dd),
                                device_id_type=MESH)
    pl.semaphore_wait(barrier, 2 + peers - 1 + (reps - 1 if hand else 0))
    handed = []
    if hand:
        for offset in range(1, reps):
            target = lax.rem(rep + offset, reps)
            copy = pltpu.make_async_remote_copy(
                src_ref=outgoing_ref.at[target],
                dst_ref=hand_buf.at[rep],
                send_sem=hand_send.at[offset],
                recv_sem=hand_recv.at[rep],
                device_id=(target, me, yy, dd),
                device_id_type=MESH,
            )
            copy.start()
            handed.append(copy)
        hand_buf[rep] = outgoing_ref[rep]
    for way in range(2):
        if way == 0:
            block = lax.rem(me + n - 1, n)
        else:
            block = lax.rem(me + 1, n)
        send_buf[way, 0] = block_part(block, way).astype(send_buf.dtype)
    for step in range(n - 1):
        copies = []
        for way in range(2):
            target = right if way == 0 else left
            copy = pltpu.make_async_remote_copy(
                src_ref=send_buf.at[way, step],
                dst_ref=recv_buf.at[way, step],
                send_sem=send_sem.at[way, step],
                recv_sem=recv_sem.at[way, step],
                device_id=(rep, target, yy, dd),
                device_id_type=MESH,
            )
            copy.start()
            copies.append(copy)
        for way in range(2):
            if way == 0:
                block = lax.rem(me + 2 * n - 2 - step, n)
            else:
                block = lax.rem(me + 2 + step, n)
            own = block_part(block, way)
            copies[way].wait()
            total = recv_buf[way, step].astype(jnp.float32) + own
            if step < n - 2:
                send_buf[way, step + 1] = total.astype(send_buf.dtype)
            else:
                ring_out[pl.ds(way * half, half), :] = total
    for index in range(peers):
        plane_send[index] = ring_out[pl.ds(index * per_peer, per_peer), :].astype(plane_send.dtype)
    sent = []
    for offset in range(1, peers):
        target = lax.rem(me_plane + offset, peers)
        copy = pltpu.make_async_remote_copy(
            src_ref=plane_send.at[target],
            dst_ref=plane_recv.at[me_plane],
            send_sem=plane_send_sem.at[offset],
            recv_sem=plane_recv_sem.at[me_plane],
            device_id=plane_device(target),
            device_id_type=MESH,
        )
        copy.start()
        sent.append(copy)
    plane_recv[me_plane] = plane_send[me_plane]
    for copy in sent:
        copy.wait_send()
    for offset in range(1, peers):
        source = lax.rem(me_plane + peers - offset, peers)
        arrival = pltpu.make_async_remote_copy(
            src_ref=plane_send.at[source],
            dst_ref=plane_recv.at[source],
            send_sem=plane_send_sem.at[offset],
            recv_sem=plane_recv_sem.at[source],
            device_id=plane_device(source),
            device_id_type=MESH,
        )
        arrival.wait_recv()
    for group in range(groups):
        total = plane_recv[group].astype(jnp.float32)
        for index in range(group + groups, peers, groups):
            total = total + plane_recv[index].astype(jnp.float32)
        out_ref[group] = total
    if hand:
        for copy in handed:
            copy.wait_send()
        for offset in range(1, reps):
            source = lax.rem(rep + reps - offset, reps)
            arrival = pltpu.make_async_remote_copy(
                src_ref=outgoing_ref.at[source],
                dst_ref=hand_buf.at[source],
                send_sem=hand_send.at[offset],
                recv_sem=hand_recv.at[source],
                device_id=(source, me, yy, dd),
                device_id_type=MESH,
            )
            arrival.wait_recv()
        total = hand_buf[0].astype(jnp.float32)
        for index in range(1, reps):
            total = total + hand_buf[index].astype(jnp.float32)
        decode_ref[...] = total.astype(decode_ref.dtype)


def ring_reduce_scatter(rows, weight, n, peers, plane, call_id, whole=False, outgoing=None):
    half = rows.shape[0] // (2 * n)
    weights = tuple(weight) if isinstance(weight, (tuple, list)) else (weight,)
    width = weights[-1].shape[-1]
    groups = 2 if len(plane) == 2 else 1
    per_peer = 2 * half // peers
    hand = outgoing is not None
    operands = (rows,) + weights + ((outgoing,) if hand else ())
    out_shape = jax.ShapeDtypeStruct((groups, per_peer, width), jnp.float32)
    if hand:
        out_shape = (out_shape, jax.ShapeDtypeStruct(outgoing.shape[1:], outgoing.dtype))
    return pl.pallas_call(
        functools.partial(_ring_kernel, whole, plane, hand),
        out_shape=out_shape,
        in_specs=[pl.BlockSpec(memory_space=pltpu.VMEM)] * len(operands),
        out_specs=(
            (pl.BlockSpec(memory_space=pltpu.VMEM),) * 2 if hand else pl.BlockSpec(memory_space=pltpu.VMEM)
        ),
        scratch_shapes=[
            pltpu.VMEM((2, n - 1, half, width), jnp.bfloat16),
            pltpu.VMEM((2, n - 1, half, width), jnp.bfloat16),
            pltpu.SemaphoreType.DMA((2, n - 1)),
            pltpu.SemaphoreType.DMA((2, n - 1)),
            pltpu.VMEM((2 * half, width), jnp.float32),
            pltpu.VMEM((peers, per_peer, width), jnp.bfloat16),
            pltpu.VMEM((peers, per_peer, width), jnp.bfloat16),
            pltpu.SemaphoreType.DMA((peers,)),
            pltpu.SemaphoreType.DMA((peers,)),
        ]
        + (
            [
                pltpu.VMEM(outgoing.shape, outgoing.dtype),
                pltpu.SemaphoreType.DMA((outgoing.shape[0],)),
                pltpu.SemaphoreType.DMA((outgoing.shape[0],)),
            ]
            if hand
            else []
        )
        + ([pltpu.VMEM((rows.shape[0], width), jnp.float32)] if whole else []),
        compiler_params=pltpu.CompilerParams(collective_id=call_id, has_side_effects=True),
    )(*operands)


def _pages_kernel(pages_ref, where_ref, out_ref, picked_ref, arrived, z_send, z_recv, p_send, p_recv):
    nz = pages_ref.shape[0]
    peers = out_ref.shape[1]
    groups = lax.axis_size("dec")
    mz = lax.axis_index("z")
    rep = lax.axis_index("rep")
    yy = lax.axis_index("y")
    dd = lax.axis_index("dec")
    mp = yy * groups + dd

    def z_device(index):
        return (rep, index, yy, dd)

    def plane_device(index):
        return (rep, mz, index // groups, lax.rem(index, groups))

    barrier = pltpu.get_barrier_semaphore()
    for offset in range(1, nz):
        pl.semaphore_signal(barrier, inc=1, device_id=z_device(lax.rem(mz + offset, nz)),
                            device_id_type=MESH)
    for offset in range(1, peers):
        pl.semaphore_signal(barrier, inc=1, device_id=plane_device(lax.rem(mp + offset, peers)),
                            device_id_type=MESH)
    pl.semaphore_wait(barrier, nz - 1 + peers - 1)
    z_copies = []
    for offset in range(1, nz):
        target = lax.rem(mz + offset, nz)
        copy = pltpu.make_async_remote_copy(
            src_ref=pages_ref.at[target],
            dst_ref=arrived.at[mz],
            send_sem=z_send.at[offset],
            recv_sem=z_recv.at[mz],
            device_id=z_device(target),
            device_id_type=MESH,
        )
        copy.start()
        z_copies.append(copy)
    forwards = []

    def forward(source, page_ref):
        for offset in range(1, peers):
            target = lax.rem(mp + offset, peers)
            copy = pltpu.make_async_remote_copy(
                src_ref=page_ref,
                dst_ref=out_ref.at[source, mp],
                send_sem=p_send.at[source, offset],
                recv_sem=p_recv.at[source, mp],
                device_id=plane_device(target),
                device_id_type=MESH,
            )
            copy.start()
            forwards.append(copy)
        out_ref[source, mp] = page_ref[...]

    forward(mz, pages_ref.at[mz])
    order = []
    for distance in range(1, nz // 2 + 1):
        for offset in (nz - distance, distance):
            if offset not in order:
                order.append(offset)
    for offset in order:
        source = lax.rem(mz + offset, nz)
        arrival = pltpu.make_async_remote_copy(
            src_ref=pages_ref.at[source],
            dst_ref=arrived.at[source],
            send_sem=z_send.at[offset],
            recv_sem=z_recv.at[source],
            device_id=z_device(source),
            device_id_type=MESH,
        )
        arrival.wait_recv()
        forward(source, arrived.at[source])
    for copy in z_copies:
        copy.wait_send()
    for copy in forwards:
        copy.wait_send()
    for source in range(nz):
        for offset in range(1, peers):
            sender = lax.rem(mp + peers - offset, peers)
            arrival = pltpu.make_async_remote_copy(
                src_ref=pages_ref.at[source],
                dst_ref=out_ref.at[source, sender],
                send_sem=p_send.at[source, offset],
                recv_sem=p_recv.at[source, sender],
                device_id=plane_device(sender),
                device_id_type=MESH,
            )
            arrival.wait_recv()

    def pick(index, carry):
        picked_ref[index] = out_ref[where_ref[0, index], where_ref[1, index]]
        return carry

    lax.fori_loop(0, picked_ref.shape[0], pick, 0)


def exchange_pages(pages, peers, where):
    nz = pages.shape[0]
    block = pages.shape[1:]
    return pl.pallas_call(
        _pages_kernel,
        out_shape=(
            jax.ShapeDtypeStruct((nz, peers) + block, pages.dtype),
            jax.ShapeDtypeStruct((where.shape[1],) + block, pages.dtype),
        ),
        in_specs=[pl.BlockSpec(memory_space=pltpu.VMEM), pl.BlockSpec(memory_space=pltpu.SMEM)],
        out_specs=(pl.BlockSpec(memory_space=pltpu.VMEM),) * 2,
        scratch_shapes=[
            pltpu.VMEM((nz,) + block, pages.dtype),
            pltpu.SemaphoreType.DMA((nz,)),
            pltpu.SemaphoreType.DMA((nz,)),
            pltpu.SemaphoreType.DMA((nz, peers)),
            pltpu.SemaphoreType.DMA((nz, peers)),
        ],
        compiler_params=pltpu.CompilerParams(collective_id=2, has_side_effects=True),
    )(pages, where)


def _rows_kernel(rows_ref, out_ref, plane_rows, p_send, p_recv, send_sem, recv_sem):
    nz = out_ref.shape[0]
    peers = plane_rows.shape[0]
    each = plane_rows.shape[1]
    part = out_ref.shape[1] // 2
    groups = lax.axis_size("dec")
    mz = lax.axis_index("z")
    rep = lax.axis_index("rep")
    yy = lax.axis_index("y")
    dd = lax.axis_index("dec")
    mp = yy * groups + dd
    right = lax.rem(mz + 1, nz)
    left = lax.rem(mz + nz - 1, nz)

    def plane_device(index):
        return (rep, mz, index // groups, lax.rem(index, groups))

    barrier = pltpu.get_barrier_semaphore()
    for neighbour in (left, right):
        pl.semaphore_signal(barrier, inc=1, device_id=(rep, neighbour, yy, dd), device_id_type=MESH)
    for offset in range(1, peers):
        pl.semaphore_signal(barrier, inc=1, device_id=plane_device(lax.rem(mp + offset, peers)),
                            device_id_type=MESH)
    pl.semaphore_wait(barrier, 2 + peers - 1)
    sent = []
    for offset in range(1, peers):
        target = lax.rem(mp + offset, peers)
        copy = pltpu.make_async_remote_copy(
            src_ref=rows_ref.at[lax.rem(target, groups)],
            dst_ref=plane_rows.at[mp],
            send_sem=p_send.at[offset],
            recv_sem=p_recv.at[mp],
            device_id=plane_device(target),
            device_id_type=MESH,
        )
        copy.start()
        sent.append(copy)
    plane_rows[mp] = rows_ref[dd]
    for copy in sent:
        copy.wait_send()
    for offset in range(1, peers):
        sender = lax.rem(mp + peers - offset, peers)
        arrival = pltpu.make_async_remote_copy(
            src_ref=rows_ref.at[0],
            dst_ref=plane_rows.at[sender],
            send_sem=p_send.at[offset],
            recv_sem=p_recv.at[sender],
            device_id=plane_device(sender),
            device_id_type=MESH,
        )
        arrival.wait_recv()
    for index in range(peers):
        out_ref[mz, pl.ds(index * each, each), :] = plane_rows[index]
    for step in range(nz - 1):
        copies = []
        for way in range(2):
            if way == 0:
                target, source = right, lax.rem(mz + nz - step, nz)
            else:
                target, source = left, lax.rem(mz + step, nz)
            src = out_ref.at[source, pl.ds(way * part, part)]
            copy = pltpu.make_async_remote_copy(
                src_ref=src,
                dst_ref=out_ref.at[source, pl.ds(way * part, part)],
                send_sem=send_sem.at[way, step],
                recv_sem=recv_sem.at[way, step],
                device_id=(rep, target, yy, dd),
                device_id_type=MESH,
            )
            copy.start()
            copies.append(copy)
        for copy in copies:
            copy.wait()


def gather_rows(rows, nz, peers):
    block = rows.shape[1:]
    return pl.pallas_call(
        _rows_kernel,
        out_shape=jax.ShapeDtypeStruct((nz, peers * block[0], block[1]), rows.dtype),
        in_specs=[pl.BlockSpec(memory_space=pltpu.VMEM)],
        out_specs=pl.BlockSpec(memory_space=pltpu.VMEM),
        scratch_shapes=[
            pltpu.VMEM((peers,) + block, rows.dtype),
            pltpu.SemaphoreType.DMA((peers,)),
            pltpu.SemaphoreType.DMA((peers,)),
            pltpu.SemaphoreType.DMA((2, nz - 1)),
            pltpu.SemaphoreType.DMA((2, nz - 1)),
        ],
        compiler_params=pltpu.CompilerParams(collective_id=3, has_side_effects=True),
    )(rows)


def hand_over(kv_pool, page_target):
    rep_size = lax.axis_size("rep")
    owners = jnp.arange(rep_size, dtype=jnp.int32)
    selected = (page_target[None, :] == owners[:, None])[:, :, None, None, None]
    outgoing = jnp.where(selected, kv_pool[None], jnp.zeros((), kv_pool.dtype))
    incoming = lax.all_to_all(outgoing, "rep", split_axis=0, concat_axis=0, tiled=True)
    return jnp.sum(incoming, axis=0)


def on_device(
    residual,
    queries,
    kv_pool,
    prior_len,
    page_table,
    page_target,
    out_weight,
    moe_gain,
    expert_ids,
    expert_gates,
    w_gate,
    w_up,
    w_down,
):
    tp_size = lax.axis_size("z") * lax.axis_size("y")
    dec_size = lax.axis_size("dec")
    dec_index = lax.axis_index("dec")
    slots_dev, kv_heads, page_rows, both_dim = kv_pool.shape
    head_dim = both_dim // 2
    heads_dev = queries.shape[3] // head_dim
    group_size = QH // KVH
    kv_dev = max(1, heads_dev // group_size)
    copies = max(1, group_size // heads_dev)
    per_kv = heads_dev // kv_dev
    requests = prior_len.shape[0]
    tok_dev = queries.shape[2]
    half_rows = queries.shape[0] * tok_dev // requests
    pages_max = page_table.shape[1]
    team_size = tp_size * dec_size
    z_size = lax.axis_size("z")
    plane_size = team_size // z_size
    local_slot = (page_table % (team_size * slots_dev)).reshape(-1)
    where = jnp.stack([local_slot // plane_size, local_slot % plane_size]).astype(jnp.int32)
    _, picked = exchange_pages(kv_pool.reshape(z_size * kv_dev, page_rows, both_dim), plane_size, where)
    gathered_pages = picked.reshape(requests, pages_max, kv_dev, page_rows, both_dim)
    keys_part = gathered_pages[..., :head_dim]
    values_part = gathered_pages[..., head_dim:]
    query_rows = queries.reshape(requests, half_rows, kv_dev, per_kv, head_dim)
    key_count = pages_max * page_rows
    scores = jnp.einsum(
        "rukgd,rpkwd->rukgpw", query_rows, keys_part, preferred_element_type=jnp.float32
    )
    scores = scores.reshape(requests, half_rows, kv_dev, per_kv, key_count) * head_dim ** (-0.5)
    position = jnp.arange(key_count, dtype=jnp.int32)
    local_row = jnp.arange(half_rows, dtype=jnp.int32)
    offset = (local_row // tok_dev * dec_size + dec_index) * tok_dev + local_row % tok_dev
    last_seen = prior_len[:, None] + offset[None, :]
    visible = (position[None, None, :] <= last_seen[:, :, None])[:, :, None, None, :]
    scores = jnp.where(visible, scores, -1e30)
    row_top = jnp.max(scores, axis=-1, keepdims=True)
    raw_weights = jnp.where(visible, jnp.exp(scores - row_top), 0.0)
    totals = jnp.sum(raw_weights, axis=-1)
    weights_low = raw_weights.astype(jnp.bfloat16).reshape(
        requests, half_rows, kv_dev, per_kv, pages_max, page_rows
    )
    weighted = jnp.einsum(
        "rukgpw,rpkwd->rukgd", weights_low, values_part, preferred_element_type=jnp.float32
    )
    attended = (
        (weighted / totals[..., None])
        .astype(jnp.bfloat16)
        .reshape(requests * half_rows, heads_dev * head_dim)
    )
    y_size = lax.axis_size("y")
    width = out_weight.shape[1]
    rep_size = lax.axis_size("rep")
    owners = jnp.arange(rep_size, dtype=jnp.int32)
    chosen = (page_target[None, :] == owners[:, None])[:, :, None, None, None]
    outgoing = jnp.where(chosen, kv_pool[None], jnp.zeros((), kv_pool.dtype))
    outgoing = outgoing.reshape((rep_size,) + kv_pool.shape[1:])
    projected, handed = ring_reduce_scatter(
        attended, out_weight, z_size, y_size, ("y",), 0, outgoing=outgoing
    )
    projected = projected[0]
    decode_pages = handed.reshape(kv_pool.shape)
    mid_state = residual.astype(jnp.float32) + projected
    routed_dev = tok_dev * TOPK // EXPERTS
    token_index = jnp.arange(tok_dev, dtype=jnp.int32)
    names_it = expert_ids[None, :, :] == jnp.arange(EXP_WIN, dtype=jnp.int32)[:, None, None]
    named = jnp.any(names_it, axis=-1)
    rank = jnp.cumsum(named.astype(jnp.int32), axis=1) - 1
    slot_hit = named[:, None, :] & (rank[:, None, :] == jnp.arange(routed_dev, dtype=jnp.int32)[None, :, None])
    picked_rows = jnp.sum(jnp.where(slot_hit, token_index, 0), axis=-1)
    gate_sum = jnp.sum(jnp.where(names_it, expert_gates[None], 0.0), axis=-1)
    picked_gates = jnp.sum(jnp.where(slot_hit, gate_sum[:, None, :], 0.0), axis=-1)
    inverse = lax.rsqrt(jnp.mean(mid_state * mid_state, axis=-1, keepdims=True) + 1e-05)
    normed_all = (mid_state * inverse * moe_gain).astype(jnp.bfloat16)
    width = normed_all.shape[1]
    by_expert = normed_all[picked_rows]
    row_piece = gather_rows(by_expert, z_size, plane_size)
    row_piece = row_piece.reshape(team_size * routed_dev, width)
    expert_out = ring_reduce_scatter(
        row_piece, (w_gate[0], w_up[0], w_down[0]), z_size, y_size * dec_size, ("y", "dec"), 1,
        whole=True,
    )
    one_hot = slot_hit.astype(jnp.float32)
    mixture = jnp.einsum(
        "eki,ekd->id", one_hot, expert_out * picked_gates[..., None], precision=lax.Precision.HIGHEST
    )
    layer_out = (mid_state + mixture).astype(jnp.bfloat16)
    return (layer_out, decode_pages)


def fine_mesh(mesh):
    tp_devices = mesh.devices[0, :, 0]
    y_size = len({device.coords[1] for device in tp_devices})
    shape = (mesh.shape["rep"], mesh.shape["tp"] // y_size, y_size, mesh.shape["dec"])
    return jax.sharding.Mesh(mesh.devices.reshape(shape), ("rep", "z", "y", "dec"))


def solution(mesh):
    team = ("rep", "z", "y", "dec")
    return jax.shard_map(
        on_device,
        mesh=fine_mesh(mesh),
        in_specs=(
            P(team, None),
            P("rep", "dec", None, ("z", "y")),
            P(team, None, None, None),
            P("rep"),
            P("rep", None),
            P(team),
            P(("z", "y"), None),
            P(),
            P(team, None),
            P(team, None),
            P("dec", ("z", "y"), None),
            P("dec", ("z", "y"), None),
            P("dec", ("z", "y"), None),
        ),
        out_specs=(P(team, None), P(team, None, None, None)),
        check_vma=False,
    )
```

```python
import functools

import jax
import jax.numpy as jnp
from jax import lax
from jax.sharding import PartitionSpec as P
from jax.experimental import pallas as pl
from jax.experimental.pallas import tpu as pltpu

QH = 32
KVH = 8
EXPERTS = 8
TOPK = 2
EXP_WIN = 2


MESH = pl.DeviceIdType.MESH

def _ring_kernel(whole, plane, hand, *refs):
    count = 3 if whole else 1
    rows_ref = refs[0]
    weight_ref = refs[1] if count == 1 else refs[1:1 + count]
    refs = refs[1 + count:]
    if hand:
        page_ref, chosen_ref, out_ref, decode_ref = refs[:4]
        rest = refs[4:]
    else:
        out_ref = refs[0]
        rest = refs[1:]
    (recv_buf, send_buf, send_sem, recv_sem, ring_out, plane_send, plane_recv,
     plane_send_sem, plane_recv_sem) = rest[:9]
    rest = rest[9:]
    if hand:
        hand_buf, hand_out, hand_send, hand_recv = rest[:4]
        rest = rest[4:]
    product = rest
    n = recv_buf.shape[1] + 1
    half = recv_buf.shape[2]
    peers = plane_send.shape[0]
    groups = out_ref.shape[0]
    per_peer = plane_send.shape[1]
    me = lax.axis_index("z")
    rep = lax.axis_index("rep")
    yy = lax.axis_index("y")
    dd = lax.axis_index("dec")
    right = lax.rem(me + 1, n)
    left = lax.rem(me + n - 1, n)
    if len(plane) == 2:
        me_plane = yy * groups + dd

        def plane_device(index):
            return (rep, me, index // groups, lax.rem(index, groups))
    else:
        me_plane = yy

        def plane_device(index):
            return (rep, me, index, dd)

    if whole:
        features = rows_ref[...]
        contract = (((1,), (1,)), ((), ()))
        gate = lax.dot_general(features, weight_ref[0][...], contract, preferred_element_type=jnp.float32)
        up = lax.dot_general(features, weight_ref[1][...], contract, preferred_element_type=jnp.float32)
        hidden = (gate / (1.0 + jnp.exp(-gate)) * up).astype(features.dtype)
        product[0][...] = jnp.dot(hidden, weight_ref[2][...], preferred_element_type=jnp.float32)

    def block_part(block, way):
        start = pl.multiple_of(block * (2 * half) + way * half, half)
        if whole:
            return product[0][pl.ds(start, half), :]
        piece = rows_ref[pl.ds(start, half), :]
        return jnp.dot(piece, weight_ref[...], preferred_element_type=jnp.float32)

    barrier = pltpu.get_barrier_semaphore()
    for neighbour in (left, right):
        pl.semaphore_signal(barrier, inc=1, device_id=(rep, neighbour, yy, dd), device_id_type=MESH)
    for offset in range(1, peers):
        target = lax.rem(me_plane + offset, peers)
        pl.semaphore_signal(barrier, inc=1, device_id=plane_device(target), device_id_type=MESH)
    reps = lax.axis_size("rep")
    if hand:
        for offset in range(1, reps):
            pl.semaphore_signal(barrier, inc=1, device_id=(lax.rem(rep + offset, reps), me, yy, dd),
                                device_id_type=MESH)
    pl.semaphore_wait(barrier, 2 + peers - 1 + (reps - 1 if hand else 0))
    handed = []
    if hand:
        for offset in range(1, reps):
            target = lax.rem(rep + offset, reps)
            hand_out[offset] = jnp.where(chosen_ref[target] != 0, page_ref[...], jnp.zeros((), page_ref.dtype))
            copy = pltpu.make_async_remote_copy(
                src_ref=hand_out.at[offset],
                dst_ref=hand_buf.at[rep],
                send_sem=hand_send.at[offset],
                recv_sem=hand_recv.at[rep],
                device_id=(target, me, yy, dd),
                device_id_type=MESH,
            )
            copy.start()
            handed.append(copy)
        hand_buf[rep] = jnp.where(chosen_ref[rep] != 0, page_ref[...], jnp.zeros((), page_ref.dtype))
    for way in range(2):
        if way == 0:
            block = lax.rem(me + n - 1, n)
        else:
            block = lax.rem(me + 1, n)
        send_buf[way, 0] = block_part(block, way).astype(send_buf.dtype)
    for step in range(n - 1):
        copies = []
        for way in range(2):
            target = right if way == 0 else left
            copy = pltpu.make_async_remote_copy(
                src_ref=send_buf.at[way, step],
                dst_ref=recv_buf.at[way, step],
                send_sem=send_sem.at[way, step],
                recv_sem=recv_sem.at[way, step],
                device_id=(rep, target, yy, dd),
                device_id_type=MESH,
            )
            copy.start()
            copies.append(copy)
        for way in range(2):
            if way == 0:
                block = lax.rem(me + 2 * n - 2 - step, n)
            else:
                block = lax.rem(me + 2 + step, n)
            own = block_part(block, way)
            copies[way].wait()
            total = recv_buf[way, step].astype(jnp.float32) + own
            if step < n - 2:
                send_buf[way, step + 1] = total.astype(send_buf.dtype)
            else:
                ring_out[pl.ds(way * half, half), :] = total
    for index in range(peers):
        plane_send[index] = ring_out[pl.ds(index * per_peer, per_peer), :].astype(plane_send.dtype)
    sent = []
    for offset in range(1, peers):
        target = lax.rem(me_plane + offset, peers)
        copy = pltpu.make_async_remote_copy(
            src_ref=plane_send.at[target],
            dst_ref=plane_recv.at[me_plane],
            send_sem=plane_send_sem.at[offset],
            recv_sem=plane_recv_sem.at[me_plane],
            device_id=plane_device(target),
            device_id_type=MESH,
        )
        copy.start()
        sent.append(copy)
    plane_recv[me_plane] = plane_send[me_plane]
    for copy in sent:
        copy.wait_send()
    for offset in range(1, peers):
        source = lax.rem(me_plane + peers - offset, peers)
        arrival = pltpu.make_async_remote_copy(
            src_ref=plane_send.at[source],
            dst_ref=plane_recv.at[source],
            send_sem=plane_send_sem.at[offset],
            recv_sem=plane_recv_sem.at[source],
            device_id=plane_device(source),
            device_id_type=MESH,
        )
        arrival.wait_recv()
    for group in range(groups):
        total = plane_recv[group].astype(jnp.float32)
        for index in range(group + groups, peers, groups):
            total = total + plane_recv[index].astype(jnp.float32)
        out_ref[group] = total
    if hand:
        for copy in handed:
            copy.wait_send()
        for offset in range(1, reps):
            source = lax.rem(rep + reps - offset, reps)
            arrival = pltpu.make_async_remote_copy(
                src_ref=hand_out.at[0],
                dst_ref=hand_buf.at[source],
                send_sem=hand_send.at[offset],
                recv_sem=hand_recv.at[source],
                device_id=(source, me, yy, dd),
                device_id_type=MESH,
            )
            arrival.wait_recv()
        total = hand_buf[0].astype(jnp.float32)
        for index in range(1, reps):
            total = total + hand_buf[index].astype(jnp.float32)
        decode_ref[...] = total.astype(decode_ref.dtype)


def ring_reduce_scatter(rows, weight, n, peers, plane, call_id, whole=False, outgoing=None):
    half = rows.shape[0] // (2 * n)
    weights = tuple(weight) if isinstance(weight, (tuple, list)) else (weight,)
    width = weights[-1].shape[-1]
    groups = 2 if len(plane) == 2 else 1
    per_peer = 2 * half // peers
    hand = outgoing is not None
    operands = (rows,) + weights + (outgoing if hand else ())
    if hand:
        page, chosen = outgoing
    out_shape = jax.ShapeDtypeStruct((groups, per_peer, width), jnp.float32)
    if hand:
        out_shape = (out_shape, jax.ShapeDtypeStruct(page.shape, page.dtype))
    return pl.pallas_call(
        functools.partial(_ring_kernel, whole, plane, hand),
        out_shape=out_shape,
        in_specs=[pl.BlockSpec(memory_space=pltpu.VMEM)] * (len(operands) - hand)
        + [pl.BlockSpec(memory_space=pltpu.SMEM)] * hand,
        out_specs=(
            (pl.BlockSpec(memory_space=pltpu.VMEM),) * 2 if hand else pl.BlockSpec(memory_space=pltpu.VMEM)
        ),
        scratch_shapes=[
            pltpu.VMEM((2, n - 1, half, width), jnp.bfloat16),
            pltpu.VMEM((2, n - 1, half, width), jnp.bfloat16),
            pltpu.SemaphoreType.DMA((2, n - 1)),
            pltpu.SemaphoreType.DMA((2, n - 1)),
            pltpu.VMEM((2 * half, width), jnp.float32),
            pltpu.VMEM((peers, per_peer, width), jnp.bfloat16),
            pltpu.VMEM((peers, per_peer, width), jnp.bfloat16),
            pltpu.SemaphoreType.DMA((peers,)),
            pltpu.SemaphoreType.DMA((peers,)),
        ]
        + (
            [
                pltpu.VMEM(chosen.shape + page.shape, page.dtype),
                pltpu.VMEM(chosen.shape + page.shape, page.dtype),
                pltpu.SemaphoreType.DMA(chosen.shape),
                pltpu.SemaphoreType.DMA(chosen.shape),
            ]
            if hand
            else []
        )
        + ([pltpu.VMEM((rows.shape[0], width), jnp.float32)] if whole else []),
        compiler_params=pltpu.CompilerParams(collective_id=call_id, has_side_effects=True),
    )(*operands)


def _pages_kernel(pages_ref, where_ref, out_ref, picked_ref, arrived, z_send, z_recv, p_send, p_recv):
    nz = pages_ref.shape[0]
    peers = out_ref.shape[1]
    groups = lax.axis_size("dec")
    mz = lax.axis_index("z")
    rep = lax.axis_index("rep")
    yy = lax.axis_index("y")
    dd = lax.axis_index("dec")
    mp = yy * groups + dd

    def z_device(index):
        return (rep, index, yy, dd)

    def plane_device(index):
        return (rep, mz, index // groups, lax.rem(index, groups))

    barrier = pltpu.get_barrier_semaphore()
    for offset in range(1, nz):
        pl.semaphore_signal(barrier, inc=1, device_id=z_device(lax.rem(mz + offset, nz)),
                            device_id_type=MESH)
    for offset in range(1, peers):
        pl.semaphore_signal(barrier, inc=1, device_id=plane_device(lax.rem(mp + offset, peers)),
                            device_id_type=MESH)
    pl.semaphore_wait(barrier, nz - 1 + peers - 1)
    z_copies = []
    for offset in range(1, nz):
        target = lax.rem(mz + offset, nz)
        copy = pltpu.make_async_remote_copy(
            src_ref=pages_ref.at[target],
            dst_ref=arrived.at[mz],
            send_sem=z_send.at[offset],
            recv_sem=z_recv.at[mz],
            device_id=z_device(target),
            device_id_type=MESH,
        )
        copy.start()
        z_copies.append(copy)
    forwards = []

    def forward(source, page_ref):
        for offset in range(1, peers):
            target = lax.rem(mp + offset, peers)
            copy = pltpu.make_async_remote_copy(
                src_ref=page_ref,
                dst_ref=out_ref.at[source, mp],
                send_sem=p_send.at[source, offset],
                recv_sem=p_recv.at[source, mp],
                device_id=plane_device(target),
                device_id_type=MESH,
            )
            copy.start()
            forwards.append(copy)
        out_ref[source, mp] = page_ref[...]

    forward(mz, pages_ref.at[mz])
    order = []
    for distance in range(1, nz // 2 + 1):
        for offset in (nz - distance, distance):
            if offset not in order:
                order.append(offset)
    for offset in order:
        source = lax.rem(mz + offset, nz)
        arrival = pltpu.make_async_remote_copy(
            src_ref=pages_ref.at[source],
            dst_ref=arrived.at[source],
            send_sem=z_send.at[offset],
            recv_sem=z_recv.at[source],
            device_id=z_device(source),
            device_id_type=MESH,
        )
        arrival.wait_recv()
        forward(source, arrived.at[source])
    for copy in z_copies:
        copy.wait_send()
    for copy in forwards:
        copy.wait_send()
    for source in range(nz):
        for offset in range(1, peers):
            sender = lax.rem(mp + peers - offset, peers)
            arrival = pltpu.make_async_remote_copy(
                src_ref=pages_ref.at[source],
                dst_ref=out_ref.at[source, sender],
                send_sem=p_send.at[source, offset],
                recv_sem=p_recv.at[source, sender],
                device_id=plane_device(sender),
                device_id_type=MESH,
            )
            arrival.wait_recv()

    def pick(index, carry):
        picked_ref[index] = out_ref[where_ref[0, index], where_ref[1, index]]
        return carry

    lax.fori_loop(0, picked_ref.shape[0], pick, 0)


def exchange_pages(pages, peers, where):
    nz = pages.shape[0]
    block = pages.shape[1:]
    return pl.pallas_call(
        _pages_kernel,
        out_shape=(
            jax.ShapeDtypeStruct((nz, peers) + block, pages.dtype),
            jax.ShapeDtypeStruct((where.shape[1],) + block, pages.dtype),
        ),
        in_specs=[pl.BlockSpec(memory_space=pltpu.VMEM), pl.BlockSpec(memory_space=pltpu.SMEM)],
        out_specs=(pl.BlockSpec(memory_space=pltpu.VMEM),) * 2,
        scratch_shapes=[
            pltpu.VMEM((nz,) + block, pages.dtype),
            pltpu.SemaphoreType.DMA((nz,)),
            pltpu.SemaphoreType.DMA((nz,)),
            pltpu.SemaphoreType.DMA((nz, peers)),
            pltpu.SemaphoreType.DMA((nz, peers)),
        ],
        compiler_params=pltpu.CompilerParams(collective_id=2, has_side_effects=True),
    )(pages, where)


def _rows_kernel(rows_ref, out_ref, plane_rows, p_send, p_recv, send_sem, recv_sem):
    nz = out_ref.shape[0]
    peers = plane_rows.shape[0]
    each = plane_rows.shape[1]
    part = out_ref.shape[1] // 2
    groups = lax.axis_size("dec")
    mz = lax.axis_index("z")
    rep = lax.axis_index("rep")
    yy = lax.axis_index("y")
    dd = lax.axis_index("dec")
    mp = yy * groups + dd
    right = lax.rem(mz + 1, nz)
    left = lax.rem(mz + nz - 1, nz)

    def plane_device(index):
        return (rep, mz, index // groups, lax.rem(index, groups))

    barrier = pltpu.get_barrier_semaphore()
    for neighbour in (left, right):
        pl.semaphore_signal(barrier, inc=1, device_id=(rep, neighbour, yy, dd), device_id_type=MESH)
    for offset in range(1, peers):
        pl.semaphore_signal(barrier, inc=1, device_id=plane_device(lax.rem(mp + offset, peers)),
                            device_id_type=MESH)
    pl.semaphore_wait(barrier, 2 + peers - 1)
    sent = []
    for offset in range(1, peers):
        target = lax.rem(mp + offset, peers)
        copy = pltpu.make_async_remote_copy(
            src_ref=rows_ref.at[lax.rem(target, groups)],
            dst_ref=plane_rows.at[mp],
            send_sem=p_send.at[offset],
            recv_sem=p_recv.at[mp],
            device_id=plane_device(target),
            device_id_type=MESH,
        )
        copy.start()
        sent.append(copy)
    plane_rows[mp] = rows_ref[dd]
    for copy in sent:
        copy.wait_send()
    for offset in range(1, peers):
        sender = lax.rem(mp + peers - offset, peers)
        arrival = pltpu.make_async_remote_copy(
            src_ref=rows_ref.at[0],
            dst_ref=plane_rows.at[sender],
            send_sem=p_send.at[offset],
            recv_sem=p_recv.at[sender],
            device_id=plane_device(sender),
            device_id_type=MESH,
        )
        arrival.wait_recv()
    for index in range(peers):
        out_ref[mz, pl.ds(index * each, each), :] = plane_rows[index]
    for step in range(nz - 1):
        copies = []
        for way in range(2):
            if way == 0:
                target, source = right, lax.rem(mz + nz - step, nz)
            else:
                target, source = left, lax.rem(mz + step, nz)
            src = out_ref.at[source, pl.ds(way * part, part)]
            copy = pltpu.make_async_remote_copy(
                src_ref=src,
                dst_ref=out_ref.at[source, pl.ds(way * part, part)],
                send_sem=send_sem.at[way, step],
                recv_sem=recv_sem.at[way, step],
                device_id=(rep, target, yy, dd),
                device_id_type=MESH,
            )
            copy.start()
            copies.append(copy)
        for copy in copies:
            copy.wait()


def gather_rows(rows, nz, peers):
    block = rows.shape[1:]
    return pl.pallas_call(
        _rows_kernel,
        out_shape=jax.ShapeDtypeStruct((nz, peers * block[0], block[1]), rows.dtype),
        in_specs=[pl.BlockSpec(memory_space=pltpu.VMEM)],
        out_specs=pl.BlockSpec(memory_space=pltpu.VMEM),
        scratch_shapes=[
            pltpu.VMEM((peers,) + block, rows.dtype),
            pltpu.SemaphoreType.DMA((peers,)),
            pltpu.SemaphoreType.DMA((peers,)),
            pltpu.SemaphoreType.DMA((2, nz - 1)),
            pltpu.SemaphoreType.DMA((2, nz - 1)),
        ],
        compiler_params=pltpu.CompilerParams(collective_id=3, has_side_effects=True),
    )(rows)


def hand_over(kv_pool, page_target):
    rep_size = lax.axis_size("rep")
    owners = jnp.arange(rep_size, dtype=jnp.int32)
    selected = (page_target[None, :] == owners[:, None])[:, :, None, None, None]
    outgoing = jnp.where(selected, kv_pool[None], jnp.zeros((), kv_pool.dtype))
    incoming = lax.all_to_all(outgoing, "rep", split_axis=0, concat_axis=0, tiled=True)
    return jnp.sum(incoming, axis=0)


def on_device(
    residual,
    queries,
    kv_pool,
    prior_len,
    page_table,
    page_target,
    out_weight,
    moe_gain,
    expert_ids,
    expert_gates,
    w_gate,
    w_up,
    w_down,
):
    tp_size = lax.axis_size("z") * lax.axis_size("y")
    dec_size = lax.axis_size("dec")
    dec_index = lax.axis_index("dec")
    slots_dev, kv_heads, page_rows, both_dim = kv_pool.shape
    head_dim = both_dim // 2
    heads_dev = queries.shape[3] // head_dim
    group_size = QH // KVH
    kv_dev = max(1, heads_dev // group_size)
    copies = max(1, group_size // heads_dev)
    per_kv = heads_dev // kv_dev
    requests = prior_len.shape[0]
    tok_dev = queries.shape[2]
    half_rows = queries.shape[0] * tok_dev // requests
    pages_max = page_table.shape[1]
    team_size = tp_size * dec_size
    z_size = lax.axis_size("z")
    plane_size = team_size // z_size
    local_slot = (page_table % (team_size * slots_dev)).reshape(-1)
    where = jnp.stack([local_slot // plane_size, local_slot % plane_size]).astype(jnp.int32)
    _, picked = exchange_pages(kv_pool.reshape(z_size * kv_dev, page_rows, both_dim), plane_size, where)
    gathered_pages = picked.reshape(requests, pages_max, kv_dev, page_rows, both_dim)
    keys_part = gathered_pages[..., :head_dim]
    values_part = gathered_pages[..., head_dim:]
    query_rows = queries.reshape(requests, half_rows, kv_dev, per_kv, head_dim)
    key_count = pages_max * page_rows
    scores = jnp.einsum(
        "rukgd,rpkwd->rukgpw", query_rows, keys_part, preferred_element_type=jnp.float32
    )
    scores = scores.reshape(requests, half_rows, kv_dev, per_kv, key_count) * head_dim ** (-0.5)
    position = jnp.arange(key_count, dtype=jnp.int32)
    local_row = jnp.arange(half_rows, dtype=jnp.int32)
    offset = (local_row // tok_dev * dec_size + dec_index) * tok_dev + local_row % tok_dev
    last_seen = prior_len[:, None] + offset[None, :]
    visible = (position[None, None, :] <= last_seen[:, :, None])[:, :, None, None, :]
    scores = jnp.where(visible, scores, -1e30)
    row_top = jnp.max(scores, axis=-1, keepdims=True)
    raw_weights = jnp.where(visible, jnp.exp(scores - row_top), 0.0)
    totals = jnp.sum(raw_weights, axis=-1)
    weights_low = raw_weights.astype(jnp.bfloat16).reshape(
        requests, half_rows, kv_dev, per_kv, pages_max, page_rows
    )
    weighted = jnp.einsum(
        "rukgpw,rpkwd->rukgd", weights_low, values_part, preferred_element_type=jnp.float32
    )
    attended = (
        (weighted / totals[..., None])
        .astype(jnp.bfloat16)
        .reshape(requests * half_rows, heads_dev * head_dim)
    )
    y_size = lax.axis_size("y")
    width = out_weight.shape[1]
    rep_size = lax.axis_size("rep")
    owners = jnp.arange(rep_size, dtype=jnp.int32)
    chosen = (page_target[0] == owners).astype(jnp.int32)
    outgoing = (kv_pool.reshape(kv_pool.shape[1:]), chosen)
    projected, handed = ring_reduce_scatter(
        attended, out_weight, z_size, y_size, ("y",), 0, outgoing=outgoing
    )
    projected = projected[0]
    decode_pages = handed.reshape(kv_pool.shape)
    mid_state = residual.astype(jnp.float32) + projected
    routed_dev = tok_dev * TOPK // EXPERTS
    token_index = jnp.arange(tok_dev, dtype=jnp.int32)
    names_it = expert_ids[None, :, :] == jnp.arange(EXP_WIN, dtype=jnp.int32)[:, None, None]
    named = jnp.any(names_it, axis=-1)
    rank = jnp.cumsum(named.astype(jnp.int32), axis=1) - 1
    slot_hit = named[:, None, :] & (rank[:, None, :] == jnp.arange(routed_dev, dtype=jnp.int32)[None, :, None])
    picked_rows = jnp.sum(jnp.where(slot_hit, token_index, 0), axis=-1)
    gate_sum = jnp.sum(jnp.where(names_it, expert_gates[None], 0.0), axis=-1)
    picked_gates = jnp.sum(jnp.where(slot_hit, gate_sum[:, None, :], 0.0), axis=-1)
    inverse = lax.rsqrt(jnp.mean(mid_state * mid_state, axis=-1, keepdims=True) + 1e-05)
    normed_all = (mid_state * inverse * moe_gain).astype(jnp.bfloat16)
    width = normed_all.shape[1]
    by_expert = normed_all[picked_rows]
    row_piece = gather_rows(by_expert, z_size, plane_size)
    row_piece = row_piece.reshape(team_size * routed_dev, width)
    expert_out = ring_reduce_scatter(
        row_piece, (w_gate[0], w_up[0], w_down[0]), z_size, y_size * dec_size, ("y", "dec"), 1,
        whole=True,
    )
    one_hot = slot_hit.astype(jnp.float32)
    mixture = jnp.einsum(
        "eki,ekd->id", one_hot, expert_out * picked_gates[..., None], precision=lax.Precision.HIGHEST
    )
    layer_out = (mid_state + mixture).astype(jnp.bfloat16)
    return (layer_out, decode_pages)


def fine_mesh(mesh):
    tp_devices = mesh.devices[0, :, 0]
    y_size = len({device.coords[1] for device in tp_devices})
    shape = (mesh.shape["rep"], mesh.shape["tp"] // y_size, y_size, mesh.shape["dec"])
    return jax.sharding.Mesh(mesh.devices.reshape(shape), ("rep", "z", "y", "dec"))


def solution(mesh):
    team = ("rep", "z", "y", "dec")
    return jax.shard_map(
        on_device,
        mesh=fine_mesh(mesh),
        in_specs=(
            P(team, None),
            P("rep", "dec", None, ("z", "y")),
            P(team, None, None, None),
            P("rep"),
            P("rep", None),
            P(team),
            P(("z", "y"), None),
            P(),
            P(team, None),
            P(team, None),
            P("dec", ("z", "y"), None),
            P("dec", ("z", "y"), None),
            P("dec", ("z", "y"), None),
        ),
        out_specs=(P(team, None), P(team, None, None, None)),
        check_vma=False,
    )
```

```python
import functools

import jax
import jax.numpy as jnp
from jax import lax
from jax.sharding import PartitionSpec as P
from jax.experimental import pallas as pl
from jax.experimental.pallas import tpu as pltpu

QH = 32
KVH = 8
EXPERTS = 8
TOPK = 2
EXP_WIN = 2


MESH = pl.DeviceIdType.MESH

def _ring_kernel(whole, plane, hand, *refs):
    count = 3 if whole else 1
    rows_ref = refs[0]
    weight_ref = refs[1] if count == 1 else refs[1:1 + count]
    refs = refs[1 + count:]
    if hand:
        page_ref, chosen_ref, out_ref, decode_ref = refs[:4]
        rest = refs[4:]
    else:
        out_ref = refs[0]
        rest = refs[1:]
    (recv_buf, send_buf, send_sem, recv_sem, ring_out, plane_send, plane_recv,
     plane_send_sem, plane_recv_sem) = rest[:9]
    rest = rest[9:]
    if hand:
        hand_buf, hand_out, hand_send, hand_recv = rest[:4]
        rest = rest[4:]
    product = rest
    n = recv_buf.shape[1] + 1
    half = recv_buf.shape[2]
    peers = plane_send.shape[0]
    groups = out_ref.shape[0]
    per_peer = plane_send.shape[1]
    me = lax.axis_index("z")
    rep = lax.axis_index("rep")
    yy = lax.axis_index("y")
    dd = lax.axis_index("dec")
    right = lax.rem(me + 1, n)
    left = lax.rem(me + n - 1, n)
    if len(plane) == 2:
        me_plane = yy * groups + dd

        def plane_device(index):
            return (rep, me, index // groups, lax.rem(index, groups))
    else:
        me_plane = yy

        def plane_device(index):
            return (rep, me, index, dd)

    if whole:
        features = rows_ref[...]
        contract = (((1,), (1,)), ((), ()))
        gate = lax.dot_general(features, weight_ref[0][...], contract, preferred_element_type=jnp.float32)
        up = lax.dot_general(features, weight_ref[1][...], contract, preferred_element_type=jnp.float32)
        hidden = (gate / (1.0 + jnp.exp(-gate)) * up).astype(features.dtype)
        product[0][...] = jnp.dot(hidden, weight_ref[2][...], preferred_element_type=jnp.float32)

    def block_part(block, way):
        start = pl.multiple_of(block * (2 * half) + way * half, half)
        if whole:
            return product[0][pl.ds(start, half), :]
        piece = rows_ref[pl.ds(start, half), :]
        return jnp.dot(piece, weight_ref[...], preferred_element_type=jnp.float32)

    barrier = pltpu.get_barrier_semaphore()
    for neighbour in (left, right):
        pl.semaphore_signal(barrier, inc=1, device_id=(rep, neighbour, yy, dd), device_id_type=MESH)
    for offset in range(1, peers):
        target = lax.rem(me_plane + offset, peers)
        pl.semaphore_signal(barrier, inc=1, device_id=plane_device(target), device_id_type=MESH)
    reps = lax.axis_size("rep")
    if hand:
        for offset in range(1, reps):
            pl.semaphore_signal(barrier, inc=1, device_id=(lax.rem(rep + offset, reps), me, yy, dd),
                                device_id_type=MESH)
    pl.semaphore_wait(barrier, 2 + peers - 1 + (reps - 1 if hand else 0))
    handed = []
    if hand:
        for offset in range(1, reps):
            target = lax.rem(rep + offset, reps)
            hand_out[offset] = jnp.where(chosen_ref[target] != 0, page_ref[...], jnp.zeros((), page_ref.dtype))
            copy = pltpu.make_async_remote_copy(
                src_ref=hand_out.at[offset],
                dst_ref=hand_buf.at[rep],
                send_sem=hand_send.at[offset],
                recv_sem=hand_recv.at[rep],
                device_id=(target, me, yy, dd),
                device_id_type=MESH,
            )
            copy.start()
            handed.append(copy)
        hand_buf[rep] = jnp.where(chosen_ref[rep] != 0, page_ref[...], jnp.zeros((), page_ref.dtype))
    for way in range(2):
        if way == 0:
            block = lax.rem(me + n - 1, n)
        else:
            block = lax.rem(me + 1, n)
        send_buf[way, 0] = block_part(block, way).astype(send_buf.dtype)
    for step in range(n - 1):
        copies = []
        for way in range(2):
            target = right if way == 0 else left
            copy = pltpu.make_async_remote_copy(
                src_ref=send_buf.at[way, step],
                dst_ref=recv_buf.at[way, step],
                send_sem=send_sem.at[way, step],
                recv_sem=recv_sem.at[way, step],
                device_id=(rep, target, yy, dd),
                device_id_type=MESH,
            )
            copy.start()
            copies.append(copy)
        for way in range(2):
            if way == 0:
                block = lax.rem(me + 2 * n - 2 - step, n)
            else:
                block = lax.rem(me + 2 + step, n)
            own = block_part(block, way)
            copies[way].wait()
            total = recv_buf[way, step].astype(jnp.float32) + own
            if step < n - 2:
                send_buf[way, step + 1] = total.astype(send_buf.dtype)
            else:
                ring_out[pl.ds(way * half, half), :] = total
    for index in range(peers):
        plane_send[index] = ring_out[pl.ds(index * per_peer, per_peer), :].astype(plane_send.dtype)
    sent = []
    for offset in range(1, peers):
        target = lax.rem(me_plane + offset, peers)
        copy = pltpu.make_async_remote_copy(
            src_ref=plane_send.at[target],
            dst_ref=plane_recv.at[me_plane],
            send_sem=plane_send_sem.at[offset],
            recv_sem=plane_recv_sem.at[me_plane],
            device_id=plane_device(target),
            device_id_type=MESH,
        )
        copy.start()
        sent.append(copy)
    plane_recv[me_plane] = plane_send[me_plane]
    for copy in sent:
        copy.wait_send()
    for offset in range(1, peers):
        source = lax.rem(me_plane + peers - offset, peers)
        arrival = pltpu.make_async_remote_copy(
            src_ref=plane_send.at[source],
            dst_ref=plane_recv.at[source],
            send_sem=plane_send_sem.at[offset],
            recv_sem=plane_recv_sem.at[source],
            device_id=plane_device(source),
            device_id_type=MESH,
        )
        arrival.wait_recv()
    for group in range(groups):
        total = plane_recv[group].astype(jnp.float32)
        for index in range(group + groups, peers, groups):
            total = total + plane_recv[index].astype(jnp.float32)
        out_ref[group] = total
    if hand:
        for copy in handed:
            copy.wait_send()
        for offset in range(1, reps):
            source = lax.rem(rep + reps - offset, reps)
            arrival = pltpu.make_async_remote_copy(
                src_ref=hand_out.at[0],
                dst_ref=hand_buf.at[source],
                send_sem=hand_send.at[offset],
                recv_sem=hand_recv.at[source],
                device_id=(source, me, yy, dd),
                device_id_type=MESH,
            )
            arrival.wait_recv()
        total = hand_buf[0].astype(jnp.float32)
        for index in range(1, reps):
            total = total + hand_buf[index].astype(jnp.float32)
        decode_ref[...] = total.astype(decode_ref.dtype)


def ring_reduce_scatter(rows, weight, n, peers, plane, call_id, whole=False, outgoing=None):
    half = rows.shape[0] // (2 * n)
    weights = tuple(weight) if isinstance(weight, (tuple, list)) else (weight,)
    width = weights[-1].shape[-1]
    groups = 2 if len(plane) == 2 else 1
    per_peer = 2 * half // peers
    hand = outgoing is not None
    operands = (rows,) + weights + (outgoing if hand else ())
    if hand:
        page, chosen = outgoing
    out_shape = jax.ShapeDtypeStruct((groups, per_peer, width), jnp.float32)
    if hand:
        out_shape = (out_shape, jax.ShapeDtypeStruct(page.shape, page.dtype))
    return pl.pallas_call(
        functools.partial(_ring_kernel, whole, plane, hand),
        out_shape=out_shape,
        in_specs=[pl.BlockSpec(memory_space=pltpu.VMEM)] * (len(operands) - hand)
        + [pl.BlockSpec(memory_space=pltpu.SMEM)] * hand,
        out_specs=(
            (pl.BlockSpec(memory_space=pltpu.VMEM),) * 2 if hand else pl.BlockSpec(memory_space=pltpu.VMEM)
        ),
        scratch_shapes=[
            pltpu.VMEM((2, n - 1, half, width), jnp.bfloat16),
            pltpu.VMEM((2, n - 1, half, width), jnp.bfloat16),
            pltpu.SemaphoreType.DMA((2, n - 1)),
            pltpu.SemaphoreType.DMA((2, n - 1)),
            pltpu.VMEM((2 * half, width), jnp.float32),
            pltpu.VMEM((peers, per_peer, width), jnp.bfloat16),
            pltpu.VMEM((peers, per_peer, width), jnp.bfloat16),
            pltpu.SemaphoreType.DMA((peers,)),
            pltpu.SemaphoreType.DMA((peers,)),
        ]
        + (
            [
                pltpu.VMEM(chosen.shape + page.shape, page.dtype),
                pltpu.VMEM(chosen.shape + page.shape, page.dtype),
                pltpu.SemaphoreType.DMA(chosen.shape),
                pltpu.SemaphoreType.DMA(chosen.shape),
            ]
            if hand
            else []
        )
        + ([pltpu.VMEM((rows.shape[0], width), jnp.float32)] if whole else []),
        compiler_params=pltpu.CompilerParams(collective_id=call_id, has_side_effects=True),
    )(*operands)


def _pages_kernel(pages_ref, where_ref, out_ref, picked_ref, arrived, z_send, z_recv, p_send, p_recv):
    nz = pages_ref.shape[0]
    peers = out_ref.shape[1]
    groups = lax.axis_size("dec")
    mz = lax.axis_index("z")
    rep = lax.axis_index("rep")
    yy = lax.axis_index("y")
    dd = lax.axis_index("dec")
    mp = yy * groups + dd

    def z_device(index):
        return (rep, index, yy, dd)

    def plane_device(index):
        return (rep, mz, index // groups, lax.rem(index, groups))

    barrier = pltpu.get_barrier_semaphore()
    for offset in range(1, nz):
        pl.semaphore_signal(barrier, inc=1, device_id=z_device(lax.rem(mz + offset, nz)),
                            device_id_type=MESH)
    for offset in range(1, peers):
        pl.semaphore_signal(barrier, inc=1, device_id=plane_device(lax.rem(mp + offset, peers)),
                            device_id_type=MESH)
    pl.semaphore_wait(barrier, nz - 1 + peers - 1)
    z_copies = []
    for offset in range(1, nz):
        target = lax.rem(mz + offset, nz)
        copy = pltpu.make_async_remote_copy(
            src_ref=pages_ref.at[target],
            dst_ref=arrived.at[mz],
            send_sem=z_send.at[offset],
            recv_sem=z_recv.at[mz],
            device_id=z_device(target),
            device_id_type=MESH,
        )
        copy.start()
        z_copies.append(copy)
    forwards = []

    def forward(source, page_ref):
        for offset in range(1, peers):
            target = lax.rem(mp + offset, peers)
            copy = pltpu.make_async_remote_copy(
                src_ref=page_ref,
                dst_ref=out_ref.at[source, mp],
                send_sem=p_send.at[source, offset],
                recv_sem=p_recv.at[source, mp],
                device_id=plane_device(target),
                device_id_type=MESH,
            )
            copy.start()
            forwards.append(copy)
        out_ref[source, mp] = page_ref[...]

    forward(mz, pages_ref.at[mz])
    order = []
    for distance in range(1, nz // 2 + 1):
        for offset in (nz - distance, distance):
            if offset not in order:
                order.append(offset)
    for offset in order:
        source = lax.rem(mz + offset, nz)
        arrival = pltpu.make_async_remote_copy(
            src_ref=pages_ref.at[source],
            dst_ref=arrived.at[source],
            send_sem=z_send.at[offset],
            recv_sem=z_recv.at[source],
            device_id=z_device(source),
            device_id_type=MESH,
        )
        arrival.wait_recv()
        forward(source, arrived.at[source])
    for copy in z_copies:
        copy.wait_send()
    for copy in forwards:
        copy.wait_send()
    for source in range(nz):
        for offset in range(1, peers):
            sender = lax.rem(mp + peers - offset, peers)
            arrival = pltpu.make_async_remote_copy(
                src_ref=pages_ref.at[source],
                dst_ref=out_ref.at[source, sender],
                send_sem=p_send.at[source, offset],
                recv_sem=p_recv.at[source, sender],
                device_id=plane_device(sender),
                device_id_type=MESH,
            )
            arrival.wait_recv()

    pages_max = where_ref.shape[1]
    slots = nz * peers

    def pick(index, carry):
        slot = where_ref[index // pages_max, lax.rem(index, pages_max)]
        local = lax.rem(jnp.maximum(slot, 0), slots)
        picked_ref[index] = out_ref[local // peers, lax.rem(local, peers)]
        return carry

    lax.fori_loop(0, picked_ref.shape[0], pick, 0)


def exchange_pages(pages, peers, where):
    nz = pages.shape[0]
    block = pages.shape[1:]
    return pl.pallas_call(
        _pages_kernel,
        out_shape=(
            jax.ShapeDtypeStruct((nz, peers) + block, pages.dtype),
            jax.ShapeDtypeStruct((where.shape[0] * where.shape[1],) + block, pages.dtype),
        ),
        in_specs=[pl.BlockSpec(memory_space=pltpu.VMEM), pl.BlockSpec(memory_space=pltpu.SMEM)],
        out_specs=(pl.BlockSpec(memory_space=pltpu.VMEM),) * 2,
        scratch_shapes=[
            pltpu.VMEM((nz,) + block, pages.dtype),
            pltpu.SemaphoreType.DMA((nz,)),
            pltpu.SemaphoreType.DMA((nz,)),
            pltpu.SemaphoreType.DMA((nz, peers)),
            pltpu.SemaphoreType.DMA((nz, peers)),
        ],
        compiler_params=pltpu.CompilerParams(collective_id=2, has_side_effects=True),
    )(pages, where)


def _rows_kernel(rows_ref, out_ref, plane_rows, p_send, p_recv, send_sem, recv_sem):
    nz = out_ref.shape[0]
    peers = plane_rows.shape[0]
    each = plane_rows.shape[1]
    part = out_ref.shape[1] // 2
    groups = lax.axis_size("dec")
    mz = lax.axis_index("z")
    rep = lax.axis_index("rep")
    yy = lax.axis_index("y")
    dd = lax.axis_index("dec")
    mp = yy * groups + dd
    right = lax.rem(mz + 1, nz)
    left = lax.rem(mz + nz - 1, nz)

    def plane_device(index):
        return (rep, mz, index // groups, lax.rem(index, groups))

    barrier = pltpu.get_barrier_semaphore()
    for neighbour in (left, right):
        pl.semaphore_signal(barrier, inc=1, device_id=(rep, neighbour, yy, dd), device_id_type=MESH)
    for offset in range(1, peers):
        pl.semaphore_signal(barrier, inc=1, device_id=plane_device(lax.rem(mp + offset, peers)),
                            device_id_type=MESH)
    pl.semaphore_wait(barrier, 2 + peers - 1)
    sent = []
    for offset in range(1, peers):
        target = lax.rem(mp + offset, peers)
        copy = pltpu.make_async_remote_copy(
            src_ref=rows_ref.at[lax.rem(target, groups)],
            dst_ref=plane_rows.at[mp],
            send_sem=p_send.at[offset],
            recv_sem=p_recv.at[mp],
            device_id=plane_device(target),
            device_id_type=MESH,
        )
        copy.start()
        sent.append(copy)
    plane_rows[mp] = rows_ref[dd]
    for copy in sent:
        copy.wait_send()
    for offset in range(1, peers):
        sender = lax.rem(mp + peers - offset, peers)
        arrival = pltpu.make_async_remote_copy(
            src_ref=rows_ref.at[0],
            dst_ref=plane_rows.at[sender],
            send_sem=p_send.at[offset],
            recv_sem=p_recv.at[sender],
            device_id=plane_device(sender),
            device_id_type=MESH,
        )
        arrival.wait_recv()
    for index in range(peers):
        out_ref[mz, pl.ds(index * each, each), :] = plane_rows[index]
    for step in range(nz - 1):
        copies = []
        for way in range(2):
            if way == 0:
                target, source = right, lax.rem(mz + nz - step, nz)
            else:
                target, source = left, lax.rem(mz + step, nz)
            src = out_ref.at[source, pl.ds(way * part, part)]
            copy = pltpu.make_async_remote_copy(
                src_ref=src,
                dst_ref=out_ref.at[source, pl.ds(way * part, part)],
                send_sem=send_sem.at[way, step],
                recv_sem=recv_sem.at[way, step],
                device_id=(rep, target, yy, dd),
                device_id_type=MESH,
            )
            copy.start()
            copies.append(copy)
        for copy in copies:
            copy.wait()


def gather_rows(rows, nz, peers):
    block = rows.shape[1:]
    return pl.pallas_call(
        _rows_kernel,
        out_shape=jax.ShapeDtypeStruct((nz, peers * block[0], block[1]), rows.dtype),
        in_specs=[pl.BlockSpec(memory_space=pltpu.VMEM)],
        out_specs=pl.BlockSpec(memory_space=pltpu.VMEM),
        scratch_shapes=[
            pltpu.VMEM((peers,) + block, rows.dtype),
            pltpu.SemaphoreType.DMA((peers,)),
            pltpu.SemaphoreType.DMA((peers,)),
            pltpu.SemaphoreType.DMA((2, nz - 1)),
            pltpu.SemaphoreType.DMA((2, nz - 1)),
        ],
        compiler_params=pltpu.CompilerParams(collective_id=3, has_side_effects=True),
    )(rows)


def hand_over(kv_pool, page_target):
    rep_size = lax.axis_size("rep")
    owners = jnp.arange(rep_size, dtype=jnp.int32)
    selected = (page_target[None, :] == owners[:, None])[:, :, None, None, None]
    outgoing = jnp.where(selected, kv_pool[None], jnp.zeros((), kv_pool.dtype))
    incoming = lax.all_to_all(outgoing, "rep", split_axis=0, concat_axis=0, tiled=True)
    return jnp.sum(incoming, axis=0)


def on_device(
    residual,
    queries,
    kv_pool,
    prior_len,
    page_table,
    page_target,
    out_weight,
    moe_gain,
    expert_ids,
    expert_gates,
    w_gate,
    w_up,
    w_down,
):
    tp_size = lax.axis_size("z") * lax.axis_size("y")
    dec_size = lax.axis_size("dec")
    dec_index = lax.axis_index("dec")
    slots_dev, kv_heads, page_rows, both_dim = kv_pool.shape
    head_dim = both_dim // 2
    heads_dev = queries.shape[3] // head_dim
    group_size = QH // KVH
    kv_dev = max(1, heads_dev // group_size)
    copies = max(1, group_size // heads_dev)
    per_kv = heads_dev // kv_dev
    requests = prior_len.shape[0]
    tok_dev = queries.shape[2]
    half_rows = queries.shape[0] * tok_dev // requests
    pages_max = page_table.shape[1]
    team_size = tp_size * dec_size
    z_size = lax.axis_size("z")
    plane_size = team_size // z_size
    _, picked = exchange_pages(kv_pool.reshape(z_size * kv_dev, page_rows, both_dim), plane_size, page_table)
    gathered_pages = picked.reshape(requests, pages_max, kv_dev, page_rows, both_dim)
    keys_part = gathered_pages[..., :head_dim]
    values_part = gathered_pages[..., head_dim:]
    query_rows = queries.reshape(requests, half_rows, kv_dev, per_kv, head_dim)
    key_count = pages_max * page_rows
    scores = jnp.einsum(
        "rukgd,rpkwd->rukgpw", query_rows, keys_part, preferred_element_type=jnp.float32
    )
    scores = scores.reshape(requests, half_rows, kv_dev, per_kv, key_count) * head_dim ** (-0.5)
    position = jnp.arange(key_count, dtype=jnp.int32)
    local_row = jnp.arange(half_rows, dtype=jnp.int32)
    offset = (local_row // tok_dev * dec_size + dec_index) * tok_dev + local_row % tok_dev
    last_seen = prior_len[:, None] + offset[None, :]
    visible = (position[None, None, :] <= last_seen[:, :, None])[:, :, None, None, :]
    scores = jnp.where(visible, scores, -1e30)
    row_top = jnp.max(scores, axis=-1, keepdims=True)
    raw_weights = jnp.where(visible, jnp.exp(scores - row_top), 0.0)
    totals = jnp.sum(raw_weights, axis=-1)
    weights_low = raw_weights.astype(jnp.bfloat16).reshape(
        requests, half_rows, kv_dev, per_kv, pages_max, page_rows
    )
    weighted = jnp.einsum(
        "rukgpw,rpkwd->rukgd", weights_low, values_part, preferred_element_type=jnp.float32
    )
    attended = (
        (weighted / totals[..., None])
        .astype(jnp.bfloat16)
        .reshape(requests * half_rows, heads_dev * head_dim)
    )
    y_size = lax.axis_size("y")
    width = out_weight.shape[1]
    rep_size = lax.axis_size("rep")
    owners = jnp.arange(rep_size, dtype=jnp.int32)
    chosen = (page_target[0] == owners).astype(jnp.int32)
    outgoing = (kv_pool.reshape(kv_pool.shape[1:]), chosen)
    projected, handed = ring_reduce_scatter(
        attended, out_weight, z_size, y_size, ("y",), 0, outgoing=outgoing
    )
    projected = projected[0]
    decode_pages = handed.reshape(kv_pool.shape)
    mid_state = residual.astype(jnp.float32) + projected
    routed_dev = tok_dev * TOPK // EXPERTS
    token_index = jnp.arange(tok_dev, dtype=jnp.int32)
    names_it = expert_ids[None, :, :] == jnp.arange(EXP_WIN, dtype=jnp.int32)[:, None, None]
    named = jnp.any(names_it, axis=-1)
    rank = jnp.cumsum(named.astype(jnp.int32), axis=1) - 1
    slot_hit = named[:, None, :] & (rank[:, None, :] == jnp.arange(routed_dev, dtype=jnp.int32)[None, :, None])
    picked_rows = jnp.sum(jnp.where(slot_hit, token_index, 0), axis=-1)
    gate_sum = jnp.sum(jnp.where(names_it, expert_gates[None], 0.0), axis=-1)
    picked_gates = jnp.sum(jnp.where(slot_hit, gate_sum[:, None, :], 0.0), axis=-1)
    inverse = lax.rsqrt(jnp.mean(mid_state * mid_state, axis=-1, keepdims=True) + 1e-05)
    normed_all = (mid_state * inverse * moe_gain).astype(jnp.bfloat16)
    width = normed_all.shape[1]
    by_expert = normed_all[picked_rows]
    row_piece = gather_rows(by_expert, z_size, plane_size)
    row_piece = row_piece.reshape(team_size * routed_dev, width)
    expert_out = ring_reduce_scatter(
        row_piece, (w_gate[0], w_up[0], w_down[0]), z_size, y_size * dec_size, ("y", "dec"), 1,
        whole=True,
    )
    one_hot = slot_hit.astype(jnp.float32)
    mixture = jnp.einsum(
        "eki,ekd->id", one_hot, expert_out * picked_gates[..., None], precision=lax.Precision.HIGHEST
    )
    layer_out = (mid_state + mixture).astype(jnp.bfloat16)
    return (layer_out, decode_pages)


def fine_mesh(mesh):
    tp_devices = mesh.devices[0, :, 0]
    y_size = len({device.coords[1] for device in tp_devices})
    shape = (mesh.shape["rep"], mesh.shape["tp"] // y_size, y_size, mesh.shape["dec"])
    return jax.sharding.Mesh(mesh.devices.reshape(shape), ("rep", "z", "y", "dec"))


def solution(mesh):
    team = ("rep", "z", "y", "dec")
    return jax.shard_map(
        on_device,
        mesh=fine_mesh(mesh),
        in_specs=(
            P(team, None),
            P("rep", "dec", None, ("z", "y")),
            P(team, None, None, None),
            P("rep"),
            P("rep", None),
            P(team),
            P(("z", "y"), None),
            P(),
            P(team, None),
            P(team, None),
            P("dec", ("z", "y"), None),
            P("dec", ("z", "y"), None),
            P("dec", ("z", "y"), None),
        ),
        out_specs=(P(team, None), P(team, None, None, None)),
        check_vma=False,
    )
```

```python
import functools

import jax
import jax.numpy as jnp
from jax import lax
from jax.sharding import PartitionSpec as P
from jax.experimental import pallas as pl
from jax.experimental.pallas import tpu as pltpu

QH = 32
KVH = 8
EXPERTS = 8
TOPK = 2
EXP_WIN = 2


MESH = pl.DeviceIdType.MESH

def _ring_kernel(whole, plane, hand, *refs):
    count = 3 if whole else 1
    rows_ref = refs[0]
    weight_ref = refs[1] if count == 1 else refs[1:1 + count]
    refs = refs[1 + count:]
    if hand:
        page_ref, chosen_ref, out_ref, decode_ref = refs[:4]
        rest = refs[4:]
    else:
        out_ref = refs[0]
        rest = refs[1:]
    (recv_buf, send_buf, send_sem, recv_sem, ring_out, plane_send, plane_recv,
     plane_send_sem, plane_recv_sem) = rest[:9]
    rest = rest[9:]
    if hand:
        hand_buf, hand_out, hand_send, hand_recv = rest[:4]
        rest = rest[4:]
    product = rest
    n = recv_buf.shape[1] + 1
    half = recv_buf.shape[2]
    peers = plane_send.shape[0]
    groups = out_ref.shape[0]
    per_peer = plane_send.shape[1]
    me = lax.axis_index("z")
    rep = lax.axis_index("rep")
    yy = lax.axis_index("y")
    dd = lax.axis_index("dec")
    right = lax.rem(me + 1, n)
    left = lax.rem(me + n - 1, n)
    if len(plane) == 2:
        me_plane = yy * groups + dd

        def plane_device(index):
            return (rep, me, index // groups, lax.rem(index, groups))
    else:
        me_plane = yy

        def plane_device(index):
            return (rep, me, index, dd)

    if whole:
        features = rows_ref[...]
        contract = (((1,), (1,)), ((), ()))
        gate = lax.dot_general(features, weight_ref[0][...], contract, preferred_element_type=jnp.float32)
        up = lax.dot_general(features, weight_ref[1][...], contract, preferred_element_type=jnp.float32)
        hidden = (gate / (1.0 + jnp.exp(-gate)) * up).astype(features.dtype)
        product[0][...] = jnp.dot(hidden, weight_ref[2][...], preferred_element_type=jnp.float32)

    def block_part(block, way):
        start = pl.multiple_of(block * (2 * half) + way * half, half)
        if whole:
            return product[0][pl.ds(start, half), :]
        piece = rows_ref[pl.ds(start, half), :]
        return jnp.dot(piece, weight_ref[...], preferred_element_type=jnp.float32)

    barrier = pltpu.get_barrier_semaphore()
    for neighbour in (left, right):
        pl.semaphore_signal(barrier, inc=1, device_id=(rep, neighbour, yy, dd), device_id_type=MESH)
    for offset in range(1, peers):
        target = lax.rem(me_plane + offset, peers)
        pl.semaphore_signal(barrier, inc=1, device_id=plane_device(target), device_id_type=MESH)
    reps = lax.axis_size("rep")
    if hand:
        for offset in range(1, reps):
            pl.semaphore_signal(barrier, inc=1, device_id=(lax.rem(rep + offset, reps), me, yy, dd),
                                device_id_type=MESH)
    pl.semaphore_wait(barrier, 2 + peers - 1 + (reps - 1 if hand else 0))
    handed = []
    if hand:
        for offset in range(1, reps):
            target = lax.rem(rep + offset, reps)
            hand_out[offset] = jnp.where(chosen_ref[target] != 0, page_ref[...], jnp.zeros((), page_ref.dtype))
            copy = pltpu.make_async_remote_copy(
                src_ref=hand_out.at[offset],
                dst_ref=hand_buf.at[rep],
                send_sem=hand_send.at[offset],
                recv_sem=hand_recv.at[rep],
                device_id=(target, me, yy, dd),
                device_id_type=MESH,
            )
            copy.start()
            handed.append(copy)
        hand_buf[rep] = jnp.where(chosen_ref[rep] != 0, page_ref[...], jnp.zeros((), page_ref.dtype))
    for way in range(2):
        if way == 0:
            block = lax.rem(me + n - 1, n)
        else:
            block = lax.rem(me + 1, n)
        send_buf[way, 0] = block_part(block, way).astype(send_buf.dtype)
    for step in range(n - 1):
        copies = []
        for way in range(2):
            target = right if way == 0 else left
            copy = pltpu.make_async_remote_copy(
                src_ref=send_buf.at[way, step],
                dst_ref=recv_buf.at[way, step],
                send_sem=send_sem.at[way, step],
                recv_sem=recv_sem.at[way, step],
                device_id=(rep, target, yy, dd),
                device_id_type=MESH,
            )
            copy.start()
            copies.append(copy)
        for way in range(2):
            if way == 0:
                block = lax.rem(me + 2 * n - 2 - step, n)
            else:
                block = lax.rem(me + 2 + step, n)
            own = block_part(block, way)
            copies[way].wait()
            total = recv_buf[way, step].astype(jnp.float32) + own
            if step < n - 2:
                send_buf[way, step + 1] = total.astype(send_buf.dtype)
            else:
                ring_out[pl.ds(way * half, half), :] = total
    for index in range(peers):
        plane_send[index] = ring_out[pl.ds(index * per_peer, per_peer), :].astype(plane_send.dtype)
    sent = []
    for offset in range(1, peers):
        target = lax.rem(me_plane + offset, peers)
        copy = pltpu.make_async_remote_copy(
            src_ref=plane_send.at[target],
            dst_ref=plane_recv.at[me_plane],
            send_sem=plane_send_sem.at[offset],
            recv_sem=plane_recv_sem.at[me_plane],
            device_id=plane_device(target),
            device_id_type=MESH,
        )
        copy.start()
        sent.append(copy)
    plane_recv[me_plane] = plane_send[me_plane]
    for copy in sent:
        copy.wait_send()
    for offset in range(1, peers):
        source = lax.rem(me_plane + peers - offset, peers)
        arrival = pltpu.make_async_remote_copy(
            src_ref=plane_send.at[source],
            dst_ref=plane_recv.at[source],
            send_sem=plane_send_sem.at[offset],
            recv_sem=plane_recv_sem.at[source],
            device_id=plane_device(source),
            device_id_type=MESH,
        )
        arrival.wait_recv()
    for group in range(groups):
        total = plane_recv[group].astype(jnp.float32)
        for index in range(group + groups, peers, groups):
            total = total + plane_recv[index].astype(jnp.float32)
        out_ref[group] = total
    if hand:
        for copy in handed:
            copy.wait_send()
        for offset in range(1, reps):
            source = lax.rem(rep + reps - offset, reps)
            arrival = pltpu.make_async_remote_copy(
                src_ref=hand_out.at[0],
                dst_ref=hand_buf.at[source],
                send_sem=hand_send.at[offset],
                recv_sem=hand_recv.at[source],
                device_id=(source, me, yy, dd),
                device_id_type=MESH,
            )
            arrival.wait_recv()
        total = hand_buf[0].astype(jnp.float32)
        for index in range(1, reps):
            total = total + hand_buf[index].astype(jnp.float32)
        decode_ref[...] = total.astype(decode_ref.dtype)


def ring_reduce_scatter(rows, weight, n, peers, plane, call_id, whole=False, outgoing=None):
    half = rows.shape[0] // (2 * n)
    weights = tuple(weight) if isinstance(weight, (tuple, list)) else (weight,)
    width = weights[-1].shape[-1]
    groups = 2 if len(plane) == 2 else 1
    per_peer = 2 * half // peers
    hand = outgoing is not None
    operands = (rows,) + weights + (outgoing if hand else ())
    if hand:
        page, chosen = outgoing
    out_shape = jax.ShapeDtypeStruct((groups, per_peer, width), jnp.float32)
    if hand:
        out_shape = (out_shape, jax.ShapeDtypeStruct(page.shape, page.dtype))
    return pl.pallas_call(
        functools.partial(_ring_kernel, whole, plane, hand),
        out_shape=out_shape,
        in_specs=[pl.BlockSpec(memory_space=pltpu.VMEM)] * (len(operands) - hand)
        + [pl.BlockSpec(memory_space=pltpu.SMEM)] * hand,
        out_specs=(
            (pl.BlockSpec(memory_space=pltpu.VMEM),) * 2 if hand else pl.BlockSpec(memory_space=pltpu.VMEM)
        ),
        scratch_shapes=[
            pltpu.VMEM((2, n - 1, half, width), jnp.bfloat16),
            pltpu.VMEM((2, n - 1, half, width), jnp.bfloat16),
            pltpu.SemaphoreType.DMA((2, n - 1)),
            pltpu.SemaphoreType.DMA((2, n - 1)),
            pltpu.VMEM((2 * half, width), jnp.float32),
            pltpu.VMEM((peers, per_peer, width), jnp.bfloat16),
            pltpu.VMEM((peers, per_peer, width), jnp.bfloat16),
            pltpu.SemaphoreType.DMA((peers,)),
            pltpu.SemaphoreType.DMA((peers,)),
        ]
        + (
            [
                pltpu.VMEM(chosen.shape + page.shape, page.dtype),
                pltpu.VMEM(chosen.shape + page.shape, page.dtype),
                pltpu.SemaphoreType.DMA(chosen.shape),
                pltpu.SemaphoreType.DMA(chosen.shape),
            ]
            if hand
            else []
        )
        + ([pltpu.VMEM((rows.shape[0], width), jnp.float32)] if whole else []),
        compiler_params=pltpu.CompilerParams(collective_id=call_id, has_side_effects=True),
    )(*operands)


def _pages_kernel(pages_ref, where_ref, out_ref, picked_ref, arrived, z_send, z_recv, p_send, p_recv):
    nz = pages_ref.shape[0]
    peers = out_ref.shape[1]
    groups = lax.axis_size("dec")
    mz = lax.axis_index("z")
    rep = lax.axis_index("rep")
    yy = lax.axis_index("y")
    dd = lax.axis_index("dec")
    mp = yy * groups + dd

    def z_device(index):
        return (rep, index, yy, dd)

    def plane_device(index):
        return (rep, mz, index // groups, lax.rem(index, groups))

    barrier = pltpu.get_barrier_semaphore()
    for offset in range(1, nz):
        pl.semaphore_signal(barrier, inc=1, device_id=z_device(lax.rem(mz + offset, nz)),
                            device_id_type=MESH)
    for offset in range(1, peers):
        pl.semaphore_signal(barrier, inc=1, device_id=plane_device(lax.rem(mp + offset, peers)),
                            device_id_type=MESH)
    pl.semaphore_wait(barrier, nz - 1 + peers - 1)
    z_copies = []
    for offset in range(1, nz):
        target = lax.rem(mz + offset, nz)
        copy = pltpu.make_async_remote_copy(
            src_ref=pages_ref.at[target],
            dst_ref=arrived.at[mz],
            send_sem=z_send.at[offset],
            recv_sem=z_recv.at[mz],
            device_id=z_device(target),
            device_id_type=MESH,
        )
        copy.start()
        z_copies.append(copy)
    forwards = []

    def forward(source, page_ref):
        for offset in range(1, peers):
            target = lax.rem(mp + offset, peers)
            copy = pltpu.make_async_remote_copy(
                src_ref=page_ref,
                dst_ref=out_ref.at[source, mp],
                send_sem=p_send.at[source, offset],
                recv_sem=p_recv.at[source, mp],
                device_id=plane_device(target),
                device_id_type=MESH,
            )
            copy.start()
            forwards.append(copy)
        out_ref[source, mp] = page_ref[...]

    forward(mz, pages_ref.at[mz])
    order = []
    for distance in range(1, nz // 2 + 1):
        for offset in (nz - distance, distance):
            if offset not in order:
                order.append(offset)
    for offset in order:
        source = lax.rem(mz + offset, nz)
        arrival = pltpu.make_async_remote_copy(
            src_ref=pages_ref.at[source],
            dst_ref=arrived.at[source],
            send_sem=z_send.at[offset],
            recv_sem=z_recv.at[source],
            device_id=z_device(source),
            device_id_type=MESH,
        )
        arrival.wait_recv()
        forward(source, arrived.at[source])
    for copy in z_copies:
        copy.wait_send()
    for copy in forwards:
        copy.wait_send()
    for source in range(nz):
        for offset in range(1, peers):
            sender = lax.rem(mp + peers - offset, peers)
            arrival = pltpu.make_async_remote_copy(
                src_ref=pages_ref.at[source],
                dst_ref=out_ref.at[source, sender],
                send_sem=p_send.at[source, offset],
                recv_sem=p_recv.at[source, sender],
                device_id=plane_device(sender),
                device_id_type=MESH,
            )
            arrival.wait_recv()

    pages_max = where_ref.shape[1]
    slots = nz * peers

    def pick(index, carry):
        slot = where_ref[index // pages_max, lax.rem(index, pages_max)]
        local = lax.rem(jnp.maximum(slot, 0), slots)
        picked_ref[index] = out_ref[local // peers, lax.rem(local, peers)]
        return carry

    lax.fori_loop(0, picked_ref.shape[0], pick, 0, unroll=4)


def exchange_pages(pages, peers, where):
    nz = pages.shape[0]
    block = pages.shape[1:]
    return pl.pallas_call(
        _pages_kernel,
        out_shape=(
            jax.ShapeDtypeStruct((nz, peers) + block, pages.dtype),
            jax.ShapeDtypeStruct((where.shape[0] * where.shape[1],) + block, pages.dtype),
        ),
        in_specs=[pl.BlockSpec(memory_space=pltpu.VMEM), pl.BlockSpec(memory_space=pltpu.SMEM)],
        out_specs=(pl.BlockSpec(memory_space=pltpu.VMEM),) * 2,
        scratch_shapes=[
            pltpu.VMEM((nz,) + block, pages.dtype),
            pltpu.SemaphoreType.DMA((nz,)),
            pltpu.SemaphoreType.DMA((nz,)),
            pltpu.SemaphoreType.DMA((nz, peers)),
            pltpu.SemaphoreType.DMA((nz, peers)),
        ],
        compiler_params=pltpu.CompilerParams(collective_id=2, has_side_effects=True),
    )(pages, where)


def _rows_kernel(rows_ref, out_ref, plane_rows, p_send, p_recv, send_sem, recv_sem):
    nz = out_ref.shape[0]
    peers = plane_rows.shape[0]
    each = plane_rows.shape[1]
    part = out_ref.shape[1] // 2
    groups = lax.axis_size("dec")
    mz = lax.axis_index("z")
    rep = lax.axis_index("rep")
    yy = lax.axis_index("y")
    dd = lax.axis_index("dec")
    mp = yy * groups + dd
    right = lax.rem(mz + 1, nz)
    left = lax.rem(mz + nz - 1, nz)

    def plane_device(index):
        return (rep, mz, index // groups, lax.rem(index, groups))

    barrier = pltpu.get_barrier_semaphore()
    for neighbour in (left, right):
        pl.semaphore_signal(barrier, inc=1, device_id=(rep, neighbour, yy, dd), device_id_type=MESH)
    for offset in range(1, peers):
        pl.semaphore_signal(barrier, inc=1, device_id=plane_device(lax.rem(mp + offset, peers)),
                            device_id_type=MESH)
    pl.semaphore_wait(barrier, 2 + peers - 1)
    sent = []
    for offset in range(1, peers):
        target = lax.rem(mp + offset, peers)
        copy = pltpu.make_async_remote_copy(
            src_ref=rows_ref.at[lax.rem(target, groups)],
            dst_ref=plane_rows.at[mp],
            send_sem=p_send.at[offset],
            recv_sem=p_recv.at[mp],
            device_id=plane_device(target),
            device_id_type=MESH,
        )
        copy.start()
        sent.append(copy)
    plane_rows[mp] = rows_ref[dd]
    for copy in sent:
        copy.wait_send()
    for offset in range(1, peers):
        sender = lax.rem(mp + peers - offset, peers)
        arrival = pltpu.make_async_remote_copy(
            src_ref=rows_ref.at[0],
            dst_ref=plane_rows.at[sender],
            send_sem=p_send.at[offset],
            recv_sem=p_recv.at[sender],
            device_id=plane_device(sender),
            device_id_type=MESH,
        )
        arrival.wait_recv()
    for index in range(peers):
        out_ref[mz, pl.ds(index * each, each), :] = plane_rows[index]
    for step in range(nz - 1):
        copies = []
        for way in range(2):
            if way == 0:
                target, source = right, lax.rem(mz + nz - step, nz)
            else:
                target, source = left, lax.rem(mz + step, nz)
            src = out_ref.at[source, pl.ds(way * part, part)]
            copy = pltpu.make_async_remote_copy(
                src_ref=src,
                dst_ref=out_ref.at[source, pl.ds(way * part, part)],
                send_sem=send_sem.at[way, step],
                recv_sem=recv_sem.at[way, step],
                device_id=(rep, target, yy, dd),
                device_id_type=MESH,
            )
            copy.start()
            copies.append(copy)
        for copy in copies:
            copy.wait()


def gather_rows(rows, nz, peers):
    block = rows.shape[1:]
    return pl.pallas_call(
        _rows_kernel,
        out_shape=jax.ShapeDtypeStruct((nz, peers * block[0], block[1]), rows.dtype),
        in_specs=[pl.BlockSpec(memory_space=pltpu.VMEM)],
        out_specs=pl.BlockSpec(memory_space=pltpu.VMEM),
        scratch_shapes=[
            pltpu.VMEM((peers,) + block, rows.dtype),
            pltpu.SemaphoreType.DMA((peers,)),
            pltpu.SemaphoreType.DMA((peers,)),
            pltpu.SemaphoreType.DMA((2, nz - 1)),
            pltpu.SemaphoreType.DMA((2, nz - 1)),
        ],
        compiler_params=pltpu.CompilerParams(collective_id=3, has_side_effects=True),
    )(rows)


def hand_over(kv_pool, page_target):
    rep_size = lax.axis_size("rep")
    owners = jnp.arange(rep_size, dtype=jnp.int32)
    selected = (page_target[None, :] == owners[:, None])[:, :, None, None, None]
    outgoing = jnp.where(selected, kv_pool[None], jnp.zeros((), kv_pool.dtype))
    incoming = lax.all_to_all(outgoing, "rep", split_axis=0, concat_axis=0, tiled=True)
    return jnp.sum(incoming, axis=0)


def on_device(
    residual,
    queries,
    kv_pool,
    prior_len,
    page_table,
    page_target,
    out_weight,
    moe_gain,
    expert_ids,
    expert_gates,
    w_gate,
    w_up,
    w_down,
):
    tp_size = lax.axis_size("z") * lax.axis_size("y")
    dec_size = lax.axis_size("dec")
    dec_index = lax.axis_index("dec")
    slots_dev, kv_heads, page_rows, both_dim = kv_pool.shape
    head_dim = both_dim // 2
    heads_dev = queries.shape[3] // head_dim
    group_size = QH // KVH
    kv_dev = max(1, heads_dev // group_size)
    copies = max(1, group_size // heads_dev)
    per_kv = heads_dev // kv_dev
    requests = prior_len.shape[0]
    tok_dev = queries.shape[2]
    half_rows = queries.shape[0] * tok_dev // requests
    pages_max = page_table.shape[1]
    team_size = tp_size * dec_size
    z_size = lax.axis_size("z")
    plane_size = team_size // z_size
    _, picked = exchange_pages(kv_pool.reshape(z_size * kv_dev, page_rows, both_dim), plane_size, page_table)
    gathered_pages = picked.reshape(requests, pages_max, kv_dev, page_rows, both_dim)
    keys_part = gathered_pages[..., :head_dim]
    values_part = gathered_pages[..., head_dim:]
    query_rows = queries.reshape(requests, half_rows, kv_dev, per_kv, head_dim)
    key_count = pages_max * page_rows
    scores = jnp.einsum(
        "rukgd,rpkwd->rukgpw", query_rows, keys_part, preferred_element_type=jnp.float32
    )
    scores = scores.reshape(requests, half_rows, kv_dev, per_kv, key_count) * head_dim ** (-0.5)
    position = jnp.arange(key_count, dtype=jnp.int32)
    local_row = jnp.arange(half_rows, dtype=jnp.int32)
    offset = (local_row // tok_dev * dec_size + dec_index) * tok_dev + local_row % tok_dev
    last_seen = prior_len[:, None] + offset[None, :]
    visible = (position[None, None, :] <= last_seen[:, :, None])[:, :, None, None, :]
    scores = jnp.where(visible, scores, -1e30)
    row_top = jnp.max(scores, axis=-1, keepdims=True)
    raw_weights = jnp.where(visible, jnp.exp(scores - row_top), 0.0)
    totals = jnp.sum(raw_weights, axis=-1)
    weights_low = raw_weights.astype(jnp.bfloat16).reshape(
        requests, half_rows, kv_dev, per_kv, pages_max, page_rows
    )
    weighted = jnp.einsum(
        "rukgpw,rpkwd->rukgd", weights_low, values_part, preferred_element_type=jnp.float32
    )
    attended = (
        (weighted / totals[..., None])
        .astype(jnp.bfloat16)
        .reshape(requests * half_rows, heads_dev * head_dim)
    )
    y_size = lax.axis_size("y")
    width = out_weight.shape[1]
    rep_size = lax.axis_size("rep")
    owners = jnp.arange(rep_size, dtype=jnp.int32)
    chosen = (page_target[0] == owners).astype(jnp.int32)
    outgoing = (kv_pool.reshape(kv_pool.shape[1:]), chosen)
    projected, handed = ring_reduce_scatter(
        attended, out_weight, z_size, y_size, ("y",), 0, outgoing=outgoing
    )
    projected = projected[0]
    decode_pages = handed.reshape(kv_pool.shape)
    mid_state = residual.astype(jnp.float32) + projected
    routed_dev = tok_dev * TOPK // EXPERTS
    token_index = jnp.arange(tok_dev, dtype=jnp.int32)
    names_it = expert_ids[None, :, :] == jnp.arange(EXP_WIN, dtype=jnp.int32)[:, None, None]
    named = jnp.any(names_it, axis=-1)
    rank = jnp.cumsum(named.astype(jnp.int32), axis=1) - 1
    slot_hit = named[:, None, :] & (rank[:, None, :] == jnp.arange(routed_dev, dtype=jnp.int32)[None, :, None])
    picked_rows = jnp.sum(jnp.where(slot_hit, token_index, 0), axis=-1)
    gate_sum = jnp.sum(jnp.where(names_it, expert_gates[None], 0.0), axis=-1)
    picked_gates = jnp.sum(jnp.where(slot_hit, gate_sum[:, None, :], 0.0), axis=-1)
    inverse = lax.rsqrt(jnp.mean(mid_state * mid_state, axis=-1, keepdims=True) + 1e-05)
    normed_all = (mid_state * inverse * moe_gain).astype(jnp.bfloat16)
    width = normed_all.shape[1]
    by_expert = normed_all[picked_rows]
    row_piece = gather_rows(by_expert, z_size, plane_size)
    row_piece = row_piece.reshape(team_size * routed_dev, width)
    expert_out = ring_reduce_scatter(
        row_piece, (w_gate[0], w_up[0], w_down[0]), z_size, y_size * dec_size, ("y", "dec"), 1,
        whole=True,
    )
    one_hot = slot_hit.astype(jnp.float32)
    mixture = jnp.einsum(
        "eki,ekd->id", one_hot, expert_out * picked_gates[..., None], precision=lax.Precision.HIGHEST
    )
    layer_out = (mid_state + mixture).astype(jnp.bfloat16)
    return (layer_out, decode_pages)


def fine_mesh(mesh):
    tp_devices = mesh.devices[0, :, 0]
    y_size = len({device.coords[1] for device in tp_devices})
    shape = (mesh.shape["rep"], mesh.shape["tp"] // y_size, y_size, mesh.shape["dec"])
    return jax.sharding.Mesh(mesh.devices.reshape(shape), ("rep", "z", "y", "dec"))


def solution(mesh):
    team = ("rep", "z", "y", "dec")
    return jax.shard_map(
        on_device,
        mesh=fine_mesh(mesh),
        in_specs=(
            P(team, None),
            P("rep", "dec", None, ("z", "y")),
            P(team, None, None, None),
            P("rep"),
            P("rep", None),
            P(team),
            P(("z", "y"), None),
            P(),
            P(team, None),
            P(team, None),
            P("dec", ("z", "y"), None),
            P("dec", ("z", "y"), None),
            P("dec", ("z", "y"), None),
        ),
        out_specs=(P(team, None), P(team, None, None, None)),
        check_vma=False,
    )
```
